32 devices in a mesh: shard: 8 (over z, y), ctx: 2 (over core), tp: 2 (over x).
Axes of the slice: x: 2, y: 2, z: 4, core: 2. Of those that a mesh axis runs over, the one named last changes fastest.
Arguments:
- tokens: bfloat16 [8192, 2048], P(('shard', 'ctx')), may hold values from -6 to 6
- segments: int32 [8, 1024], P('shard'), may hold values from 0 to 15, never falling along the last dimension, each value on 1 to 512 neighbouring positions
- gain_attn: bfloat16 [2048], P(('shard', 'ctx')), may hold values from 0.5 to 1.5
- w_query: bfloat16 [2048, 2048], P(('shard', 'ctx'), 'tp'), may hold values from -0.125 to 0.125
- w_key: bfloat16 [2048, 2048], P(('shard', 'ctx'), 'tp'), may hold values from -0.125 to 0.125
- w_value: bfloat16 [2048, 2048], P(('shard', 'ctx'), 'tp'), may hold values from -0.125 to 0.125
- w_out: bfloat16 [2048, 2048], P(('shard', 'ctx'), 'tp'), may hold values from -3 to 3
- gain_mlp: bfloat16 [2048], P(('shard', 'ctx')), may hold values from 0.5 to 1.5
- w_gate: bfloat16 [2048, 8192], P(('shard', 'ctx'), 'tp'), may hold values from -0.125 to 0.125
- w_up: bfloat16 [2048, 8192], P(('shard', 'ctx'), 'tp'), may hold values from -0.125 to 0.125
- w_down: bfloat16 [2048, 8192], P(('shard', 'ctx'), 'tp'), may hold values from -0.0625 to 0.0625
- cotangent: bfloat16 [8192, 2048], P(('shard', 'ctx')), may hold values from -6 to 6
Outputs:
- output: bfloat16 [8192, 2048], P(('shard', 'ctx'))
- grad_tokens: bfloat16 [8192, 2048], P(('shard', 'ctx'))
- grad_gain_attn: float32 [2048], P(('shard', 'ctx'))
- grad_w_query: float32 [2048, 2048], P(('shard', 'ctx'), 'tp')
- grad_w_key: float32 [2048, 2048], P(('shard', 'ctx'), 'tp')
- grad_w_value: float32 [2048, 2048], P(('shard', 'ctx'), 'tp')
- grad_w_out: float32 [2048, 2048], P(('shard', 'ctx'), 'tp')
- grad_gain_mlp: float32 [2048], P(('shard', 'ctx'))
- grad_w_gate: float32 [2048, 8192], P(('shard', 'ctx'), 'tp')
- grad_w_up: float32 [2048, 8192], P(('shard', 'ctx'), 'tp')
- grad_w_down: float32 [2048, 8192], P(('shard', 'ctx'), 'tp')
The draws below stay inside these ranges and needn't reach their ends.
Inputs may be any that keep to these rules, and one draw needn't show every extreme that they name: `segments`: within each sequence the segment numbers never fall; each number marks one document of consecutive tokens, and some document holds exactly 512 tokens.
All inputs are finite; a program needn't handle non-finite values.
Results may differ from the reference program's by a relative error of at most 0.015.
Values may be sent and summed in bfloat16 or wider, within the bound.
No kernel may reach another device: no remote copies, remote signals or barrier semaphores. Data moves between devices by JAX's collectives and lax.ppermute only.
A program may use at most 320 MiB of HBM per device.

```python
import math
import jax
import jax.numpy as jnp
import numpy as np
from jax import lax

D = 2048
H = 16
HD = 128
FF = 8192
LENGTH = 1024
NSEQ = 8
TOKENS = 8192


def strengthened(values, own_key, source, target, shards_of, factor):
    def block_of(position):
        return (jnp.arange(values.shape[position]) // (values.shape[position] // shards_of)).reshape((-1,) + (1,) * (values.ndim - 1 - position))

    first = jax.random.permutation(own_key, shards_of)[block_of(target)]
    far = (block_of(target) + shards_of // 2) % shards_of
    return jnp.where((block_of(source) == first) | (block_of(source) == far), factor * values, values)


def steps_of(own_key, shape, split, low, high):
    def one(dim, shards_of):
        heights = jax.random.uniform(jax.random.fold_in(jax.random.fold_in(own_key, 6), dim), (shards_of,), jnp.float32, low / len(split), high / len(split))
        return jnp.repeat(jnp.exp(heights), shape[dim] // shards_of).reshape((-1,) + (1,) * (len(shape) - dim - 1))

    factor_of = one(*split[0])
    for cut in split[1:]:
        factor_of = factor_of * one(*cut)
    return factor_of


def length_profile(count, total, reach, lean):
    portions = [(1 << 20) // math.isqrt(standing ** lean) + 1 for standing in range(2, count + 1)]
    rest, given = total - reach - (count - 1), [1] * (count - 1)
    while rest > 0:
        movable = [i for i in range(count - 1) if given[i] < reach]
        pool, remaining = sum([portions[i] for i in movable]), rest
        for i in movable:
            addition = min(reach - given[i], max(1, remaining * portions[i] // pool), rest)
            given[i] = given[i] + addition
            rest = rest - addition
    return np.array([reach] + given)


def uneven(key, amount, total, reach, skew):
    if amount == 2:
        one = jax.random.randint(key, (), max(1, total - reach), min(reach, total - 1) + 1)
        return jnp.stack([one, total - one])
    tallies = jnp.asarray(length_profile(amount, total, reach, skew), jnp.int32)
    pairs = (amount - 1) // 2
    source_of, sink = tallies[1:1 + 2 * pairs:2], tallies[2:2 + 2 * pairs:2]
    slack = jnp.minimum(source_of - 1, reach - sink)
    passed = jax.random.randint(jax.random.fold_in(key, 1), (pairs,), 0, 1 << 20) % (slack + 1)
    tallies = tallies.at[1:1 + 2 * pairs:2].set(source_of - passed).at[2:2 + 2 * pairs:2].set(sink + passed)
    return tallies[jax.random.permutation(jax.random.fold_in(key, 2), amount)]


def centred(own_key, dims, scale, most, shards=(), kind=jnp.bfloat16):
    entries = scale * jax.random.normal(own_key, dims, jnp.float32)
    if shards:
        entries = entries * steps_of(own_key, dims, shards, -0.22, 0.18)
    return jnp.clip(entries, -most, most).astype(kind)


def noise_with(stream_key, extent, deviation, most, cuts, heavy, kind=jnp.bfloat16):
    array = deviation * jax.random.normal(stream_key, extent, jnp.float32)
    if cuts:
        array = array * steps_of(stream_key, extent, cuts, -0.22, 0.18)
    return jnp.clip(strengthened(array, jax.random.fold_in(stream_key, 3), *heavy), -most, most).astype(kind)


def setup_inputs(seed: int = 0) -> dict:
    key_list = jax.random.split(jax.random.key(seed), 13)
    tokens = noise_with(key_list[0], (TOKENS, D), 1.0, 6.0, ((0, 16),), (0, 1, 16, 2.0))
    segments = jax.vmap(lambda own: jnp.searchsorted(jnp.cumsum(uneven(own, max(4, LENGTH // 64), LENGTH, LENGTH // 2, 2)), jnp.arange(LENGTH), side="right"))(jax.random.split(key_list[1], NSEQ)).reshape((NSEQ, LENGTH)).astype(jnp.int32)
    gain_attn = jnp.clip(1.0 + 0.1 * jax.random.normal(key_list[2], (D,), jnp.float32), 0.5, 1.5).astype(jnp.bfloat16)
    w_query = centred(key_list[3], (D, H * HD), D ** -0.5, 0.125, ((0, 16), (1, 2)))
    w_key = centred(key_list[4], (D, H * HD), D ** -0.5, 0.125, ((0, 16), (1, 2)))
    w_value = centred(key_list[5], (D, H * HD), D ** -0.5, 0.125, ((0, 16), (1, 2)))
    w_out = centred(key_list[6], (D, H * HD), (max(1, 2 * H * HD // LENGTH)) ** -0.5, 3.0, ((0, 16), (1, 2)))
    gain_mlp = jnp.clip(1.0 + 0.1 * jax.random.normal(key_list[7], (D,), jnp.float32), 0.5, 1.5).astype(jnp.bfloat16)
    w_gate = centred(key_list[8], (D, FF), D ** -0.5, 0.125, ((0, 16), (1, 2)))
    w_up = centred(key_list[9], (D, FF), D ** -0.5, 0.125, ((0, 16), (1, 2)))
    w_down = centred(key_list[10], (D, FF), FF ** -0.5, 0.0625, ((0, 16), (1, 2)))
    cotangent = noise_with(key_list[11], (TOKENS, D), 1.0, 6.0, ((0, 16),), (0, 1, 16, 2.0))
    return {"tokens": tokens, "segments": segments, "gain_attn": gain_attn, "w_query": w_query, "w_key": w_key, "w_value": w_value, "w_out": w_out, "gain_mlp": gain_mlp, "w_gate": w_gate, "w_up": w_up, "w_down": w_down, "cotangent": cotangent}


@jax.custom_vjp
def low(v):
    return lax.optimization_barrier(v.astype(jnp.bfloat16)).astype(jnp.float32)

@jax.custom_vjp
def low_back(v):
    return v

def low_keep(v):
    return (low(v), None)

def low_pass(kept, grad):
    return (grad,)

def back_keep(v):
    return (v, None)

def back_low(kept, grad):
    return (low(grad),)
low.defvjp(low_keep, low_pass)
low_back.defvjp(back_keep, back_low)
norm_eps = 1e-05
rope_base = 10000.0

def product(left, right):
    return jnp.dot(left, right, precision=lax.Precision.HIGHEST)

def normalize(values, gain):
    return values * lax.rsqrt(lax.optimization_barrier(jnp.mean(values * values, axis=-1, keepdims=True)) + norm_eps) * gain

def doc_positions(seg_row):
    places = jnp.arange(seg_row.shape[0], dtype=jnp.int32)
    starts_here = jnp.concatenate([jnp.ones((1,), dtype=jnp.bool_), seg_row[1:] != seg_row[:-1]])
    starts = lax.cummax(jnp.where(starts_here, places, jnp.zeros_like(places)), axis=0)
    return places - starts

def rope_tables(positions):
    half_dim = HD // 2
    freqs = rope_base ** (-(jnp.arange(half_dim, dtype=jnp.float32) * (2.0 / HD)))
    angles = positions.astype(jnp.float32)[:, None] * freqs[None, :]
    return (jnp.cos(angles)[:, None, :], jnp.sin(angles)[:, None, :])

def rotate(values, cosine, sine_table):
    half_dim = values.shape[-1] // 2
    first_half = values[..., :half_dim]
    second_half = values[..., half_dim:]
    return jnp.concatenate([first_half * cosine - second_half * sine_table, second_half * cosine + first_half * sine_table], axis=-1)

def attend(pieces):
    queries, key_rows, values, seg_row = pieces
    places = jnp.arange(seg_row.shape[0], dtype=jnp.int32)
    scores = jnp.einsum('qhd,khd->hqk', queries, key_rows, precision=lax.Precision.HIGHEST) * (1.0 / math.sqrt(HD)) - math.log(LENGTH)
    allowed = (places[:, None] >= places[None, :]) & (seg_row[:, None] == seg_row[None, :])
    weights = low(jnp.where(allowed[None], jax.nn.sigmoid(low_back(scores)), 0.0))
    return jnp.einsum('hqk,khd->qhd', weights, values, precision=lax.Precision.HIGHEST)

def block_layer(group_x, group_seg, params):
    gain_a, weight_q, weight_k, weight_v, weight_o, gain_m, weight_g, weight_u, weight_d = params
    token_count = group_x.shape[0]
    seq_count = token_count // LENGTH
    h_one = low(normalize(group_x, gain_a))
    positions = jax.vmap(doc_positions)(group_seg).reshape(token_count)
    cosine, sine_table = rope_tables(positions)
    queries = low(rotate(low_back(product(h_one, weight_q)).reshape(token_count, H, HD), cosine, sine_table))
    key_rows = low(rotate(low_back(product(h_one, weight_k)).reshape(token_count, H, HD), cosine, sine_table))
    values = low(low_back(product(h_one, weight_v))).reshape(token_count, H, HD)

    def shaped(tensor):
        return tensor.reshape(seq_count, LENGTH, H, HD)
    mixed_heads = lax.map(jax.checkpoint(attend), (shaped(queries), shaped(key_rows), shaped(values), group_seg))
    mixed_heads = low(low_back(mixed_heads.reshape(token_count, H * HD)))
    after_attn = group_x + low_back(product(mixed_heads, weight_o.T))
    h_two = low(normalize(after_attn, gain_m))
    gate_pre = low_back(product(h_two, weight_g))
    up_pre = low_back(product(h_two, weight_u))
    hidden = low(jax.nn.silu(gate_pre) * up_pre)
    return after_attn + low_back(product(hidden, weight_d.T))

def reference(tokens, segments, gain_attn, w_query, w_key, w_value, w_out, gain_mlp, w_gate, w_up, w_down, cotangent):
    seq_total = segments.shape[0]
    per_group = 4 if seq_total % 4 == 0 else 2 if seq_total % 2 == 0 else 1
    group_total = seq_total // per_group
    seg_groups = segments.reshape(group_total, per_group, LENGTH)

    def forward(x_all, params):
        x_groups = x_all.reshape(group_total, per_group * LENGTH, D)

        def group_step(scan_carry, scan_item):
            return (scan_carry, jax.checkpoint(block_layer)(scan_item[0], scan_item[1], params))
        _, group_outs = lax.scan(group_step, jnp.zeros((), jnp.float32), (x_groups, seg_groups))
        return group_outs.reshape(group_total * per_group * LENGTH, D)
    params = (gain_attn.astype(jnp.float32), w_query.astype(jnp.float32), w_key.astype(jnp.float32), w_value.astype(jnp.float32), w_out.astype(jnp.float32), gain_mlp.astype(jnp.float32), w_gate.astype(jnp.float32), w_up.astype(jnp.float32), w_down.astype(jnp.float32))
    result, pullback = jax.vjp(forward, tokens.astype(jnp.float32), params)
    grad_x, grad_params = pullback(cotangent.astype(jnp.float32))
    return (result.astype(jnp.bfloat16), grad_x.astype(jnp.bfloat16), grad_params[0], grad_params[1], grad_params[2], grad_params[3], grad_params[4], grad_params[5], grad_params[6], grad_params[7], grad_params[8])
```

```python
import math

import jax
import jax.numpy as jnp
from jax import lax
from jax.sharding import PartitionSpec as P

HD = 128
LENGTH = 1024


norm_eps = 1e-05
rope_base = 10000.0

bf16 = jnp.bfloat16
f32 = jnp.float32


def matmul(left, right):
    return jnp.dot(left, right, preferred_element_type=jnp.float32)


def contract_rows(left, right):
    return lax.dot_general(
        left, right, (((0,), (0,)), ((), ())), preferred_element_type=jnp.float32
    )


def contract_cols(left, right):
    return lax.dot_general(
        left, right, (((1,), (1,)), ((), ())), preferred_element_type=jnp.float32
    )


def norm_parts(values):
    inverse = lax.rsqrt(jnp.mean(values * values, axis=-1, keepdims=True) + norm_eps)
    return (values * inverse, inverse)


def norm_back(grad_scaled, normed, inverse):
    return inverse * (grad_scaled - normed * jnp.mean(grad_scaled * normed, axis=-1, keepdims=True))


def doc_positions(seg_row):
    places = jnp.arange(seg_row.shape[0], dtype=jnp.int32)
    starts_here = jnp.concatenate([jnp.ones((1,), dtype=jnp.bool_), seg_row[1:] != seg_row[:-1]])
    starts = lax.cummax(jnp.where(starts_here, places, jnp.zeros_like(places)), axis=0)
    return places - starts


def rope_tables(positions):
    half_dim = HD // 2
    freqs = rope_base ** (-(jnp.arange(half_dim, dtype=jnp.float32) * (2.0 / HD)))
    angles = positions.astype(jnp.float32)[:, None] * freqs[None, :]
    return (jnp.cos(angles)[:, None, :], jnp.sin(angles)[:, None, :])


def rotate(values, cosine, sine_table):
    half_dim = values.shape[-1] // 2
    first_half = values[..., :half_dim]
    second_half = values[..., half_dim:]
    return jnp.concatenate(
        [
            first_half * cosine - second_half * sine_table,
            second_half * cosine + first_half * sine_table,
        ],
        axis=-1,
    )


def unrotate(values, cosine, sine_table):
    half_dim = values.shape[-1] // 2
    first_half = values[..., :half_dim]
    second_half = values[..., half_dim:]
    return jnp.concatenate(
        [
            first_half * cosine + second_half * sine_table,
            second_half * cosine - first_half * sine_table,
        ],
        axis=-1,
    )


def visible(places, seg_row, start_row, end_row):
    rows_q = places[start_row:end_row]
    rows_k = places[:end_row]
    same_doc = seg_row[start_row:end_row][:, None] == seg_row[:end_row][None, :]
    return (rows_q[:, None] >= rows_k[None, :]) & same_doc


def block_scores(queries, key_rows, start_row, end_row):
    raw_scores = jnp.einsum(
        "qhd,khd->hqk",
        queries[start_row:end_row],
        key_rows[:end_row],
        preferred_element_type=jnp.float32,
    )
    return raw_scores * (1.0 / math.sqrt(HD)) - math.log(LENGTH)


def attend_forward(query_heads, key_heads, value_heads, seg_row):
    length = seg_row.shape[0]
    head_count = query_heads.shape[1] // HD
    queries = query_heads.reshape(length, head_count, HD)
    key_rows = key_heads.reshape(length, head_count, HD)
    value_rows = value_heads.reshape(length, head_count, HD)
    block_rows = min(512, length)
    places = jnp.arange(length, dtype=jnp.int32)
    pieces = []
    for block_number in range(length // block_rows):
        start_row = block_number * block_rows
        end_row = start_row + block_rows
        allowed = visible(places, seg_row, start_row, end_row)
        scores = block_scores(queries, key_rows, start_row, end_row)
        weights = jnp.where(allowed[None], jax.nn.sigmoid(scores), 0.0).astype(jnp.bfloat16)
        pieces.append(
            jnp.einsum(
                "hqk,khd->qhd", weights, value_rows[:end_row], preferred_element_type=jnp.float32
            )
        )
    return jnp.concatenate(pieces, axis=0).reshape(length, head_count * HD).astype(jnp.bfloat16)


def attend_backward(query_heads, key_heads, value_heads, grad_heads, seg_row, cosine, sine_table):
    length = seg_row.shape[0]
    head_count = query_heads.shape[1] // HD
    queries = query_heads.reshape(length, head_count, HD)
    key_rows = key_heads.reshape(length, head_count, HD)
    value_rows = value_heads.reshape(length, head_count, HD)
    grad_rows = grad_heads.reshape(length, head_count, HD)
    scale = 1.0 / math.sqrt(HD)
    block_rows = min(512, length)
    places = jnp.arange(length, dtype=jnp.int32)
    query_grads = []
    key_grad = jnp.zeros((length, head_count, HD), jnp.float32)
    value_grad = jnp.zeros((length, head_count, HD), jnp.float32)
    for block_number in range(length // block_rows):
        start_row = block_number * block_rows
        end_row = start_row + block_rows
        allowed = visible(places, seg_row, start_row, end_row)
        scores = block_scores(queries, key_rows, start_row, end_row)
        sig_scores = jax.nn.sigmoid(scores)
        weights = jnp.where(allowed[None], sig_scores, 0.0).astype(jnp.bfloat16)
        grad_block = grad_rows[start_row:end_row]
        value_grad = value_grad.at[:end_row].add(
            jnp.einsum("hqk,qhd->khd", weights, grad_block, preferred_element_type=jnp.float32)
        )
        grad_probs = jnp.einsum(
            "qhd,khd->hqk", grad_block, value_rows[:end_row], preferred_element_type=jnp.float32
        )
        grad_scores = jnp.where(
            allowed[None], grad_probs * sig_scores * (1.0 - sig_scores), 0.0
        ).astype(jnp.bfloat16)
        query_grads.append(
            jnp.einsum(
                "hqk,khd->qhd", grad_scores, key_rows[:end_row], preferred_element_type=jnp.float32
            )
            * scale
        )
        key_grad = key_grad.at[:end_row].add(
            jnp.einsum(
                "hqk,qhd->khd",
                grad_scores,
                queries[start_row:end_row],
                preferred_element_type=jnp.float32,
            )
            * scale
        )
    query_grad = unrotate(jnp.concatenate(query_grads, axis=0), cosine, sine_table)
    key_grad = unrotate(key_grad, cosine, sine_table)
    return jnp.concatenate(
        [
            query_grad.reshape(length, head_count * HD),
            key_grad.reshape(length, head_count * HD),
            value_grad.reshape(length, head_count * HD),
        ],
        axis=1,
    ).astype(jnp.bfloat16)


def cat(parts, axis=0):
    return jnp.concatenate(parts, axis=axis)


def rows_of(values, start, size):
    return lax.dynamic_slice_in_dim(values, start, size, 0)


def cols_of(values, start, size):
    return lax.dynamic_slice_in_dim(values, start, size, 1)


def ordered(index, own, other, axis=0):
    return jnp.where(index == 0, cat([own, other], axis), cat([other, own], axis))


def build(shards):
    far = [k << 2 for k in range(1, shards // 4)]
    line = [k << 1 for k in range(1, shards // 2)]

    def across(values, mask):
        return lax.ppermute(values, "shard", [(i, i ^ mask) for i in range(shards)])

    def swap_core(values):
        return lax.ppermute(values, "ctx", [(0, 1), (1, 0)])

    def swap_tp(values):
        return lax.ppermute(values, "tp", [(0, 1), (1, 0)])

    order = [(m << 1) | y for y in (0, 1) for m in range(shards // 2)]

    def gather_line(block):
        near = [block] + [across(block, mask) for mask in line]
        return cat(near + [across(part, 1) for part in near])

    def gather_far(block):
        near = [block] + [across(block, mask) for mask in far]
        return cat(near + [across(part, 1) for part in near])

    def per_device(
        tokens,
        segments,
        gain_attn,
        w_query,
        w_key,
        w_value,
        w_out,
        gain_mlp,
        w_gate,
        w_up,
        w_down,
        cotangent,
    ):
        shard = lax.axis_index("shard")
        core = lax.axis_index("ctx")
        half = lax.axis_index("tp")
        zl = (shard >> 1) & 1
        rows, width = tokens.shape
        part = rows // 2
        block = width // shards
        unit = block // 2
        n_attn = w_query.shape[1] // 2
        n_ff = w_gate.shape[1] // 4

        def relative(values):
            return cat([cols_of(values, (shard ^ mask) * block, block) for mask in order], 1)

        def natural(values):
            place = {mask: i for i, mask in enumerate(order)}
            spread = cat([values[:, place[m] * block : (place[m] + 1) * block] for m in range(shards)], 1)
            return cat([cols_of(spread, (shard ^ m) * block, block) for m in range(shards)], 1)

        def flip_zl(values):
            split = values.reshape(values.shape[0], shards // 2, 2, block)
            return jnp.where(zl == 0, split, split[:, :, ::-1]).reshape(values.shape)

        gains = jnp.stack([gain_attn, gain_mlp])
        gains = ordered(core, gains, swap_core(gains), 1)
        for bit in range(1, shards.bit_length() - 1):
            gains = cat([gains, across(gains, 1 << bit)], 1)
        gains = cat([gains, across(gains, 1)], 1).astype(f32)
        gain_a, gain_m = gains[0:1], gains[1:2]

        def core_rows(weights):
            each = [w.shape[1] // 2 for w in weights]
            keep = cat([cols_of(w, core * n, n) for w, n in zip(weights, each)], 1)
            send = cat([cols_of(w, (1 - core) * n, n) for w, n in zip(weights, each)], 1)
            return ordered(core, keep, swap_core(send))

        block_a = core_rows([w_query, w_key, w_value, w_out])
        weight_qkv = gather_line(block_a[:, : 3 * n_attn])
        weight_o = gather_line(block_a[:, 3 * n_attn :])

        block_f = core_rows([w_gate, w_up, w_down])

        def ff_weight(i):
            own = block_f[:, i * 2 * n_ff : (i + 1) * 2 * n_ff]
            keep = cols_of(own, zl * n_ff, n_ff)
            send = cols_of(own, (1 - zl) * n_ff, n_ff)
            return gather_far(ordered(zl, keep, across(send, 2)))

        weight_g, weight_u, weight_d = ff_weight(0), ff_weight(1), ff_weight(2)

        seg_row = segments[0]
        cosine, sine_table = rope_tables(doc_positions(seg_row))
        length = seg_row.shape[0]
        heads = n_attn // HD
        x_rel = relative(tokens).astype(f32)
        normed_one, inverse_one = norm_parts(x_rel)
        h_own = (normed_one * gain_a).astype(bf16)
        h_one = ordered(core, h_own, swap_core(h_own))
        qkv = matmul(h_one, weight_qkv)
        query = rotate(qkv[:, :n_attn].reshape(length, heads, HD), cosine, sine_table)
        query = query.reshape(length, n_attn).astype(bf16)
        key = rotate(qkv[:, n_attn : 2 * n_attn].reshape(length, heads, HD), cosine, sine_table)
        key = key.reshape(length, n_attn).astype(bf16)
        value = qkv[:, 2 * n_attn :].astype(bf16)
        mixed = attend_forward(query, key, value, seg_row)

        def to_slice(operand, project):
            away = project(rows_of(operand, (1 - core) * rows, rows)).astype(bf16)
            here = rows_of(operand, core * rows, rows)
            away = swap_core(away)
            other = project(rows_of(here, (1 - half) * part, part)) + rows_of(
                away, (1 - half) * part, part
            ).astype(f32)
            other = swap_tp(other.astype(bf16))
            own = project(rows_of(here, half * part, part)) + rows_of(
                away, half * part, part
            ).astype(f32)
            return own + other.astype(f32)

        x_part = rows_of(x_rel, half * part, part)
        after_attn = x_part + to_slice(mixed, lambda v: contract_cols(v, weight_o))
        normed_two, inverse_two = norm_parts(after_attn)
        h_part = flip_zl((normed_two * gain_m).astype(bf16))

        def spread_tokens(own):
            by_tp, by_zl = swap_tp(own), across(own, 2)
            mid = own.shape[0] // 2
            both = cat([across(by_tp[:mid], 2), swap_tp(by_zl[mid:])])
            near = [own, by_tp, by_zl, both]
            return cat(near + [swap_core(v) for v in near])

        h_two = spread_tokens(h_part)
        dy_rel = relative(cotangent)
        dy_ff = flip_zl(cat([rows_of(dy_rel, half * part, part), rows_of(dy_rel, (1 - half) * part, part)]))
        dy_zl = across(dy_ff[:part], 2)
        near = [dy_ff, dy_zl, swap_tp(dy_zl)]
        grad_out = cat(near + [swap_core(v) for v in near])

        gate_pre = matmul(h_two, weight_g)
        up_pre = matmul(h_two, weight_u)
        gate_sig = jax.nn.sigmoid(gate_pre)
        gate_act = gate_pre * gate_sig
        hidden = (gate_act * up_pre).astype(bf16)

        def from_tokens(project):
            count = 4 * part
            away = swap_core(project(slice(count, 2 * count)).astype(bf16))
            total = project(slice(0, count)) + away.astype(f32)
            mid = width // 2
            low, high = total[:, :mid], total[:, mid:]

            def pick(values, i):
                return values[i * part : (i + 1) * part]

            low_tp = swap_tp(cat([pick(low, 1), pick(low, 3)]).astype(bf16)).astype(f32)
            high_zl = across(cat([pick(high, 2), pick(high, 3)]).astype(bf16), 2).astype(f32)
            low_zl = across((pick(low, 2) + pick(low_tp, 1)).astype(bf16), 2).astype(f32)
            high_tp = swap_tp((pick(high, 1) + pick(high_zl, 1)).astype(bf16)).astype(f32)
            low_sum = pick(low, 0) + pick(low_tp, 0) + low_zl
            high_sum = pick(high, 0) + pick(high_zl, 0) + high_tp
            return flip_zl(cat([low_sum, high_sum], 1))

        mlp = from_tokens(lambda where: contract_cols(hidden[where], weight_d))
        out_part = (after_attn + mlp).astype(bf16)
        output = natural(ordered(half, out_part, swap_tp(out_part)))

        grad_hidden = matmul(grad_out, weight_d)
        grad_gate = (grad_hidden * up_pre * gate_sig * (1.0 + gate_pre * (1.0 - gate_sig))).astype(bf16)
        grad_up = (grad_hidden * gate_act).astype(bf16)
        grad_h_two = from_tokens(
            lambda where: contract_cols(grad_gate[where], weight_g)
            + contract_cols(grad_up[where], weight_u)
        )

        def rows_far(left, right):
            mid = width // 2
            away = across(contract_rows(left[:, mid:], right).astype(bf16), 1)
            total = contract_rows(left[:, :mid], right) + away.astype(f32)
            step = 2 * block
            own = total[:step]
            for i, mask in enumerate(far):
                sent = total[(i + 1) * step : (i + 2) * step].astype(bf16)
                own = own + across(sent, mask).astype(f32)
            own = own.astype(bf16)
            other = across(rows_of(own, (1 - zl) * block, block), 2)
            own = ordered(zl, rows_of(own, zl * block, block), other, 1)
            other = swap_core(rows_of(own, (1 - core) * unit, unit))
            return ordered(core, rows_of(own, core * unit, unit), other, 1).astype(f32)

        grad_w_down = rows_far(grad_out, hidden)
        grad_w_gate = rows_far(h_two, grad_gate)
        grad_w_up = rows_far(h_two, grad_up)

        grad_gain_m = jnp.sum(grad_h_two * normed_two, axis=0, keepdims=True)
        dy_part = rows_of(dy_rel, half * part, part).astype(f32)
        grad_after = dy_part + norm_back(grad_h_two * gain_m, normed_two, inverse_two)

        grad_part = grad_after.astype(bf16)
        grad_half = ordered(half, grad_part, swap_tp(grad_part))
        grad_attn = ordered(core, grad_half, swap_core(grad_half))
        grad_mixed = matmul(grad_attn, weight_o).astype(bf16)

        def rows_line(left, right):
            mid = width // 2
            away = across(contract_rows(left[:, mid:], right).astype(bf16), 1)
            total = contract_rows(left[:, :mid], right) + away.astype(f32)
            own = total[:block]
            for i, mask in enumerate(line):
                sent = total[(i + 1) * block : (i + 2) * block].astype(bf16)
                own = own + across(sent, mask).astype(f32)
            other = swap_core(rows_of(own, (1 - core) * unit, unit).astype(bf16))
            return ordered(core, rows_of(own, core * unit, unit), other.astype(f32), 1)

        grad_w_out = rows_line(grad_attn, mixed)
        grad_qkv = attend_backward(query, key, value, grad_mixed, seg_row, cosine, sine_table)
        grad_w_query = rows_line(h_one, grad_qkv[:, :n_attn])
        grad_w_key = rows_line(h_one, grad_qkv[:, n_attn : 2 * n_attn])
        grad_w_value = rows_line(h_one, grad_qkv[:, 2 * n_attn :])
        grad_h_one = to_slice(grad_qkv, lambda v: contract_cols(v, weight_qkv))
        normed_part = rows_of(normed_one, half * part, part)
        inverse_part = rows_of(inverse_one, half * part, part)
        grad_gain_a = jnp.sum(grad_h_one * normed_part, axis=0, keepdims=True)
        grad_x = (grad_after + norm_back(grad_h_one * gain_a, normed_part, inverse_part)).astype(bf16)
        grad_tokens = natural(ordered(half, grad_x, swap_tp(grad_x)))

        grad_gains = cat([grad_gain_a, grad_gain_m])
        grad_gains = grad_gains + swap_tp(grad_gains)
        for mask in [1] + [1 << bit for bit in range(shards.bit_length() - 2, 0, -1)]:
            mid = grad_gains.shape[1] // 2
            grad_gains = grad_gains[:, :mid] + across(grad_gains[:, mid:], mask)
        grad_gains = cols_of(grad_gains, core * unit, unit) + swap_core(
            cols_of(grad_gains, (1 - core) * unit, unit)
        )

        return (
            output,
            grad_tokens,
            grad_gains[0],
            grad_w_query,
            grad_w_key,
            grad_w_value,
            grad_w_out,
            grad_gains[1],
            grad_w_gate,
            grad_w_up,
            grad_w_down,
        )

    return per_device


def solution(mesh):
    wide = P(("shard", "ctx"), None)
    flat = P(("shard", "ctx"))
    both = P(("shard", "ctx"), "tp")
    placed = (wide, P("shard", None), flat, both, both, both, both, flat, both, both, both, wide)
    return jax.shard_map(
        build(mesh.shape["shard"]),
        mesh=mesh,
        in_specs=placed,
        out_specs=(wide, wide, flat, both, both, both, both, flat, both, both, both),
        check_vma=False,
    )
```

```python
import math

import jax
import jax.numpy as jnp
from jax import lax
from jax.experimental import pallas as pl
from jax.experimental.pallas import tpu as pltpu
from jax.sharding import PartitionSpec as P

HD = 128
LENGTH = 1024


norm_eps = 1e-05
rope_base = 10000.0

bf16 = jnp.bfloat16
f32 = jnp.float32


def matmul(left, right):
    return jnp.dot(left, right, preferred_element_type=jnp.float32)


def contract_rows(left, right):
    return lax.dot_general(
        left, right, (((0,), (0,)), ((), ())), preferred_element_type=jnp.float32
    )


def contract_cols(left, right):
    return lax.dot_general(
        left, right, (((1,), (1,)), ((), ())), preferred_element_type=jnp.float32
    )


def norm_parts(values):
    inverse = lax.rsqrt(jnp.mean(values * values, axis=-1, keepdims=True) + norm_eps)
    return (values * inverse, inverse)


def norm_back(grad_scaled, normed, inverse):
    return inverse * (grad_scaled - normed * jnp.mean(grad_scaled * normed, axis=-1, keepdims=True))


def doc_positions(seg_row):
    places = jnp.arange(seg_row.shape[0], dtype=jnp.int32)
    starts_here = jnp.concatenate([jnp.ones((1,), dtype=jnp.bool_), seg_row[1:] != seg_row[:-1]])
    starts = lax.cummax(jnp.where(starts_here, places, jnp.zeros_like(places)), axis=0)
    return places - starts


def rope_tables(positions):
    half_dim = HD // 2
    freqs = rope_base ** (-(jnp.arange(half_dim, dtype=jnp.float32) * (2.0 / HD)))
    angles = positions.astype(jnp.float32)[:, None] * freqs[None, :]
    cosine, sine = jnp.cos(angles), jnp.sin(angles)
    return cat([cosine, cosine], 1), cat([-sine, sine], 1)


def cat(parts, axis=0):
    return jnp.concatenate(parts, axis=axis)


def rows_of(values, start, size):
    return lax.dynamic_slice_in_dim(values, start, size, 0)


def ordered(index, own, other, axis=0):
    return jnp.where(index == 0, cat([own, other], axis), cat([other, own], axis))


def after(values, *events):
    return lax.optimization_barrier((values, events))[0]


def small_call(body, scalars, arrays, outs):
    scalars = jnp.stack([jnp.asarray(v, jnp.int32) for v in scalars])
    return pl.pallas_call(
        body,
        grid_spec=pltpu.PrefetchScalarGridSpec(
            num_scalar_prefetch=1,
            grid=(1,),
            in_specs=[pl.BlockSpec(a.shape, lambda i, s: (0, 0)) for a in arrays],
            out_specs=[pl.BlockSpec(o.shape, lambda i, s: (0, 0)) for o in outs],
        ),
        out_shape=outs,
    )(scalars, *arrays)


def array_of(rows, cols, dtype=bf16):
    return jax.ShapeDtypeStruct((rows, cols), dtype)


def permute_cols(values, index, block):
    rows, width = values.shape
    step = min(rows, 128)
    count = width // block
    if block % 128:
        return cat([lax.dynamic_slice_in_dim(values, index[j] * block, block, 1) for j in range(count)], 1)

    def body(index_ref, in_ref, out_ref):
        for j in range(count):
            start = pl.multiple_of(index_ref[j] * block, block)
            out_ref[:, j * block : (j + 1) * block] = in_ref[:, pl.ds(start, block)]

    spec = pl.BlockSpec((step, width), lambda i, s: (i, 0))
    return pl.pallas_call(
        body,
        grid_spec=pltpu.PrefetchScalarGridSpec(
            num_scalar_prefetch=1, grid=(rows // step,), in_specs=[spec], out_specs=spec
        ),
        out_shape=jax.ShapeDtypeStruct(values.shape, values.dtype),
    )(index, values)


def join_tokens(own, other, half, index, block):
    rows, width = own.shape
    count = width // block
    if block % 128:
        return permute_cols(ordered(half, own, other), index, block)

    def body(index_ref, own_ref, other_ref, out_ref):
        here = pl.program_id(0) == index_ref[count]

        def move(ref):
            for j in range(count):
                start = pl.multiple_of(index_ref[j] * block, block)
                out_ref[:, j * block : (j + 1) * block] = ref[:, pl.ds(start, block)]

        pl.when(here)(lambda: move(own_ref))
        pl.when(jnp.logical_not(here))(lambda: move(other_ref))

    whole = pl.BlockSpec((rows, width), lambda i, s: (0, 0))
    return pl.pallas_call(
        body,
        grid_spec=pltpu.PrefetchScalarGridSpec(
            num_scalar_prefetch=1,
            grid=(2,),
            in_specs=[whole, whole],
            out_specs=pl.BlockSpec((rows, width), lambda i, s: (i, 0)),
        ),
        out_shape=jax.ShapeDtypeStruct((2 * rows, width), own.dtype),
    )(cat([index, half[None]]), own, other)


def score_parts(query, keys, rows_seg, cols_seg, diagonal):
    scores = contract_cols(query, keys) * (1.0 / math.sqrt(HD)) - math.log(LENGTH)
    allowed = rows_seg == cols_seg
    if diagonal:
        size = query.shape[0]
        places = lax.broadcasted_iota(jnp.int32, (size, size), 0)
        allowed = allowed & (places >= lax.broadcasted_iota(jnp.int32, (size, size), 1))
    return jax.nn.sigmoid(scores), allowed


def swap_halves(values):
    return pltpu.roll(values, HD // 2, 1)


def attend_forward(qkv, seg_row, cosine, sine, tile=256):
    length = seg_row.shape[0]
    heads = qkv.shape[1] // (3 * HD)
    tiles = length // tile

    def body(seg_ref, qkv_ref, cos_ref, sin_ref, seg_col, seg_line, out_ref, kept_ref, acc):
        cos_t, sin_t = cos_ref[...], sin_ref[...]
        for part in (0, 1):
            where = slice(part * HD, (part + 1) * HD)
            value = qkv_ref[:, where]
            kept_ref[:, where] = (value * cos_t + swap_halves(value) * sin_t).astype(bf16)
        kept_ref[:, 2 * HD :] = qkv_ref[:, 2 * HD :].astype(bf16)
        for i in range(tiles):
            rows = slice(i * tile, (i + 1) * tile)

            def step(j, diagonal, rows=rows):
                cols = slice(j * tile, (j + 1) * tile)
                sig, allowed = score_parts(
                    kept_ref[rows, :HD], kept_ref[cols, HD : 2 * HD],
                    seg_col[rows, :], seg_line[:, cols], diagonal,
                )
                weights = jnp.where(allowed, sig, 0.0).astype(bf16)
                return matmul(weights, kept_ref[cols, 2 * HD :])

            acc[...] = step(i, True)
            for j in range(i):

                @pl.when(seg_ref[(j + 1) * tile - 1] == seg_ref[i * tile])
                def _(j=j):
                    acc[...] += step(j, False)

            out_ref[rows, :] = acc[...].astype(bf16)

    full = pl.BlockSpec((length, HD), lambda h, s: (0, 0))
    return pl.pallas_call(
        body,
        grid_spec=pltpu.PrefetchScalarGridSpec(
            num_scalar_prefetch=1,
            grid=(heads,),
            in_specs=[
                pl.BlockSpec((length, 3 * HD), lambda h, s: (0, h)),
                full,
                full,
                pl.BlockSpec((length, 1), lambda h, s: (0, 0)),
                pl.BlockSpec((1, length), lambda h, s: (0, 0)),
            ],
            out_specs=[
                pl.BlockSpec((length, HD), lambda h, s: (0, h)),
                pl.BlockSpec((length, 3 * HD), lambda h, s: (0, h)),
            ],
            scratch_shapes=[pltpu.VMEM((tile, HD), f32)],
        ),
        out_shape=[array_of(length, heads * HD), array_of(length, 3 * heads * HD)],
    )(seg_row, qkv, cosine, sine, seg_row[:, None], seg_row[None, :])


def attend_backward(kept, grad_heads, seg_row, cosine, sine, first, heads, tile=256):
    length = seg_row.shape[0]
    tiles = length // tile
    scale = 1.0 / math.sqrt(HD)

    def body(seg_ref, kept_ref, do_ref, cos_ref, sin_ref, seg_col, seg_line, out_ref, dq, dk, dv):
        dk[...] = jnp.zeros_like(dk)
        dv[...] = jnp.zeros_like(dv)
        for i in range(tiles):
            rows = slice(i * tile, (i + 1) * tile)

            def step(j, diagonal, rows=rows):
                cols = slice(j * tile, (j + 1) * tile)
                query, grad = kept_ref[rows, :HD], do_ref[rows, :]
                keys = kept_ref[cols, HD : 2 * HD]
                sig, allowed = score_parts(query, keys, seg_col[rows, :], seg_line[:, cols], diagonal)
                weights = jnp.where(allowed, sig, 0.0).astype(bf16)
                dv[cols, :] += contract_rows(weights, grad)
                grad_probs = contract_cols(grad, kept_ref[cols, 2 * HD :])
                grad_scores = jnp.where(allowed, grad_probs * sig * (1.0 - sig), 0.0).astype(bf16)
                dk[cols, :] += contract_rows(grad_scores, query)
                return matmul(grad_scores, keys)

            dq[rows, :] = step(i, True)
            for j in range(i):

                @pl.when(seg_ref[(j + 1) * tile - 1] == seg_ref[i * tile])
                def _(j=j, rows=rows):
                    dq[rows, :] += step(j, False)

        cos_t, sin_t = cos_ref[...], sin_ref[...]
        for part, ref in ((0, dq), (1, dk)):
            grad = ref[...] * scale
            out_ref[:, part * HD : (part + 1) * HD] = (grad * cos_t - swap_halves(grad) * sin_t).astype(bf16)
        out_ref[:, 2 * HD :] = dv[...].astype(bf16)

    full = pl.BlockSpec((length, HD), lambda h, s: (0, 0))
    return pl.pallas_call(
        body,
        grid_spec=pltpu.PrefetchScalarGridSpec(
            num_scalar_prefetch=1,
            grid=(heads,),
            in_specs=[
                pl.BlockSpec((length, 3 * HD), lambda h, s: (0, first + h)),
                pl.BlockSpec((length, HD), lambda h, s: (0, first + h)),
                full,
                full,
                pl.BlockSpec((length, 1), lambda h, s: (0, 0)),
                pl.BlockSpec((1, length), lambda h, s: (0, 0)),
            ],
            out_specs=pl.BlockSpec((length, 3 * HD), lambda h, s: (0, h)),
            scratch_shapes=[pltpu.VMEM((length, HD), f32)] * 3,
        ),
        out_shape=array_of(length, 3 * heads * HD),
    )(seg_row, kept, grad_heads, cosine, sine, seg_row[:, None], seg_row[None, :])


def build(shards):
    far = [k << 2 for k in range(1, shards // 4)]
    line = [k << 1 for k in range(1, shards // 2)]

    def across(values, mask):
        return lax.ppermute(values, "shard", [(i, i ^ mask) for i in range(shards)])

    def swap_core(values):
        return lax.ppermute(values, "ctx", [(0, 1), (1, 0)])

    def swap_tp(values):
        return lax.ppermute(values, "tp", [(0, 1), (1, 0)])

    def per_device(
        tokens,
        segments,
        gain_attn,
        w_query,
        w_key,
        w_value,
        w_out,
        gain_mlp,
        w_gate,
        w_up,
        w_down,
        cotangent,
    ):
        shard = lax.axis_index("shard").astype(jnp.int32)
        core = lax.axis_index("ctx").astype(jnp.int32)
        half = lax.axis_index("tp").astype(jnp.int32)
        y, zl = shard & 1, (shard >> 1) & 1
        rows, width = tokens.shape
        part = rows // 2
        block = width // shards
        unit = block // 2
        n_attn = w_query.shape[1] // 2
        n_ff = w_gate.shape[1] // 4
        heads = n_attn // HD
        half_s = shards // 2
        pad = 16

        place = jnp.arange(shards, dtype=jnp.int32)
        rel = (((shard >> 2) ^ ((place % half_s) >> 1)) << 2) | ((place & 1) << 1) | (y ^ (place // half_s))
        nat = ((y ^ (place & 1)) * half_s) | (((shard >> 2) ^ (place >> 2)) << 1) | ((place >> 1) & 1)

        attn_w = [w_query, w_key, w_value, w_out]
        ff_w = [w_gate, w_up, w_down]

        def send_attn(s_ref, q, k, v, o, out):
            start = pl.multiple_of((1 - s_ref[0]) * n_attn, n_attn)
            for h in range(heads):
                for i, ref in enumerate((q, k, v)):
                    out[:, (3 * h + i) * HD : (3 * h + i + 1) * HD] = ref[:, pl.ds(start + h * HD, HD)]
            out[:, 3 * n_attn :] = o[:, pl.ds(start, n_attn)]

        (sent_a,) = small_call(send_attn, [core], attn_w, [array_of(unit, 4 * n_attn)])
        other_a = swap_core(sent_a)
        gains = jnp.stack([gain_attn, gain_mlp])
        other_gains = swap_core(gains)

        def keep_attn(s_ref, q, k, v, o, other, own_g, other_g, out_qkv, out_o):
            me = s_ref[0]
            start = pl.multiple_of(me * n_attn, n_attn)
            mine, theirs = pl.ds(me * unit, unit), pl.ds((1 - me) * unit, unit)
            for h in range(heads):
                for i, ref in enumerate((q, k, v)):
                    where = slice((3 * h + i) * HD, (3 * h + i + 1) * HD)
                    out_qkv[mine, where] = ref[:, pl.ds(start + h * HD, HD)]
            out_o[mine, :] = o[:, pl.ds(start, n_attn)]
            out_qkv[theirs, :] = other[:, : 3 * n_attn]
            out_o[theirs, :] = other[:, 3 * n_attn :]
            first, second = own_g[...], other_g[...]
            low = jnp.where(me == 0, first, second)
            high = jnp.where(me == 0, second, first)
            line_g = cat([low, high, jnp.zeros((2, 3 * n_attn - block), bf16)], 1)
            out_qkv[block:, :] = cat([line_g, jnp.zeros((pad - 2, 3 * n_attn), bf16)])

        block_qkv, block_o = small_call(
            keep_attn, [core], attn_w + [other_a, gains, other_gains],
            [array_of(block + pad, 3 * n_attn), array_of(block, n_attn)],
        )

        def gather_line(own, gate):
            near = [own] + [across(own, mask) for mask in line]
            return near + [across(v, 1) for v in near]

        def place_line(parts, take):
            full = jnp.zeros((width, parts[0].shape[1]), bf16)
            for i, v in enumerate(parts):
                where = (i & ~1) | ((i & 1) ^ zl)
                full = lax.dynamic_update_slice_in_dim(full, take(v), where * block, 0)
            return full

        parts_qkv = gather_line(block_qkv, None)
        weight_qkv = place_line(parts_qkv, lambda v: v[:block])
        gain_rows = [v[block : block + 2, :block] for v in parts_qkv]
        gain_pairs = [ordered(zl, gain_rows[i], gain_rows[i + 1], 1) for i in range(0, shards, 2)]
        gains_rel = cat(gain_pairs, 1).astype(f32)
        gain_a, gain_m = gains_rel[0:1], gains_rel[1:2]

        block_o = after(block_o, parts_qkv[1])
        parts_o = gather_line(block_o, None)
        weight_o = place_line(parts_o, lambda v: v)

        def send_ff(s_ref, g, u, d, out):
            start = pl.multiple_of((1 - s_ref[0]) * 2 * n_ff, n_ff)
            for i, ref in enumerate((g, u, d)):
                out[:, i * 2 * n_ff : (i + 1) * 2 * n_ff] = ref[:, pl.ds(start, 2 * n_ff)]

        (sent_f,) = small_call(send_ff, [core], [after(w_gate, other_a)] + ff_w[1:], [array_of(unit, 6 * n_ff)])
        other_f = swap_core(sent_f)

        def keep_ff(s_ref, w, other, keep, send):
            me, low = s_ref[0], s_ref[1]
            mine, theirs = pl.ds(me * unit, unit), pl.ds((1 - me) * unit, unit)
            for out, which in ((keep, low), (send, 1 - low)):
                start = pl.multiple_of(which * n_ff, n_ff)
                out[mine, :] = w[:, pl.ds(pl.multiple_of(me * 2 * n_ff, n_ff) + start, n_ff)]
                out[theirs, :] = other[:, pl.ds(start, n_ff)]

        def pair_rows(s_ref, own, other, out):
            low = s_ref[0]
            out[pl.ds(low * block, block), :] = own[...]
            out[pl.ds((1 - low) * block, block), :] = other[...]

        def ff_weight(i, gate):
            keep, send = small_call(
                keep_ff, [core, zl], [ff_w[i], other_f[:, i * 2 * n_ff : (i + 1) * 2 * n_ff]],
                [array_of(block, n_ff)] * 2,
            )
            send = after(send, gate)
            (own,) = small_call(pair_rows, [zl], [keep, across(send, 2)], [array_of(2 * block, n_ff)])
            near = [own] + [across(own, mask) for mask in far]
            return near[1], cat(near + [across(v, 1) for v in near])

        event_g, weight_g = ff_weight(0, parts_o[1])
        event_u, weight_u = ff_weight(1, event_g)
        event_d, weight_d = ff_weight(2, event_u)

        seg_row = segments[0]
        cosine, sine = rope_tables(doc_positions(seg_row))
        x_own = permute_cols(tokens, rel, block)
        x_both = ordered(core, x_own, swap_core(x_own))
        normed_all, inverse_all = norm_parts(x_both.astype(f32))
        h_one = (normed_all * gain_a).astype(bf16)
        qkv = matmul(h_one, weight_qkv)
        mixed, kept = attend_forward(qkv, seg_row, cosine, sine)

        def to_slice(operand, project):
            away = project(rows_of(operand, (1 - core) * rows, rows)).astype(bf16)
            here = rows_of(operand, core * rows, rows)
            away = swap_core(away)
            other = project(rows_of(here, (1 - half) * part, part)) + rows_of(
                away, (1 - half) * part, part
            ).astype(f32)
            other = swap_tp(other.astype(bf16))
            own = project(rows_of(here, half * part, part)) + rows_of(
                away, half * part, part
            ).astype(f32)
            return own + other.astype(f32)

        x_part = rows_of(x_own, half * part, part).astype(f32)
        after_attn = x_part + to_slice(mixed, lambda v: contract_cols(v, weight_o))
        normed_two, inverse_two = norm_parts(after_attn)
        h_part = (normed_two * gain_m).astype(bf16)

        by_tp, by_zl = swap_tp(h_part), across(h_part, 2)
        mid = part // 2
        near = cat([h_part, by_tp, by_zl])
        far_near = swap_core(near)
        both = cat([across(by_tp[:mid], 2), swap_tp(by_zl[mid:])])
        h_two = cat([near, both, far_near, swap_core(both)])

        dy_rel = permute_cols(after(cotangent, event_g), rel, block)
        dy_ff = cat([rows_of(dy_rel, half * part, part), rows_of(dy_rel, (1 - half) * part, part)])
        dy_zl = across(dy_ff[:part], 2)
        near = cat([dy_ff, dy_zl, swap_tp(dy_zl)])
        grad_out = cat([near, swap_core(near)])

        gate_pre = matmul(h_two, weight_g)
        up_pre = matmul(h_two, weight_u)
        gate_sig = jax.nn.sigmoid(gate_pre)
        gate_act = gate_pre * gate_sig
        hidden = (gate_act * up_pre).astype(bf16)

        def from_tokens(project):
            count = 4 * part
            away = swap_core(project(slice(count, 2 * count)).astype(bf16))
            total = project(slice(0, count)) + away.astype(f32)
            mid = width // 2
            low, high = total[:, :mid], total[:, mid:]

            def pick(values, i):
                return values[i * part : (i + 1) * part]

            low_tp = swap_tp(cat([pick(low, 1), pick(low, 3)]).astype(bf16)).astype(f32)
            high_zl = across(cat([pick(high, 2), pick(high, 3)]).astype(bf16), 2).astype(f32)
            low_zl = across((pick(low, 2) + pick(low_tp, 1)).astype(bf16), 2).astype(f32)
            high_tp = swap_tp((pick(high, 1) + pick(high_zl, 1)).astype(bf16)).astype(f32)
            low_sum = pick(low, 0) + pick(low_tp, 0) + low_zl
            high_sum = pick(high, 0) + pick(high_zl, 0) + high_tp
            return away, cat([low_sum, high_sum], 1)

        grad_hidden = matmul(grad_out, weight_d)
        grad_gate = (grad_hidden * up_pre * gate_sig * (1.0 + gate_pre * (1.0 - gate_sig))).astype(bf16)
        grad_up = (grad_hidden * gate_act).astype(bf16)
        event_h, grad_h_two = from_tokens(
            lambda where: contract_cols(grad_gate[where], weight_g)
            + contract_cols(grad_up[where], weight_u)
        )
        late_gate, late_up, late_hidden = after((grad_gate, grad_up, hidden), event_h)

        def away_rows(left, right, mask=1):
            return across(contract_rows(left[:, width // 2 :], right).astype(bf16), mask)

        away_d = away_rows(grad_out, late_hidden)
        away_g = away_rows(h_two, late_gate)
        away_u = away_rows(h_two, late_up)
        late_hidden = after(late_hidden, grad_h_two)
        event_m, mlp = from_tokens(lambda where: contract_cols(late_hidden[where], weight_d))
        out_part = (after_attn + mlp).astype(bf16)
        output = join_tokens(out_part, swap_tp(out_part), half, nat, block)

        grad_gain_m = jnp.sum(grad_h_two * normed_two, axis=0, keepdims=True)
        dy_part = rows_of(dy_rel, half * part, part).astype(f32)
        grad_after = dy_part + norm_back(grad_h_two * gain_m, normed_two, inverse_two)

        grad_part = grad_after.astype(bf16)
        grad_half = ordered(half, grad_part, swap_tp(grad_part))
        grad_attn = ordered(core, grad_half, swap_core(grad_half))
        grad_mixed = matmul(grad_attn, weight_o).astype(bf16)

        def rows_far(left, right, away, event):
            away = after(away, event)
            total = contract_rows(left[:, : width // 2], right) + away.astype(f32)
            step = 2 * block
            own = total[:step]
            for i, mask in enumerate(far):
                sent = total[(i + 1) * step : (i + 2) * step].astype(bf16)
                own = own + across(sent, mask).astype(f32)
            own = own.astype(bf16)
            other = across(rows_of(own, (1 - zl) * block, block), 2)

            def send_rows(s_ref, mine, theirs, out):
                low, away_rows = s_ref[1], (1 - s_ref[0]) * unit
                out[:, pl.ds(pl.multiple_of(low * n_ff, n_ff), n_ff)] = mine[pl.ds(low * block + away_rows, unit), :]
                out[:, pl.ds(pl.multiple_of((1 - low) * n_ff, n_ff), n_ff)] = theirs[pl.ds(away_rows, unit), :]

            (sent,) = small_call(send_rows, [core, zl], [own, other], [array_of(unit, 2 * n_ff)])
            third = swap_core(sent)

            def join_rows(s_ref, mine, theirs, third_ref, out):
                me, low = s_ref[0], s_ref[1]
                start = pl.multiple_of(me * 2 * n_ff, n_ff)
                out[:, pl.ds(start + pl.multiple_of(low * n_ff, n_ff), n_ff)] = mine[
                    pl.ds(low * block + me * unit, unit), :
                ].astype(f32)
                out[:, pl.ds(start + pl.multiple_of((1 - low) * n_ff, n_ff), n_ff)] = theirs[
                    pl.ds(me * unit, unit), :
                ].astype(f32)
                out[:, pl.ds(pl.multiple_of((1 - me) * 2 * n_ff, n_ff), 2 * n_ff)] = third_ref[...].astype(f32)

            (full,) = small_call(join_rows, [core, zl], [own, other, third], [array_of(unit, 4 * n_ff, f32)])
            return full

        def rows_line(left, right, away, event):
            if event is not None:
                away = after(away, event)
            total = contract_rows(left[:, : width // 2], right) + away.astype(f32)
            own = rows_of(total, zl * block, block)
            for i, mask in enumerate(line):
                k = i + 1
                where = (k & ~1) | ((k & 1) ^ zl)
                sent = rows_of(total, where * block, block).astype(bf16)
                own = own + across(sent, mask).astype(f32)
            return own

        def send_unit(s_ref, own, out):
            out[...] = own[pl.ds((1 - s_ref[0]) * unit, unit), :].astype(bf16)

        away_o = away_rows(grad_attn, mixed)
        first_heads = heads // 2
        n_first = 3 * first_heads * HD
        grad_low = attend_backward(kept, grad_mixed, seg_row, cosine, sine, 0, first_heads)
        away_low = away_rows(h_one, grad_low)
        grad_high = attend_backward(kept, grad_mixed, seg_row, cosine, sine, first_heads, heads - first_heads)
        away_high = away_rows(h_one, grad_high)
        grad_qkv = cat([grad_low, grad_high], 1)

        event_q = grad_mixed
        grad_w_down = rows_far(grad_out, late_hidden, away_d, event_q)
        grad_w_gate = rows_far(h_two, late_gate, away_g, event_q)
        grad_w_up = rows_far(h_two, late_up, away_u, event_q)

        grad_h_one = to_slice(grad_qkv, lambda v: contract_cols(v, weight_qkv))

        own_o = rows_line(grad_attn, mixed, away_o, None)
        own_low = rows_line(h_one, grad_low, away_low, None)
        own_high = rows_line(h_one, grad_high, away_high, None)
        own_a = cat([own_low, own_high, own_o], 1)
        (sent_g,) = small_call(send_unit, [core], [own_a], [array_of(unit, 4 * n_attn)])
        other_a = swap_core(sent_g)

        def join_attn(s_ref, own, other, q, k, v, o):
            me = s_ref[0]
            mine = pl.ds(pl.multiple_of(me * unit, unit), unit)
            here, there = me * n_attn, (1 - me) * n_attn
            for start, load in (
                (here, lambda c: own[mine, c]),
                (there, lambda c: other[:, c].astype(f32)),
            ):
                start = pl.multiple_of(start, n_attn)
                for h in range(heads):
                    for i, ref in enumerate((q, k, v)):
                        ref[:, pl.ds(start + h * HD, HD)] = load(slice((3 * h + i) * HD, (3 * h + i + 1) * HD))
                o[:, pl.ds(start, n_attn)] = load(slice(3 * n_attn, 4 * n_attn))

        grad_w_query, grad_w_key, grad_w_value, grad_w_out = small_call(
            join_attn, [core], [own_a, other_a], [array_of(unit, 2 * n_attn, f32)] * 4
        )

        normed_part = rows_of(normed_all, core * rows + half * part, part)
        inverse_part = rows_of(inverse_all, core * rows + half * part, part)
        grad_gain_a = jnp.sum(grad_h_one * normed_part, axis=0, keepdims=True)
        grad_x = (grad_after + norm_back(grad_h_one * gain_a, normed_part, inverse_part)).astype(bf16)
        grad_tokens = join_tokens(grad_x, swap_tp(grad_x), half, nat, block)

        grad_gains = cat([grad_gain_a, grad_gain_m])
        grad_gains = grad_gains + swap_tp(grad_gains)
        for mask in [1] + [1 << bit for bit in range(shards.bit_length() - 2, 1, -1)]:
            mid = grad_gains.shape[1] // 2
            grad_gains = grad_gains[:, :mid] + across(grad_gains[:, mid:], mask)
        first, second = grad_gains[:, :block], grad_gains[:, block:]
        grad_gains = jnp.where(zl == 0, first, second) + across(jnp.where(zl == 0, second, first), 2)
        first, second = grad_gains[:, :unit], grad_gains[:, unit:]
        grad_gains = jnp.where(core == 0, first, second) + swap_core(jnp.where(core == 0, second, first))

        return (
            output,
            grad_tokens,
            grad_gains[0],
            grad_w_query,
            grad_w_key,
            grad_w_value,
            grad_w_out,
            grad_gains[1],
            grad_w_gate,
            grad_w_up,
            grad_w_down,
        )

    return per_device


def solution(mesh):
    wide = P(("shard", "ctx"), None)
    flat = P(("shard", "ctx"))
    both = P(("shard", "ctx"), "tp")
    placed = (wide, P("shard", None), flat, both, both, both, both, flat, both, both, both, wide)
    return jax.shard_map(
        build(mesh.shape["shard"]),
        mesh=mesh,
        in_specs=placed,
        out_specs=(wide, wide, flat, both, both, both, both, flat, both, both, both),
        check_vma=False,
    )
```

```python
import math

import jax
import jax.numpy as jnp
from jax import lax
from jax.experimental import pallas as pl
from jax.experimental.pallas import tpu as pltpu
from jax.sharding import PartitionSpec as P

HD = 128
LENGTH = 1024


norm_eps = 1e-05
rope_base = 10000.0

bf16 = jnp.bfloat16
f32 = jnp.float32


def matmul(left, right):
    return jnp.dot(left, right, preferred_element_type=jnp.float32)


def contract_rows(left, right):
    return lax.dot_general(
        left, right, (((0,), (0,)), ((), ())), preferred_element_type=jnp.float32
    )


def contract_cols(left, right):
    return lax.dot_general(
        left, right, (((1,), (1,)), ((), ())), preferred_element_type=jnp.float32
    )


def norm_parts(values):
    inverse = lax.rsqrt(jnp.mean(values * values, axis=-1, keepdims=True) + norm_eps)
    return (values * inverse, inverse)


def norm_back(grad_scaled, normed, inverse):
    return inverse * (grad_scaled - normed * jnp.mean(grad_scaled * normed, axis=-1, keepdims=True))


def doc_positions(seg_row):
    places = jnp.arange(seg_row.shape[0], dtype=jnp.int32)
    starts_here = jnp.concatenate([jnp.ones((1,), dtype=jnp.bool_), seg_row[1:] != seg_row[:-1]])
    starts = lax.cummax(jnp.where(starts_here, places, jnp.zeros_like(places)), axis=0)
    return places - starts


def rope_tables(positions):
    half_dim = HD // 2
    freqs = rope_base ** (-(jnp.arange(half_dim, dtype=jnp.float32) * (2.0 / HD)))
    angles = positions.astype(jnp.float32)[:, None] * freqs[None, :]
    cosine, sine = jnp.cos(angles), jnp.sin(angles)
    return cat([cosine, cosine], 1), cat([-sine, sine], 1)


def cat(parts, axis=0):
    return jnp.concatenate(parts, axis=axis)


def rows_of(values, start, size):
    return lax.dynamic_slice_in_dim(values, start, size, 0)


def ordered(index, own, other, axis=0):
    return jnp.where(index == 0, cat([own, other], axis), cat([other, own], axis))


def after(values, *events):
    return lax.optimization_barrier((values, events))[0]


def small_call(body, scalars, arrays, outs):
    scalars = jnp.stack([jnp.asarray(v, jnp.int32) for v in scalars])
    return pl.pallas_call(
        body,
        grid_spec=pltpu.PrefetchScalarGridSpec(
            num_scalar_prefetch=1,
            grid=(1,),
            in_specs=[pl.BlockSpec(a.shape, lambda i, s: (0, 0)) for a in arrays],
            out_specs=[pl.BlockSpec(o.shape, lambda i, s: (0, 0)) for o in outs],
        ),
        out_shape=outs,
    )(scalars, *arrays)


def array_of(rows, cols, dtype=bf16):
    return jax.ShapeDtypeStruct((rows, cols), dtype)


def permute_cols(values, index, block):
    rows, width = values.shape
    step = min(rows, 128)
    count = width // block
    if block % 128:
        return cat([lax.dynamic_slice_in_dim(values, index[j] * block, block, 1) for j in range(count)], 1)

    def body(index_ref, in_ref, out_ref):
        for j in range(count):
            start = pl.multiple_of(index_ref[j] * block, block)
            out_ref[:, j * block : (j + 1) * block] = in_ref[:, pl.ds(start, block)]

    spec = pl.BlockSpec((step, width), lambda i, s: (i, 0))
    return pl.pallas_call(
        body,
        grid_spec=pltpu.PrefetchScalarGridSpec(
            num_scalar_prefetch=1, grid=(rows // step,), in_specs=[spec], out_specs=spec
        ),
        out_shape=jax.ShapeDtypeStruct(values.shape, values.dtype),
    )(index, values)


def join_tokens(own, other, half, index, block):
    rows, width = own.shape
    count = width // block
    if block % 128:
        return permute_cols(ordered(half, own, other), index, block)

    def body(index_ref, own_ref, other_ref, out_ref):
        here = pl.program_id(0) == index_ref[count]

        def move(ref):
            for j in range(count):
                start = pl.multiple_of(index_ref[j] * block, block)
                out_ref[:, j * block : (j + 1) * block] = ref[:, pl.ds(start, block)]

        pl.when(here)(lambda: move(own_ref))
        pl.when(jnp.logical_not(here))(lambda: move(other_ref))

    whole = pl.BlockSpec((rows, width), lambda i, s: (0, 0))
    return pl.pallas_call(
        body,
        grid_spec=pltpu.PrefetchScalarGridSpec(
            num_scalar_prefetch=1,
            grid=(2,),
            in_specs=[whole, whole],
            out_specs=pl.BlockSpec((rows, width), lambda i, s: (i, 0)),
        ),
        out_shape=jax.ShapeDtypeStruct((2 * rows, width), own.dtype),
    )(cat([index, half[None]]), own, other)


def score_parts(query, keys, rows_seg, cols_seg, diagonal):
    scores = contract_cols(query, keys) * (1.0 / math.sqrt(HD)) - math.log(LENGTH)
    allowed = rows_seg == cols_seg
    if diagonal:
        size = query.shape[0]
        places = lax.broadcasted_iota(jnp.int32, (size, size), 0)
        allowed = allowed & (places >= lax.broadcasted_iota(jnp.int32, (size, size), 1))
    return jax.nn.sigmoid(scores), allowed


def swap_halves(values):
    return pltpu.roll(values, HD // 2, 1)


def attend_forward(qkv, seg_row, cosine, sine, tile=256):
    length = seg_row.shape[0]
    heads = qkv.shape[1] // (3 * HD)
    tiles = length // tile

    def body(seg_ref, qkv_ref, cos_ref, sin_ref, seg_col, seg_line, out_ref, kept_ref, acc):
        cos_t, sin_t = cos_ref[...], sin_ref[...]
        for part in (0, 1):
            where = slice(part * HD, (part + 1) * HD)
            value = qkv_ref[:, where]
            kept_ref[:, where] = (value * cos_t + swap_halves(value) * sin_t).astype(bf16)
        kept_ref[:, 2 * HD :] = qkv_ref[:, 2 * HD :].astype(bf16)
        for i in range(tiles):
            rows = slice(i * tile, (i + 1) * tile)

            def step(j, diagonal, rows=rows):
                cols = slice(j * tile, (j + 1) * tile)
                sig, allowed = score_parts(
                    kept_ref[rows, :HD], kept_ref[cols, HD : 2 * HD],
                    seg_col[rows, :], seg_line[:, cols], diagonal,
                )
                weights = jnp.where(allowed, sig, 0.0).astype(bf16)
                return matmul(weights, kept_ref[cols, 2 * HD :])

            acc[...] = step(i, True)
            for j in range(i):

                @pl.when(seg_ref[(j + 1) * tile - 1] == seg_ref[i * tile])
                def _(j=j):
                    acc[...] += step(j, False)

            out_ref[rows, :] = acc[...].astype(bf16)

    full = pl.BlockSpec((length, HD), lambda h, s: (0, 0))
    return pl.pallas_call(
        body,
        grid_spec=pltpu.PrefetchScalarGridSpec(
            num_scalar_prefetch=1,
            grid=(heads,),
            in_specs=[
                pl.BlockSpec((length, 3 * HD), lambda h, s: (0, h)),
                full,
                full,
                pl.BlockSpec((length, 1), lambda h, s: (0, 0)),
                pl.BlockSpec((1, length), lambda h, s: (0, 0)),
            ],
            out_specs=[
                pl.BlockSpec((length, HD), lambda h, s: (0, h)),
                pl.BlockSpec((length, 3 * HD), lambda h, s: (0, h)),
            ],
            scratch_shapes=[pltpu.VMEM((tile, HD), f32)],
        ),
        out_shape=[array_of(length, heads * HD), array_of(length, 3 * heads * HD)],
    )(seg_row, qkv, cosine, sine, seg_row[:, None], seg_row[None, :])


def attend_backward(kept, grad_heads, seg_row, cosine, sine, first, heads, tile=256):
    length = seg_row.shape[0]
    tiles = length // tile
    scale = 1.0 / math.sqrt(HD)

    def body(seg_ref, kept_ref, do_ref, cos_ref, sin_ref, seg_col, seg_line, out_ref, dq, dk, dv):
        dk[...] = jnp.zeros_like(dk)
        dv[...] = jnp.zeros_like(dv)
        for i in range(tiles):
            rows = slice(i * tile, (i + 1) * tile)

            def step(j, diagonal, rows=rows):
                cols = slice(j * tile, (j + 1) * tile)
                query, grad = kept_ref[rows, :HD], do_ref[rows, :]
                keys = kept_ref[cols, HD : 2 * HD]
                sig, allowed = score_parts(query, keys, seg_col[rows, :], seg_line[:, cols], diagonal)
                weights = jnp.where(allowed, sig, 0.0).astype(bf16)
                dv[cols, :] += contract_rows(weights, grad)
                grad_probs = contract_cols(grad, kept_ref[cols, 2 * HD :])
                grad_scores = jnp.where(allowed, grad_probs * sig * (1.0 - sig), 0.0).astype(bf16)
                dk[cols, :] += contract_rows(grad_scores, query)
                return matmul(grad_scores, keys)

            dq[rows, :] = step(i, True)
            for j in range(i):

                @pl.when(seg_ref[(j + 1) * tile - 1] == seg_ref[i * tile])
                def _(j=j, rows=rows):
                    dq[rows, :] += step(j, False)

        cos_t, sin_t = cos_ref[...], sin_ref[...]
        for part, ref in ((0, dq), (1, dk)):
            grad = ref[...] * scale
            out_ref[:, part * HD : (part + 1) * HD] = (grad * cos_t - swap_halves(grad) * sin_t).astype(bf16)
        out_ref[:, 2 * HD :] = dv[...].astype(bf16)

    full = pl.BlockSpec((length, HD), lambda h, s: (0, 0))
    return pl.pallas_call(
        body,
        grid_spec=pltpu.PrefetchScalarGridSpec(
            num_scalar_prefetch=1,
            grid=(heads,),
            in_specs=[
                pl.BlockSpec((length, 3 * HD), lambda h, s: (0, first + h)),
                pl.BlockSpec((length, HD), lambda h, s: (0, first + h)),
                full,
                full,
                pl.BlockSpec((length, 1), lambda h, s: (0, 0)),
                pl.BlockSpec((1, length), lambda h, s: (0, 0)),
            ],
            out_specs=pl.BlockSpec((length, 3 * HD), lambda h, s: (0, h)),
            scratch_shapes=[pltpu.VMEM((length, HD), f32)] * 3,
        ),
        out_shape=array_of(length, 3 * heads * HD),
    )(seg_row, kept, grad_heads, cosine, sine, seg_row[:, None], seg_row[None, :])


def build(shards):
    line = [k << 1 for k in range(1, shards // 2)]

    groups = [[i for i in range(shards) if (i >> 1) & 1 == bit] for bit in (0, 1)]
    every = [[(i & ~3) | ((i & 1) << 1) | ((i >> 1) & 1) for i in range(shards)]]

    def across(values, mask):
        return lax.ppermute(values, "shard", [(i, i ^ mask) for i in range(shards)])

    def swap_core(values):
        return lax.ppermute(values, "ctx", [(0, 1), (1, 0)])

    def swap_tp(values):
        return lax.ppermute(values, "tp", [(0, 1), (1, 0)])

    def per_device(
        tokens,
        segments,
        gain_attn,
        w_query,
        w_key,
        w_value,
        w_out,
        gain_mlp,
        w_gate,
        w_up,
        w_down,
        cotangent,
    ):
        shard = lax.axis_index("shard").astype(jnp.int32)
        core = lax.axis_index("ctx").astype(jnp.int32)
        half = lax.axis_index("tp").astype(jnp.int32)
        y, zl = shard & 1, (shard >> 1) & 1
        rows, width = tokens.shape
        part = rows // 2
        block = width // shards
        unit = block // 2
        n_attn = w_query.shape[1] // 2
        n_ff = w_gate.shape[1] // 4
        heads = n_attn // HD
        half_s = shards // 2
        pad = 16

        def place_of(number):
            return (number & ~3) | ((number & 1) << 1) | ((number >> 1) & 1)

        rel = place_of(jnp.arange(shards, dtype=jnp.int32))
        nat = rel

        attn_w = [w_query, w_key, w_value, w_out]
        ff_w = [w_gate, w_up, w_down]

        def send_attn(s_ref, q, k, v, o, out):
            start = pl.multiple_of((1 - s_ref[0]) * n_attn, n_attn)
            for h in range(heads):
                for i, ref in enumerate((q, k, v)):
                    out[:, (3 * h + i) * HD : (3 * h + i + 1) * HD] = ref[:, pl.ds(start + h * HD, HD)]
            out[:, 3 * n_attn :] = o[:, pl.ds(start, n_attn)]

        (sent_a,) = small_call(send_attn, [core], attn_w, [array_of(unit, 4 * n_attn)])
        other_a = swap_core(sent_a)
        gains = jnp.stack([gain_attn, gain_mlp])
        other_gains = swap_core(gains)

        def keep_attn(s_ref, q, k, v, o, other, own_g, other_g, out_qkv, out_o):
            me = s_ref[0]
            start = pl.multiple_of(me * n_attn, n_attn)
            mine, theirs = pl.ds(me * unit, unit), pl.ds((1 - me) * unit, unit)
            for h in range(heads):
                for i, ref in enumerate((q, k, v)):
                    where = slice((3 * h + i) * HD, (3 * h + i + 1) * HD)
                    out_qkv[mine, where] = ref[:, pl.ds(start + h * HD, HD)]
            out_o[mine, :] = o[:, pl.ds(start, n_attn)]
            out_qkv[theirs, :] = other[:, : 3 * n_attn]
            out_o[theirs, :] = other[:, 3 * n_attn :]
            first, second = own_g[...], other_g[...]
            low = jnp.where(me == 0, first, second)
            high = jnp.where(me == 0, second, first)
            line_g = cat([low, high, jnp.zeros((2, 3 * n_attn - block), bf16)], 1)
            out_qkv[block:, :] = cat([line_g, jnp.zeros((pad - 2, 3 * n_attn), bf16)])

        block_qkv, block_o = small_call(
            keep_attn, [core], attn_w + [other_a, gains, other_gains],
            [array_of(block + pad, 3 * n_attn), array_of(block, n_attn)],
        )

        def shard_at(i):
            return shard ^ (((i % half_s) << 1) | (i // half_s))

        def place_line(parts, take):
            full = jnp.zeros((width, parts[0].shape[1]), bf16)
            for i, v in enumerate(parts):
                full = lax.dynamic_update_slice_in_dim(full, take(v), place_of(shard_at(i)) * block, 0)
            return full

        near_qkv = [block_qkv] + [across(block_qkv, mask) for mask in line]
        parts_qkv = near_qkv + [across(v, 1) for v in near_qkv]
        weight_qkv = place_line(parts_qkv, lambda v: v[:block])
        gain_rows = jnp.stack([v[block : block + 2, :block] for v in parts_qkv])
        away_bits = place_of(jnp.arange(shards, dtype=jnp.int32)) ^ shard
        gain_rows = gain_rows[(away_bits >> 1) + half_s * (away_bits & 1)]
        gains_rel = jnp.transpose(gain_rows, (1, 0, 2)).reshape(2, width).astype(f32)
        gain_a, gain_m = gains_rel[0:1], gains_rel[1:2]

        block_o = after(block_o, *near_qkv[1:])
        near_o = cat([block_o] + [across(block_o, mask) for mask in line])
        parts_o = cat([near_o, across(after(near_o, *parts_qkv[half_s:]), 1)])
        weight_o = place_line([parts_o[i * block : (i + 1) * block] for i in range(shards)], lambda v: v)

        def send_ff(s_ref, g, u, d, out):
            start = pl.multiple_of((1 - s_ref[0]) * 2 * n_ff, n_ff)
            for i, ref in enumerate((g, u, d)):
                out[:, i * 2 * n_ff : (i + 1) * 2 * n_ff] = ref[:, pl.ds(start, 2 * n_ff)]

        (sent_f,) = small_call(send_ff, [core], ff_w, [array_of(unit, 6 * n_ff)])
        other_f = swap_core(sent_f)

        def keep_ff(s_ref, g, u, d, other, keep, send):
            me, low = s_ref[0], s_ref[1]
            mine, theirs = pl.ds(pl.multiple_of(me * unit, unit), unit), pl.ds(pl.multiple_of((1 - me) * unit, unit), unit)
            for out, which in ((keep, low), (send, 1 - low)):
                start = pl.multiple_of(which * n_ff, n_ff)
                for i, ref in enumerate((g, u, d)):
                    cols = slice(i * n_ff, (i + 1) * n_ff)
                    out[mine, cols] = ref[:, pl.ds(pl.multiple_of(me * 2 * n_ff, n_ff) + start, n_ff)]
                    out[theirs, cols] = other[:, pl.ds(i * 2 * n_ff + start, n_ff)]

        keep_f, send_f = small_call(keep_ff, [core, zl], ff_w + [other_f], [array_of(block, 3 * n_ff)] * 2)
        recv_f = across(send_f, 2)

        def pair_rows(s_ref, own, other, out):
            low = s_ref[0]
            out[pl.ds(pl.multiple_of(low * block, block), block), :] = own[...]
            out[pl.ds(pl.multiple_of((1 - low) * block, block), block), :] = other[...]

        (pair_f,) = small_call(pair_rows, [zl], [keep_f, recv_f], [array_of(2 * block, 3 * n_ff)])
        weight_f = lax.all_gather(pair_f, "shard", axis=0, tiled=True, axis_index_groups=groups)
        weight_g, weight_u, weight_d = [weight_f[:, i * n_ff : (i + 1) * n_ff] for i in range(3)]

        seg_row = segments[0]
        cosine, sine = rope_tables(doc_positions(seg_row))
        x_own = permute_cols(tokens, rel, block)
        x_both = ordered(core, x_own, swap_core(x_own))
        normed_all, inverse_all = norm_parts(x_both.astype(f32))
        h_one = (normed_all * gain_a).astype(bf16)
        qkv = matmul(h_one, weight_qkv)
        mixed, kept = attend_forward(qkv, seg_row, cosine, sine)

        def to_slice(operand, project):
            away = project(rows_of(operand, (1 - core) * rows, rows)).astype(bf16)
            here = rows_of(operand, core * rows, rows)
            away = swap_core(away)
            other = project(rows_of(here, (1 - half) * part, part)) + rows_of(
                away, (1 - half) * part, part
            ).astype(f32)
            other = swap_tp(other.astype(bf16))
            own = project(rows_of(here, half * part, part)) + rows_of(
                away, half * part, part
            ).astype(f32)
            return own + other.astype(f32)

        x_part = rows_of(x_own, half * part, part).astype(f32)
        after_attn = x_part + to_slice(mixed, lambda v: contract_cols(v, weight_o))
        normed_two, inverse_two = norm_parts(after_attn)
        h_part = (normed_two * gain_m).astype(bf16)

        by_tp, by_zl = swap_tp(h_part), across(h_part, 2)
        mid = part // 2
        near = cat([h_part, by_tp, by_zl])
        far_near = swap_core(near)
        both = cat([across(by_tp[:mid], 2), swap_tp(by_zl[mid:])])
        h_two = cat([near, both, far_near, swap_core(both)])

        dy_rel = permute_cols(after(cotangent, *parts_qkv[half_s:]), rel, block)
        dy_ff = cat([rows_of(dy_rel, half * part, part), rows_of(dy_rel, (1 - half) * part, part)])
        dy_zl = across(dy_ff[:part], 2)
        near = cat([dy_ff, dy_zl, swap_tp(dy_zl)])
        grad_out = cat([near, swap_core(near)])

        gate_pre = matmul(h_two, weight_g)
        up_pre = matmul(h_two, weight_u)
        gate_sig = jax.nn.sigmoid(gate_pre)
        gate_act = gate_pre * gate_sig
        hidden = (gate_act * up_pre).astype(bf16)

        def from_tokens(project):
            count = 4 * part
            away = swap_core(project(slice(count, 2 * count)).astype(bf16))
            total = project(slice(0, count)) + away.astype(f32)
            mid = width // 2
            low, high = total[:, :mid], total[:, mid:]

            def pick(values, i):
                return values[i * part : (i + 1) * part]

            low_tp = swap_tp(cat([pick(low, 1), pick(low, 3)]).astype(bf16)).astype(f32)
            high_zl = across(cat([pick(high, 2), pick(high, 3)]).astype(bf16), 2).astype(f32)
            low_zl = across((pick(low, 2) + pick(low_tp, 1)).astype(bf16), 2).astype(f32)
            high_tp = swap_tp((pick(high, 1) + pick(high_zl, 1)).astype(bf16)).astype(f32)
            low_sum = pick(low, 0) + pick(low_tp, 0) + low_zl
            high_sum = pick(high, 0) + pick(high_zl, 0) + high_tp
            return away, cat([low_sum, high_sum], 1)

        grad_hidden = matmul(grad_out, weight_d)
        grad_gate = (grad_hidden * up_pre * gate_sig * (1.0 + gate_pre * (1.0 - gate_sig))).astype(bf16)
        grad_up = (grad_hidden * gate_act).astype(bf16)
        event_h, grad_h_two = from_tokens(
            lambda where: contract_cols(grad_gate[where], weight_g)
            + contract_cols(grad_up[where], weight_u)
        )
        late_hidden = after(hidden, grad_h_two)
        event_m, mlp = from_tokens(lambda where: contract_cols(late_hidden[where], weight_d))
        out_part = (after_attn + mlp).astype(bf16)
        output = join_tokens(out_part, swap_tp(out_part), half, nat, block)

        grad_gain_m = jnp.sum(grad_h_two * normed_two, axis=0, keepdims=True)
        dy_part = rows_of(dy_rel, half * part, part).astype(f32)
        grad_after = dy_part + norm_back(grad_h_two * gain_m, normed_two, inverse_two)

        grad_part = grad_after.astype(bf16)
        grad_half = ordered(half, grad_part, swap_tp(grad_part))
        grad_attn = ordered(core, grad_half, swap_core(grad_half))
        grad_mixed = matmul(grad_attn, weight_o).astype(bf16)

        def scatter(values, members):
            return lax.psum_scatter(
                values.astype(bf16), "shard", scatter_dimension=0, tiled=True, axis_index_groups=members
            )

        def rows_pair(own, count):
            other = across(rows_of(own, (1 - zl) * block, block), 2)

            def send_rows(s_ref, mine, theirs, out):
                low, away_rows = s_ref[1], pl.multiple_of((1 - s_ref[0]) * unit, unit)
                rows_m = pl.ds(pl.multiple_of(low * block, block) + away_rows, unit)
                for i in range(count):
                    cols = slice(i * n_ff, (i + 1) * n_ff)
                    out[:, pl.ds(i * 2 * n_ff + pl.multiple_of(low * n_ff, n_ff), n_ff)] = mine[rows_m, cols]
                    out[:, pl.ds(i * 2 * n_ff + pl.multiple_of((1 - low) * n_ff, n_ff), n_ff)] = theirs[
                        pl.ds(away_rows, unit), cols
                    ]

            (sent,) = small_call(send_rows, [core, zl], [own, other], [array_of(unit, 2 * count * n_ff)])
            third = swap_core(sent)

            def join_rows(s_ref, mine, theirs, third_ref, *outs):
                me, low = s_ref[0], s_ref[1]
                start = pl.multiple_of(me * 2 * n_ff, n_ff)
                away = pl.multiple_of((1 - me) * 2 * n_ff, n_ff)
                here = pl.multiple_of(me * unit, unit)
                for i, out in enumerate(outs):
                    cols = slice(i * n_ff, (i + 1) * n_ff)
                    out[:, pl.ds(start + pl.multiple_of(low * n_ff, n_ff), n_ff)] = mine[
                        pl.ds(pl.multiple_of(low * block, block) + here, unit), cols
                    ].astype(f32)
                    out[:, pl.ds(start + pl.multiple_of((1 - low) * n_ff, n_ff), n_ff)] = theirs[
                        pl.ds(here, unit), cols
                    ].astype(f32)
                    out[:, pl.ds(away, 2 * n_ff)] = third_ref[:, i * 2 * n_ff : (i + 1) * 2 * n_ff].astype(f32)

            return small_call(join_rows, [core, zl], [own, other, third], [array_of(unit, 4 * n_ff, f32)] * count)

        def send_unit(s_ref, own, out):
            out[...] = own[pl.ds((1 - s_ref[0]) * unit, unit), :].astype(bf16)

        own_d = scatter(contract_rows(grad_out, hidden), groups)
        own_gu = scatter(
            cat([contract_rows(h_two, grad_gate).astype(bf16), contract_rows(h_two, grad_up).astype(bf16)], 1), groups
        )
        own_o = scatter(contract_rows(grad_attn, mixed), every)
        grad_qkv = attend_backward(kept, grad_mixed, seg_row, cosine, sine, 0, heads)
        own_qkv = scatter(contract_rows(h_one, grad_qkv), every)

        (grad_w_down,) = rows_pair(own_d, 1)
        grad_w_gate, grad_w_up = rows_pair(own_gu, 2)

        grad_h_one = to_slice(grad_qkv, lambda v: contract_cols(v, weight_qkv))

        own_a = cat([own_qkv, own_o], 1)
        (sent_g,) = small_call(send_unit, [core], [own_a], [array_of(unit, 4 * n_attn)])
        other_a = swap_core(sent_g)

        def join_attn(s_ref, own, other, q, k, v, o):
            me = s_ref[0]
            mine = pl.ds(pl.multiple_of(me * unit, unit), unit)
            here, there = me * n_attn, (1 - me) * n_attn
            for start, load in (
                (here, lambda c: own[mine, c].astype(f32)),
                (there, lambda c: other[:, c].astype(f32)),
            ):
                start = pl.multiple_of(start, n_attn)
                for h in range(heads):
                    for i, ref in enumerate((q, k, v)):
                        ref[:, pl.ds(start + h * HD, HD)] = load(slice((3 * h + i) * HD, (3 * h + i + 1) * HD))
                o[:, pl.ds(start, n_attn)] = load(slice(3 * n_attn, 4 * n_attn))

        grad_w_query, grad_w_key, grad_w_value, grad_w_out = small_call(
            join_attn, [core], [own_a, other_a], [array_of(unit, 2 * n_attn, f32)] * 4
        )

        normed_part = rows_of(normed_all, core * rows + half * part, part)
        inverse_part = rows_of(inverse_all, core * rows + half * part, part)
        grad_gain_a = jnp.sum(grad_h_one * normed_part, axis=0, keepdims=True)
        grad_x = (grad_after + norm_back(grad_h_one * gain_a, normed_part, inverse_part)).astype(bf16)
        grad_tokens = join_tokens(grad_x, swap_tp(grad_x), half, nat, block)

        grad_gains = cat([grad_gain_a, grad_gain_m])
        grad_gains = grad_gains + swap_tp(grad_gains)
        for mask in [1 << bit for bit in range(shards.bit_length() - 2, 1, -1)] + [1, 2]:
            mid = grad_gains.shape[1] // 2
            first, second = grad_gains[:, :mid], grad_gains[:, mid:]
            low = (shard & mask) == 0
            grad_gains = jnp.where(low, first, second) + across(jnp.where(low, second, first), mask)
        first, second = grad_gains[:, :unit], grad_gains[:, unit:]
        grad_gains = jnp.where(core == 0, first, second) + swap_core(jnp.where(core == 0, second, first))

        return (
            output,
            grad_tokens,
            grad_gains[0],
            grad_w_query,
            grad_w_key,
            grad_w_value,
            grad_w_out,
            grad_gains[1],
            grad_w_gate,
            grad_w_up,
            grad_w_down,
        )

    return per_device


def solution(mesh):
    wide = P(("shard", "ctx"), None)
    flat = P(("shard", "ctx"))
    both = P(("shard", "ctx"), "tp")
    placed = (wide, P("shard", None), flat, both, both, both, both, flat, both, both, both, wide)
    return jax.shard_map(
        build(mesh.shape["shard"]),
        mesh=mesh,
        in_specs=placed,
        out_specs=(wide, wide, flat, both, both, both, both, flat, both, both, both),
        check_vma=False,
    )
```

```python
import math

import jax
import jax.numpy as jnp
from jax import lax
from jax.experimental import pallas as pl
from jax.experimental.pallas import tpu as pltpu
from jax.sharding import PartitionSpec as P

HD = 128
LENGTH = 1024


norm_eps = 1e-05
rope_base = 10000.0

bf16 = jnp.bfloat16
f32 = jnp.float32


def matmul(left, right):
    return jnp.dot(left, right, preferred_element_type=jnp.float32)


def contract_rows(left, right):
    return lax.dot_general(
        left, right, (((0,), (0,)), ((), ())), preferred_element_type=jnp.float32
    )


def contract_cols(left, right):
    return lax.dot_general(
        left, right, (((1,), (1,)), ((), ())), preferred_element_type=jnp.float32
    )


def norm_parts(values):
    inverse = lax.rsqrt(jnp.mean(values * values, axis=-1, keepdims=True) + norm_eps)
    return (values * inverse, inverse)


def norm_back(grad_scaled, normed, inverse):
    return inverse * (grad_scaled - normed * jnp.mean(grad_scaled * normed, axis=-1, keepdims=True))


def doc_positions(seg_row):
    places = jnp.arange(seg_row.shape[0], dtype=jnp.int32)
    starts_here = jnp.concatenate([jnp.ones((1,), dtype=jnp.bool_), seg_row[1:] != seg_row[:-1]])
    starts = lax.cummax(jnp.where(starts_here, places, jnp.zeros_like(places)), axis=0)
    return places - starts


def rope_tables(positions):
    half_dim = HD // 2
    freqs = rope_base ** (-(jnp.arange(half_dim, dtype=jnp.float32) * (2.0 / HD)))
    angles = positions.astype(jnp.float32)[:, None] * freqs[None, :]
    cosine, sine = jnp.cos(angles), jnp.sin(angles)
    return cat([cosine, cosine], 1), cat([-sine, sine], 1)


def cat(parts, axis=0):
    return jnp.concatenate(parts, axis=axis)


def rows_of(values, start, size):
    return lax.dynamic_slice_in_dim(values, start, size, 0)


def ordered(index, own, other, axis=0):
    return jnp.where(index == 0, cat([own, other], axis), cat([other, own], axis))


def after(values, *events):
    return lax.optimization_barrier((values, events))[0]


def small_call(body, scalars, arrays, outs):
    scalars = jnp.stack([jnp.asarray(v, jnp.int32) for v in scalars])
    return pl.pallas_call(
        body,
        grid_spec=pltpu.PrefetchScalarGridSpec(
            num_scalar_prefetch=1,
            grid=(1,),
            in_specs=[pl.BlockSpec(a.shape, lambda i, s: (0, 0)) for a in arrays],
            out_specs=[pl.BlockSpec(o.shape, lambda i, s: (0, 0)) for o in outs],
        ),
        out_shape=outs,
    )(scalars, *arrays)


def array_of(rows, cols, dtype=bf16):
    return jax.ShapeDtypeStruct((rows, cols), dtype)


def permute_cols(values, index, block):
    rows, width = values.shape
    step = min(rows, 128)
    count = width // block
    if block % 128:
        return cat([lax.dynamic_slice_in_dim(values, index[j] * block, block, 1) for j in range(count)], 1)

    def body(index_ref, in_ref, out_ref):
        for j in range(count):
            start = pl.multiple_of(index_ref[j] * block, block)
            out_ref[:, j * block : (j + 1) * block] = in_ref[:, pl.ds(start, block)]

    spec = pl.BlockSpec((step, width), lambda i, s: (i, 0))
    return pl.pallas_call(
        body,
        grid_spec=pltpu.PrefetchScalarGridSpec(
            num_scalar_prefetch=1, grid=(rows // step,), in_specs=[spec], out_specs=spec
        ),
        out_shape=jax.ShapeDtypeStruct(values.shape, values.dtype),
    )(index, values)


def join_tokens(own, other, half, index, block):
    rows, width = own.shape
    count = width // block
    if block % 128:
        return permute_cols(ordered(half, own, other), index, block)

    def body(index_ref, own_ref, other_ref, out_ref):
        here = pl.program_id(0) == index_ref[count]

        def move(ref):
            for j in range(count):
                start = pl.multiple_of(index_ref[j] * block, block)
                out_ref[:, j * block : (j + 1) * block] = ref[:, pl.ds(start, block)]

        pl.when(here)(lambda: move(own_ref))
        pl.when(jnp.logical_not(here))(lambda: move(other_ref))

    whole = pl.BlockSpec((rows, width), lambda i, s: (0, 0))
    return pl.pallas_call(
        body,
        grid_spec=pltpu.PrefetchScalarGridSpec(
            num_scalar_prefetch=1,
            grid=(2,),
            in_specs=[whole, whole],
            out_specs=pl.BlockSpec((rows, width), lambda i, s: (i, 0)),
        ),
        out_shape=jax.ShapeDtypeStruct((2 * rows, width), own.dtype),
    )(cat([index, half[None]]), own, other)


def score_parts(query, keys, rows_seg, cols_seg, diagonal):
    scores = contract_cols(query, keys) * (1.0 / math.sqrt(HD)) - math.log(LENGTH)
    allowed = rows_seg == cols_seg
    if diagonal:
        size = query.shape[0]
        places = lax.broadcasted_iota(jnp.int32, (size, size), 0)
        allowed = allowed & (places >= lax.broadcasted_iota(jnp.int32, (size, size), 1))
    return jax.nn.sigmoid(scores), allowed


def swap_halves(values):
    return pltpu.roll(values, HD // 2, 1)


def attend_forward(qkv, seg_row, cosine, sine, tile=256):
    length = seg_row.shape[0]
    heads = qkv.shape[1] // (3 * HD)
    tiles = length // tile

    def body(seg_ref, qkv_ref, cos_ref, sin_ref, seg_col, seg_line, out_ref, kept_ref, acc):
        cos_t, sin_t = cos_ref[...], sin_ref[...]
        for part in (0, 1):
            where = slice(part * HD, (part + 1) * HD)
            value = qkv_ref[:, where]
            kept_ref[:, where] = (value * cos_t + swap_halves(value) * sin_t).astype(bf16)
        kept_ref[:, 2 * HD :] = qkv_ref[:, 2 * HD :].astype(bf16)
        for i in range(tiles):
            rows = slice(i * tile, (i + 1) * tile)

            def step(j, diagonal, rows=rows):
                cols = slice(j * tile, (j + 1) * tile)
                sig, allowed = score_parts(
                    kept_ref[rows, :HD], kept_ref[cols, HD : 2 * HD],
                    seg_col[rows, :], seg_line[:, cols], diagonal,
                )
                weights = jnp.where(allowed, sig, 0.0).astype(bf16)
                return matmul(weights, kept_ref[cols, 2 * HD :])

            acc[...] = step(i, True)
            for j in range(i):

                @pl.when(seg_ref[(j + 1) * tile - 1] == seg_ref[i * tile])
                def _(j=j):
                    acc[...] += step(j, False)

            out_ref[rows, :] = acc[...].astype(bf16)

    full = pl.BlockSpec((length, HD), lambda h, s: (0, 0))
    return pl.pallas_call(
        body,
        grid_spec=pltpu.PrefetchScalarGridSpec(
            num_scalar_prefetch=1,
            grid=(heads,),
            in_specs=[
                pl.BlockSpec((length, 3 * HD), lambda h, s: (0, h)),
                full,
                full,
                pl.BlockSpec((length, 1), lambda h, s: (0, 0)),
                pl.BlockSpec((1, length), lambda h, s: (0, 0)),
            ],
            out_specs=[
                pl.BlockSpec((length, HD), lambda h, s: (0, h)),
                pl.BlockSpec((length, 3 * HD), lambda h, s: (0, h)),
            ],
            scratch_shapes=[pltpu.VMEM((tile, HD), f32)],
        ),
        out_shape=[array_of(length, heads * HD), array_of(length, 3 * heads * HD)],
    )(seg_row, qkv, cosine, sine, seg_row[:, None], seg_row[None, :])


def attend_backward(kept, grad_heads, seg_row, cosine, sine, first, heads, tile=256):
    length = seg_row.shape[0]
    tiles = length // tile
    scale = 1.0 / math.sqrt(HD)

    def body(seg_ref, kept_ref, do_ref, cos_ref, sin_ref, seg_col, seg_line, out_ref, dq, dk, dv):
        dk[...] = jnp.zeros_like(dk)
        dv[...] = jnp.zeros_like(dv)
        for i in range(tiles):
            rows = slice(i * tile, (i + 1) * tile)

            def step(j, diagonal, rows=rows):
                cols = slice(j * tile, (j + 1) * tile)
                query, grad = kept_ref[rows, :HD], do_ref[rows, :]
                keys = kept_ref[cols, HD : 2 * HD]
                sig, allowed = score_parts(query, keys, seg_col[rows, :], seg_line[:, cols], diagonal)
                weights = jnp.where(allowed, sig, 0.0).astype(bf16)
                dv[cols, :] += contract_rows(weights, grad)
                grad_probs = contract_cols(grad, kept_ref[cols, 2 * HD :])
                grad_scores = jnp.where(allowed, grad_probs * sig * (1.0 - sig), 0.0).astype(bf16)
                dk[cols, :] += contract_rows(grad_scores, query)
                return matmul(grad_scores, keys)

            dq[rows, :] = step(i, True)
            for j in range(i):

                @pl.when(seg_ref[(j + 1) * tile - 1] == seg_ref[i * tile])
                def _(j=j, rows=rows):
                    dq[rows, :] += step(j, False)

        cos_t, sin_t = cos_ref[...], sin_ref[...]
        for part, ref in ((0, dq), (1, dk)):
            grad = ref[...] * scale
            out_ref[:, part * HD : (part + 1) * HD] = (grad * cos_t - swap_halves(grad) * sin_t).astype(bf16)
        out_ref[:, 2 * HD :] = dv[...].astype(bf16)

    full = pl.BlockSpec((length, HD), lambda h, s: (0, 0))
    return pl.pallas_call(
        body,
        grid_spec=pltpu.PrefetchScalarGridSpec(
            num_scalar_prefetch=1,
            grid=(heads,),
            in_specs=[
                pl.BlockSpec((length, 3 * HD), lambda h, s: (0, first + h)),
                pl.BlockSpec((length, HD), lambda h, s: (0, first + h)),
                full,
                full,
                pl.BlockSpec((length, 1), lambda h, s: (0, 0)),
                pl.BlockSpec((1, length), lambda h, s: (0, 0)),
            ],
            out_specs=pl.BlockSpec((length, 3 * HD), lambda h, s: (0, h)),
            scratch_shapes=[pltpu.VMEM((length, HD), f32)] * 3,
        ),
        out_shape=array_of(length, 3 * heads * HD),
    )(seg_row, kept, grad_heads, cosine, sine, seg_row[:, None], seg_row[None, :])


def build(shards):
    line = [k << 1 for k in range(1, shards // 2)]

    groups = [[i for i in range(shards) if (i >> 1) & 1 == bit] for bit in (0, 1)]
    every = [[(i & ~3) | ((i & 1) << 1) | ((i >> 1) & 1) for i in range(shards)]]

    def across(values, mask):
        return lax.ppermute(values, "shard", [(i, i ^ mask) for i in range(shards)])

    def swap_core(values):
        return lax.ppermute(values, "ctx", [(0, 1), (1, 0)])

    def swap_tp(values):
        return lax.ppermute(values, "tp", [(0, 1), (1, 0)])

    def per_device(
        tokens,
        segments,
        gain_attn,
        w_query,
        w_key,
        w_value,
        w_out,
        gain_mlp,
        w_gate,
        w_up,
        w_down,
        cotangent,
    ):
        shard = lax.axis_index("shard").astype(jnp.int32)
        core = lax.axis_index("ctx").astype(jnp.int32)
        half = lax.axis_index("tp").astype(jnp.int32)
        y, zl = shard & 1, (shard >> 1) & 1
        rows, width = tokens.shape
        part = rows // 2
        block = width // shards
        unit = block // 2
        n_attn = w_query.shape[1] // 2
        n_ff = w_gate.shape[1] // 4
        heads = n_attn // HD
        half_s = shards // 2
        pad = 16

        def place_of(number):
            return (number & ~3) | ((number & 1) << 1) | ((number >> 1) & 1)

        rel = place_of(jnp.arange(shards, dtype=jnp.int32))
        nat = rel

        attn_w = [w_query, w_key, w_value, w_out]
        ff_w = [w_gate, w_up, w_down]

        def send_attn(s_ref, q, k, v, o, out):
            start = pl.multiple_of((1 - s_ref[0]) * n_attn, n_attn)
            for h in range(heads):
                for i, ref in enumerate((q, k, v)):
                    out[:, (3 * h + i) * HD : (3 * h + i + 1) * HD] = ref[:, pl.ds(start + h * HD, HD)]
            out[:, 3 * n_attn :] = o[:, pl.ds(start, n_attn)]

        (sent_a,) = small_call(send_attn, [core], attn_w, [array_of(unit, 4 * n_attn)])
        other_a = swap_core(sent_a)
        gains = jnp.stack([gain_attn, gain_mlp])
        other_gains = swap_core(gains)

        def keep_attn(s_ref, q, k, v, o, other, own_g, other_g, out_qkv, out_o):
            me = s_ref[0]
            start = pl.multiple_of(me * n_attn, n_attn)
            mine, theirs = pl.ds(me * unit, unit), pl.ds((1 - me) * unit, unit)
            for h in range(heads):
                for i, ref in enumerate((q, k, v)):
                    where = slice((3 * h + i) * HD, (3 * h + i + 1) * HD)
                    out_qkv[mine, where] = ref[:, pl.ds(start + h * HD, HD)]
            out_o[mine, :] = o[:, pl.ds(start, n_attn)]
            out_qkv[theirs, :] = other[:, : 3 * n_attn]
            out_o[theirs, :] = other[:, 3 * n_attn :]
            first, second = own_g[...], other_g[...]
            low = jnp.where(me == 0, first, second)
            high = jnp.where(me == 0, second, first)
            line_g = cat([low, high, jnp.zeros((2, 3 * n_attn - block), bf16)], 1)
            out_qkv[block:, :] = cat([line_g, jnp.zeros((pad - 2, 3 * n_attn), bf16)])

        block_qkv, block_o = small_call(
            keep_attn, [core], attn_w + [other_a, gains, other_gains],
            [array_of(block + pad, 3 * n_attn), array_of(block, n_attn)],
        )

        def shard_at(i):
            return shard ^ (((i % half_s) << 1) | (i // half_s))

        def place_line(parts, take):
            full = jnp.zeros((width, parts[0].shape[1]), bf16)
            for i, v in enumerate(parts):
                full = lax.dynamic_update_slice_in_dim(full, take(v), place_of(shard_at(i)) * block, 0)
            return full

        near_qkv = [block_qkv] + [across(block_qkv, mask) for mask in line]
        parts_qkv = near_qkv + [across(v, 1) for v in near_qkv]
        weight_qkv = place_line(parts_qkv, lambda v: v[:block])
        gain_rows = jnp.stack([v[block : block + 2, :block] for v in parts_qkv])
        away_bits = place_of(jnp.arange(shards, dtype=jnp.int32)) ^ shard
        gain_rows = gain_rows[(away_bits >> 1) + half_s * (away_bits & 1)]
        gains_rel = jnp.transpose(gain_rows, (1, 0, 2)).reshape(2, width).astype(f32)
        gain_a, gain_m = gains_rel[0:1], gains_rel[1:2]

        block_o = after(block_o, *near_qkv[1:])
        near_o = cat([block_o] + [across(block_o, mask) for mask in line])
        parts_o = cat([near_o, across(after(near_o, *parts_qkv[half_s:]), 1)])
        weight_o = place_line([parts_o[i * block : (i + 1) * block] for i in range(shards)], lambda v: v)

        def send_ff(s_ref, g, u, d, out):
            start = pl.multiple_of((1 - s_ref[0]) * 2 * n_ff, n_ff)
            for i, ref in enumerate((g, u, d)):
                out[:, i * 2 * n_ff : (i + 1) * 2 * n_ff] = ref[:, pl.ds(start, 2 * n_ff)]

        (sent_f,) = small_call(send_ff, [core], ff_w, [array_of(unit, 6 * n_ff)])
        other_f = swap_core(sent_f)

        def keep_ff(s_ref, g, u, d, other, keep, send):
            me, low = s_ref[0], s_ref[1]
            mine, theirs = pl.ds(pl.multiple_of(me * unit, unit), unit), pl.ds(pl.multiple_of((1 - me) * unit, unit), unit)
            for out, which in ((keep, low), (send, 1 - low)):
                start = pl.multiple_of(which * n_ff, n_ff)
                for i, ref in enumerate((g, u, d)):
                    cols = slice(i * n_ff, (i + 1) * n_ff)
                    out[mine, cols] = ref[:, pl.ds(pl.multiple_of(me * 2 * n_ff, n_ff) + start, n_ff)]
                    out[theirs, cols] = other[:, pl.ds(i * 2 * n_ff + start, n_ff)]

        keep_f, send_f = small_call(keep_ff, [core, zl], ff_w + [other_f], [array_of(block, 3 * n_ff)] * 2)
        recv_f = across(send_f, 2)

        def pair_rows(s_ref, own, other, out):
            low = s_ref[0]
            out[pl.ds(pl.multiple_of(low * block, block), block), :] = own[...]
            out[pl.ds(pl.multiple_of((1 - low) * block, block), block), :] = other[...]

        (pair_f,) = small_call(pair_rows, [zl], [keep_f, recv_f], [array_of(2 * block, 3 * n_ff)])
        weight_f = lax.all_gather(pair_f, "shard", axis=0, tiled=True, axis_index_groups=groups)
        weight_g, weight_u, weight_d = [weight_f[:, i * n_ff : (i + 1) * n_ff] for i in range(3)]

        seg_row = segments[0]
        cosine, sine = rope_tables(doc_positions(seg_row))
        x_own = permute_cols(tokens, rel, block)
        x_both = ordered(core, x_own, swap_core(x_own))
        normed_all, inverse_all = norm_parts(x_both.astype(f32))
        h_one = (normed_all * gain_a).astype(bf16)
        qkv = matmul(h_one, weight_qkv)
        mixed, kept = attend_forward(qkv, seg_row, cosine, sine)

        def to_slice(operand, project):
            away = project(rows_of(operand, (1 - core) * rows, rows)).astype(bf16)
            here = rows_of(operand, core * rows, rows)
            away = swap_core(away)
            other = project(rows_of(here, (1 - half) * part, part)) + rows_of(
                away, (1 - half) * part, part
            ).astype(f32)
            other = swap_tp(other.astype(bf16))
            own = project(rows_of(here, half * part, part)) + rows_of(
                away, half * part, part
            ).astype(f32)
            return own + other.astype(f32)

        x_part = rows_of(x_own, half * part, part).astype(f32)
        after_attn = x_part + to_slice(mixed, lambda v: contract_cols(v, weight_o))
        normed_two, inverse_two = norm_parts(after_attn)
        h_part = (normed_two * gain_m).astype(bf16)

        by_tp, by_zl = swap_tp(h_part), across(h_part, 2)
        mid = part // 2
        near = cat([h_part, by_tp, by_zl])
        far_near = swap_core(near)
        both = cat([across(by_tp[:mid], 2), swap_tp(by_zl[mid:])])
        h_two = cat([near, both, far_near, swap_core(both)])

        dy_rel = permute_cols(cotangent, rel, block)
        dy_ff = cat([rows_of(dy_rel, half * part, part), rows_of(dy_rel, (1 - half) * part, part)])
        dy_zl = across(after(dy_ff[:part], weight_f), 2)
        near = cat([dy_ff, dy_zl, swap_tp(dy_zl)])
        grad_out = cat([near, swap_core(near)])

        gate_pre = matmul(h_two, weight_g)
        up_pre = matmul(h_two, weight_u)
        gate_sig = jax.nn.sigmoid(gate_pre)
        gate_act = gate_pre * gate_sig
        hidden = (gate_act * up_pre).astype(bf16)

        def from_tokens(project):
            count = 4 * part
            away = swap_core(project(slice(count, 2 * count)).astype(bf16))
            total = project(slice(0, count)) + away.astype(f32)
            mid = width // 2
            low, high = total[:, :mid], total[:, mid:]

            def pick(values, i):
                return values[i * part : (i + 1) * part]

            low_tp = swap_tp(cat([pick(low, 1), pick(low, 3)]).astype(bf16)).astype(f32)
            high_zl = across(cat([pick(high, 2), pick(high, 3)]).astype(bf16), 2).astype(f32)
            low_zl = across((pick(low, 2) + pick(low_tp, 1)).astype(bf16), 2).astype(f32)
            high_tp = swap_tp((pick(high, 1) + pick(high_zl, 1)).astype(bf16)).astype(f32)
            low_sum = pick(low, 0) + pick(low_tp, 0) + low_zl
            high_sum = pick(high, 0) + pick(high_zl, 0) + high_tp
            return away, cat([low_sum, high_sum], 1)

        grad_hidden = matmul(grad_out, weight_d)
        grad_gate = (grad_hidden * up_pre * gate_sig * (1.0 + gate_pre * (1.0 - gate_sig))).astype(bf16)
        grad_up = (grad_hidden * gate_act).astype(bf16)
        prod_d = contract_rows(grad_out, hidden).astype(bf16)
        prod_gu = cat(
            [contract_rows(h_two, grad_gate).astype(bf16), contract_rows(h_two, grad_up).astype(bf16)], 1
        )
        grad_gate, grad_up = after((grad_gate, grad_up), prod_d, prod_gu)
        event_h, grad_h_two = from_tokens(
            lambda where: contract_cols(grad_gate[where], weight_g)
            + contract_cols(grad_up[where], weight_u)
        )
        late_hidden = after(hidden, grad_h_two)
        event_m, mlp = from_tokens(lambda where: contract_cols(late_hidden[where], weight_d))
        out_part = (after_attn + mlp).astype(bf16)
        output = join_tokens(out_part, swap_tp(out_part), half, nat, block)

        grad_gain_m = jnp.sum(grad_h_two * normed_two, axis=0, keepdims=True)
        dy_part = rows_of(dy_rel, half * part, part).astype(f32)
        grad_after = dy_part + norm_back(grad_h_two * gain_m, normed_two, inverse_two)

        grad_part = grad_after.astype(bf16)
        grad_half = ordered(half, grad_part, swap_tp(grad_part))
        grad_attn = ordered(core, grad_half, swap_core(grad_half))
        grad_mixed = matmul(grad_attn, weight_o).astype(bf16)

        def scatter(values, members):
            return lax.psum_scatter(
                values.astype(bf16), "shard", scatter_dimension=0, tiled=True, axis_index_groups=members
            )

        def rows_pair(own, count):
            other = across(rows_of(own, (1 - zl) * block, block), 2)

            def send_rows(s_ref, mine, theirs, out):
                low, away_rows = s_ref[1], pl.multiple_of((1 - s_ref[0]) * unit, unit)
                rows_m = pl.ds(pl.multiple_of(low * block, block) + away_rows, unit)
                for i in range(count):
                    cols = slice(i * n_ff, (i + 1) * n_ff)
                    out[:, pl.ds(i * 2 * n_ff + pl.multiple_of(low * n_ff, n_ff), n_ff)] = mine[rows_m, cols]
                    out[:, pl.ds(i * 2 * n_ff + pl.multiple_of((1 - low) * n_ff, n_ff), n_ff)] = theirs[
                        pl.ds(away_rows, unit), cols
                    ]

            (sent,) = small_call(send_rows, [core, zl], [own, other], [array_of(unit, 2 * count * n_ff)])
            third = swap_core(sent)

            def join_rows(s_ref, mine, theirs, third_ref, *outs):
                me, low = s_ref[0], s_ref[1]
                start = pl.multiple_of(me * 2 * n_ff, n_ff)
                away = pl.multiple_of((1 - me) * 2 * n_ff, n_ff)
                here = pl.multiple_of(me * unit, unit)
                for i, out in enumerate(outs):
                    cols = slice(i * n_ff, (i + 1) * n_ff)
                    out[:, pl.ds(start + pl.multiple_of(low * n_ff, n_ff), n_ff)] = mine[
                        pl.ds(pl.multiple_of(low * block, block) + here, unit), cols
                    ].astype(f32)
                    out[:, pl.ds(start + pl.multiple_of((1 - low) * n_ff, n_ff), n_ff)] = theirs[
                        pl.ds(here, unit), cols
                    ].astype(f32)
                    out[:, pl.ds(away, 2 * n_ff)] = third_ref[:, i * 2 * n_ff : (i + 1) * 2 * n_ff].astype(f32)

            return small_call(join_rows, [core, zl], [own, other, third], [array_of(unit, 4 * n_ff, f32)] * count)

        def send_unit(s_ref, own, out):
            out[...] = own[pl.ds((1 - s_ref[0]) * unit, unit), :].astype(bf16)

        own_d = scatter(prod_d, groups)
        own_gu = scatter(prod_gu, groups)
        late_o = contract_rows(grad_attn, mixed).astype(bf16)
        own_o = scatter(after(late_o, own_d, own_gu), every)
        grad_mixed = after(grad_mixed, late_o)
        grad_qkv = attend_backward(kept, grad_mixed, seg_row, cosine, sine, 0, heads)
        own_qkv = scatter(after(contract_rows(h_one, grad_qkv).astype(bf16), own_o), every)

        (grad_w_down,) = rows_pair(own_d, 1)
        grad_w_gate, grad_w_up = rows_pair(own_gu, 2)

        grad_h_one = to_slice(grad_qkv, lambda v: contract_cols(v, weight_qkv))

        own_a = cat([own_qkv, own_o], 1)
        (sent_g,) = small_call(send_unit, [core], [own_a], [array_of(unit, 4 * n_attn)])
        other_a = swap_core(sent_g)

        def join_attn(s_ref, own, other, q, k, v, o):
            me = s_ref[0]
            mine = pl.ds(pl.multiple_of(me * unit, unit), unit)
            here, there = me * n_attn, (1 - me) * n_attn
            for start, load in (
                (here, lambda c: own[mine, c].astype(f32)),
                (there, lambda c: other[:, c].astype(f32)),
            ):
                start = pl.multiple_of(start, n_attn)
                for h in range(heads):
                    for i, ref in enumerate((q, k, v)):
                        ref[:, pl.ds(start + h * HD, HD)] = load(slice((3 * h + i) * HD, (3 * h + i + 1) * HD))
                o[:, pl.ds(start, n_attn)] = load(slice(3 * n_attn, 4 * n_attn))

        grad_w_query, grad_w_key, grad_w_value, grad_w_out = small_call(
            join_attn, [core], [own_a, other_a], [array_of(unit, 2 * n_attn, f32)] * 4
        )

        normed_part = rows_of(normed_all, core * rows + half * part, part)
        inverse_part = rows_of(inverse_all, core * rows + half * part, part)
        grad_gain_a = jnp.sum(grad_h_one * normed_part, axis=0, keepdims=True)
        grad_x = (grad_after + norm_back(grad_h_one * gain_a, normed_part, inverse_part)).astype(bf16)
        grad_tokens = join_tokens(grad_x, swap_tp(grad_x), half, nat, block)

        grad_gains = cat([grad_gain_a, grad_gain_m])
        grad_gains = grad_gains + swap_tp(grad_gains)
        for mask in [1 << bit for bit in range(shards.bit_length() - 2, 1, -1)] + [1, 2]:
            mid = grad_gains.shape[1] // 2
            first, second = grad_gains[:, :mid], grad_gains[:, mid:]
            low = (shard & mask) == 0
            grad_gains = jnp.where(low, first, second) + across(jnp.where(low, second, first), mask)
        first, second = grad_gains[:, :unit], grad_gains[:, unit:]
        grad_gains = jnp.where(core == 0, first, second) + swap_core(jnp.where(core == 0, second, first))

        return (
            output,
            grad_tokens,
            grad_gains[0],
            grad_w_query,
            grad_w_key,
            grad_w_value,
            grad_w_out,
            grad_gains[1],
            grad_w_gate,
            grad_w_up,
            grad_w_down,
        )

    return per_device


def solution(mesh):
    wide = P(("shard", "ctx"), None)
    flat = P(("shard", "ctx"))
    both = P(("shard", "ctx"), "tp")
    placed = (wide, P("shard", None), flat, both, both, both, both, flat, both, both, both, wide)
    return jax.shard_map(
        build(mesh.shape["shard"]),
        mesh=mesh,
        in_specs=placed,
        out_specs=(wide, wide, flat, both, both, both, both, flat, both, both, both),
        check_vma=False,
    )
```

```python
import math

import jax
import jax.numpy as jnp
from jax import lax
from jax.experimental import pallas as pl
from jax.experimental.pallas import tpu as pltpu
from jax.sharding import PartitionSpec as P

HD = 128
LENGTH = 1024


norm_eps = 1e-05
rope_base = 10000.0

bf16 = jnp.bfloat16
f32 = jnp.float32


def matmul(left, right):
    return jnp.dot(left, right, preferred_element_type=jnp.float32)


def contract_rows(left, right):
    return lax.dot_general(
        left, right, (((0,), (0,)), ((), ())), preferred_element_type=jnp.float32
    )


def contract_cols(left, right):
    return lax.dot_general(
        left, right, (((1,), (1,)), ((), ())), preferred_element_type=jnp.float32
    )


def norm_parts(values):
    inverse = lax.rsqrt(jnp.mean(values * values, axis=-1, keepdims=True) + norm_eps)
    return (values * inverse, inverse)


def norm_back(grad_scaled, normed, inverse):
    return inverse * (grad_scaled - normed * jnp.mean(grad_scaled * normed, axis=-1, keepdims=True))


def doc_positions(seg_row):
    places = jnp.arange(seg_row.shape[0], dtype=jnp.int32)
    starts_here = jnp.concatenate([jnp.ones((1,), dtype=jnp.bool_), seg_row[1:] != seg_row[:-1]])
    starts = lax.cummax(jnp.where(starts_here, places, jnp.zeros_like(places)), axis=0)
    return places - starts


def rope_tables(positions):
    half_dim = HD // 2
    freqs = rope_base ** (-(jnp.arange(half_dim, dtype=jnp.float32) * (2.0 / HD)))
    angles = positions.astype(jnp.float32)[:, None] * freqs[None, :]
    cosine, sine = jnp.cos(angles), jnp.sin(angles)
    return cat([cosine, cosine], 1), cat([-sine, sine], 1)


def cat(parts, axis=0):
    return jnp.concatenate(parts, axis=axis)


def rows_of(values, start, size):
    return lax.dynamic_slice_in_dim(values, start, size, 0)


def ordered(index, own, other, axis=0):
    return jnp.where(index == 0, cat([own, other], axis), cat([other, own], axis))


def after(values, *events):
    return lax.optimization_barrier((values, events))[0]


def small_call(body, scalars, arrays, outs):
    scalars = jnp.stack([jnp.asarray(v, jnp.int32) for v in scalars])
    return pl.pallas_call(
        body,
        grid_spec=pltpu.PrefetchScalarGridSpec(
            num_scalar_prefetch=1,
            grid=(1,),
            in_specs=[pl.BlockSpec(a.shape, lambda i, s: (0, 0)) for a in arrays],
            out_specs=[pl.BlockSpec(o.shape, lambda i, s: (0, 0)) for o in outs],
        ),
        out_shape=outs,
    )(scalars, *arrays)


def array_of(rows, cols, dtype=bf16):
    return jax.ShapeDtypeStruct((rows, cols), dtype)


def permute_cols(values, index, block):
    rows, width = values.shape
    step = min(rows, 128)
    count = width // block
    if block % 128:
        return cat([lax.dynamic_slice_in_dim(values, index[j] * block, block, 1) for j in range(count)], 1)

    def body(index_ref, in_ref, out_ref):
        for j in range(count):
            start = pl.multiple_of(index_ref[j] * block, block)
            out_ref[:, j * block : (j + 1) * block] = in_ref[:, pl.ds(start, block)]

    spec = pl.BlockSpec((step, width), lambda i, s: (i, 0))
    return pl.pallas_call(
        body,
        grid_spec=pltpu.PrefetchScalarGridSpec(
            num_scalar_prefetch=1, grid=(rows // step,), in_specs=[spec], out_specs=spec
        ),
        out_shape=jax.ShapeDtypeStruct(values.shape, values.dtype),
    )(index, values)


def join_tokens(own, other, half, index, block):
    rows, width = own.shape
    count = width // block
    if block % 128:
        return permute_cols(ordered(half, own, other), index, block)

    def body(index_ref, own_ref, other_ref, out_ref):
        here = pl.program_id(0) == index_ref[count]

        def move(ref):
            for j in range(count):
                start = pl.multiple_of(index_ref[j] * block, block)
                out_ref[:, j * block : (j + 1) * block] = ref[:, pl.ds(start, block)]

        pl.when(here)(lambda: move(own_ref))
        pl.when(jnp.logical_not(here))(lambda: move(other_ref))

    whole = pl.BlockSpec((rows, width), lambda i, s: (0, 0))
    return pl.pallas_call(
        body,
        grid_spec=pltpu.PrefetchScalarGridSpec(
            num_scalar_prefetch=1,
            grid=(2,),
            in_specs=[whole, whole],
            out_specs=pl.BlockSpec((rows, width), lambda i, s: (i, 0)),
        ),
        out_shape=jax.ShapeDtypeStruct((2 * rows, width), own.dtype),
    )(cat([index, half[None]]), own, other)


def score_parts(query, keys, rows_seg, cols_seg, diagonal):
    scores = contract_cols(query, keys) * (1.0 / math.sqrt(HD)) - math.log(LENGTH)
    allowed = rows_seg == cols_seg
    if diagonal:
        size = query.shape[0]
        places = lax.broadcasted_iota(jnp.int32, (size, size), 0)
        allowed = allowed & (places >= lax.broadcasted_iota(jnp.int32, (size, size), 1))
    return jax.nn.sigmoid(scores), allowed


def swap_halves(values):
    return pltpu.roll(values, HD // 2, 1)


def attend_forward(qkv, seg_row, cosine, sine, tile=256):
    length = seg_row.shape[0]
    heads = qkv.shape[1] // (3 * HD)
    tiles = length // tile

    def body(seg_ref, qkv_ref, cos_ref, sin_ref, seg_col, seg_line, out_ref, kept_ref, acc):
        cos_t, sin_t = cos_ref[...], sin_ref[...]
        for part in (0, 1):
            where = slice(part * HD, (part + 1) * HD)
            value = qkv_ref[:, where]
            kept_ref[:, where] = (value * cos_t + swap_halves(value) * sin_t).astype(bf16)
        kept_ref[:, 2 * HD :] = qkv_ref[:, 2 * HD :].astype(bf16)
        for i in range(tiles):
            rows = slice(i * tile, (i + 1) * tile)

            def step(j, diagonal, rows=rows):
                cols = slice(j * tile, (j + 1) * tile)
                sig, allowed = score_parts(
                    kept_ref[rows, :HD], kept_ref[cols, HD : 2 * HD],
                    seg_col[rows, :], seg_line[:, cols], diagonal,
                )
                weights = jnp.where(allowed, sig, 0.0).astype(bf16)
                return matmul(weights, kept_ref[cols, 2 * HD :])

            acc[...] = step(i, True)
            for j in range(i):

                @pl.when(seg_ref[(j + 1) * tile - 1] == seg_ref[i * tile])
                def _(j=j):
                    acc[...] += step(j, False)

            out_ref[rows, :] = acc[...].astype(bf16)

    full = pl.BlockSpec((length, HD), lambda h, s: (0, 0))
    return pl.pallas_call(
        body,
        grid_spec=pltpu.PrefetchScalarGridSpec(
            num_scalar_prefetch=1,
            grid=(heads,),
            in_specs=[
                pl.BlockSpec((length, 3 * HD), lambda h, s: (0, h)),
                full,
                full,
                pl.BlockSpec((length, 1), lambda h, s: (0, 0)),
                pl.BlockSpec((1, length), lambda h, s: (0, 0)),
            ],
            out_specs=[
                pl.BlockSpec((length, HD), lambda h, s: (0, h)),
                pl.BlockSpec((length, 3 * HD), lambda h, s: (0, h)),
            ],
            scratch_shapes=[pltpu.VMEM((tile, HD), f32)],
        ),
        out_shape=[array_of(length, heads * HD), array_of(length, 3 * heads * HD)],
    )(seg_row, qkv, cosine, sine, seg_row[:, None], seg_row[None, :])


def attend_backward(kept, grad_heads, seg_row, cosine, sine, first, heads, tile=256):
    length = seg_row.shape[0]
    tiles = length // tile
    scale = 1.0 / math.sqrt(HD)

    def body(seg_ref, kept_ref, do_ref, cos_ref, sin_ref, seg_col, seg_line, out_ref, dq, dk, dv):
        dk[...] = jnp.zeros_like(dk)
        dv[...] = jnp.zeros_like(dv)
        for i in range(tiles):
            rows = slice(i * tile, (i + 1) * tile)

            def step(j, diagonal, rows=rows):
                cols = slice(j * tile, (j + 1) * tile)
                query, grad = kept_ref[rows, :HD], do_ref[rows, :]
                keys = kept_ref[cols, HD : 2 * HD]
                sig, allowed = score_parts(query, keys, seg_col[rows, :], seg_line[:, cols], diagonal)
                weights = jnp.where(allowed, sig, 0.0).astype(bf16)
                dv[cols, :] += contract_rows(weights, grad)
                grad_probs = contract_cols(grad, kept_ref[cols, 2 * HD :])
                grad_scores = jnp.where(allowed, grad_probs * sig * (1.0 - sig), 0.0).astype(bf16)
                dk[cols, :] += contract_rows(grad_scores, query)
                return matmul(grad_scores, keys)

            dq[rows, :] = step(i, True)
            for j in range(i):

                @pl.when(seg_ref[(j + 1) * tile - 1] == seg_ref[i * tile])
                def _(j=j, rows=rows):
                    dq[rows, :] += step(j, False)

        cos_t, sin_t = cos_ref[...], sin_ref[...]
        for part, ref in ((0, dq), (1, dk)):
            grad = ref[...] * scale
            out_ref[:, part * HD : (part + 1) * HD] = (grad * cos_t - swap_halves(grad) * sin_t).astype(bf16)
        out_ref[:, 2 * HD :] = dv[...].astype(bf16)

    full = pl.BlockSpec((length, HD), lambda h, s: (0, 0))
    return pl.pallas_call(
        body,
        grid_spec=pltpu.PrefetchScalarGridSpec(
            num_scalar_prefetch=1,
            grid=(heads,),
            in_specs=[
                pl.BlockSpec((length, 3 * HD), lambda h, s: (0, first + h)),
                pl.BlockSpec((length, HD), lambda h, s: (0, first + h)),
                full,
                full,
                pl.BlockSpec((length, 1), lambda h, s: (0, 0)),
                pl.BlockSpec((1, length), lambda h, s: (0, 0)),
            ],
            out_specs=pl.BlockSpec((length, 3 * HD), lambda h, s: (0, h)),
            scratch_shapes=[pltpu.VMEM((length, HD), f32)] * 3,
        ),
        out_shape=array_of(length, 3 * heads * HD),
    )(seg_row, kept, grad_heads, cosine, sine, seg_row[:, None], seg_row[None, :])


def build(shards):
    line = [k << 1 for k in range(1, shards // 2)]

    groups = [[i for i in range(shards) if (i >> 1) & 1 == bit] for bit in (0, 1)]
    every = [[(i & ~3) | ((i & 1) << 1) | ((i >> 1) & 1) for i in range(shards)]]

    def across(values, mask):
        return lax.ppermute(values, "shard", [(i, i ^ mask) for i in range(shards)])

    def swap_core(values):
        return lax.ppermute(values, "ctx", [(0, 1), (1, 0)])

    def swap_tp(values):
        return lax.ppermute(values, "tp", [(0, 1), (1, 0)])

    def per_device(
        tokens,
        segments,
        gain_attn,
        w_query,
        w_key,
        w_value,
        w_out,
        gain_mlp,
        w_gate,
        w_up,
        w_down,
        cotangent,
    ):
        shard = lax.axis_index("shard").astype(jnp.int32)
        core = lax.axis_index("ctx").astype(jnp.int32)
        half = lax.axis_index("tp").astype(jnp.int32)
        y, zl = shard & 1, (shard >> 1) & 1
        rows, width = tokens.shape
        part = rows // 2
        block = width // shards
        unit = block // 2
        n_attn = w_query.shape[1] // 2
        n_ff = w_gate.shape[1] // 4
        heads = n_attn // HD
        half_s = shards // 2
        pad = 16

        def place_of(number):
            return (number & ~3) | ((number & 1) << 1) | ((number >> 1) & 1)

        rel = place_of(jnp.arange(shards, dtype=jnp.int32))
        nat = rel

        attn_w = [w_query, w_key, w_value, w_out]
        ff_w = [w_gate, w_up, w_down]

        def send_attn(s_ref, q, k, v, o, out):
            start = pl.multiple_of((1 - s_ref[0]) * n_attn, n_attn)
            for h in range(heads):
                for i, ref in enumerate((q, k, v)):
                    out[:, (3 * h + i) * HD : (3 * h + i + 1) * HD] = ref[:, pl.ds(start + h * HD, HD)]
            out[:, 3 * n_attn :] = o[:, pl.ds(start, n_attn)]

        (sent_a,) = small_call(send_attn, [core], attn_w, [array_of(unit, 4 * n_attn)])
        other_a = swap_core(sent_a)
        gains = jnp.stack([gain_attn, gain_mlp])
        other_gains = swap_core(gains)

        def keep_attn(s_ref, q, k, v, o, other, own_g, other_g, out_qkv, out_o):
            me = s_ref[0]
            start = pl.multiple_of(me * n_attn, n_attn)
            mine, theirs = pl.ds(me * unit, unit), pl.ds((1 - me) * unit, unit)
            for h in range(heads):
                for i, ref in enumerate((q, k, v)):
                    where = slice((3 * h + i) * HD, (3 * h + i + 1) * HD)
                    out_qkv[mine, where] = ref[:, pl.ds(start + h * HD, HD)]
            out_o[mine, :] = o[:, pl.ds(start, n_attn)]
            out_qkv[theirs, :] = other[:, : 3 * n_attn]
            out_o[theirs, :] = other[:, 3 * n_attn :]
            first, second = own_g[...], other_g[...]
            low = jnp.where(me == 0, first, second)
            high = jnp.where(me == 0, second, first)
            line_g = cat([low, high, jnp.zeros((2, n_attn - block), bf16)], 1)
            out_o[block:, :] = cat([line_g, jnp.zeros((pad - 2, n_attn), bf16)])

        block_qkv, block_o = small_call(
            keep_attn, [core], attn_w + [other_a, gains, other_gains],
            [array_of(block, 3 * n_attn), array_of(block + pad, n_attn)],
        )

        def shard_at(i):
            return shard ^ (((i % half_s) << 1) | (i // half_s))

        weight_qkv = lax.all_gather(block_qkv, "shard", axis=0, tiled=True, axis_index_groups=every)
        near_o = cat([block_o] + [across(block_o, mask) for mask in line])
        parts_o = cat([near_o, across(near_o, 1)]).reshape(shards, block + pad, n_attn)
        weight_o = jnp.zeros((width, n_attn), bf16)
        for i in range(shards):
            weight_o = lax.dynamic_update_slice_in_dim(
                weight_o, parts_o[i, :block], place_of(shard_at(i)) * block, 0
            )
        gain_rows = parts_o[:, block : block + 2, :block]
        away_bits = place_of(jnp.arange(shards, dtype=jnp.int32)) ^ shard
        gain_rows = gain_rows[(away_bits >> 1) + half_s * (away_bits & 1)]
        gains_rel = jnp.transpose(gain_rows, (1, 0, 2)).reshape(2, width).astype(f32)
        gain_a, gain_m = gains_rel[0:1], gains_rel[1:2]

        def send_ff(s_ref, g, u, d, out):
            start = pl.multiple_of((1 - s_ref[0]) * 2 * n_ff, n_ff)
            for i, ref in enumerate((g, u, d)):
                out[:, i * 2 * n_ff : (i + 1) * 2 * n_ff] = ref[:, pl.ds(start, 2 * n_ff)]

        (sent_f,) = small_call(send_ff, [core], ff_w, [array_of(unit, 6 * n_ff)])
        other_f = swap_core(sent_f)

        def keep_ff(s_ref, g, u, d, other, keep, send):
            me, low = s_ref[0], s_ref[1]
            mine, theirs = pl.ds(pl.multiple_of(me * unit, unit), unit), pl.ds(pl.multiple_of((1 - me) * unit, unit), unit)
            for out, which in ((keep, low), (send, 1 - low)):
                start = pl.multiple_of(which * n_ff, n_ff)
                for i, ref in enumerate((g, u, d)):
                    cols = slice(i * n_ff, (i + 1) * n_ff)
                    out[mine, cols] = ref[:, pl.ds(pl.multiple_of(me * 2 * n_ff, n_ff) + start, n_ff)]
                    out[theirs, cols] = other[:, pl.ds(i * 2 * n_ff + start, n_ff)]

        keep_f, send_f = small_call(keep_ff, [core, zl], ff_w + [other_f], [array_of(block, 3 * n_ff)] * 2)
        recv_f = across(send_f, 2)

        def pair_rows(s_ref, own, other, out):
            low = s_ref[0]
            out[pl.ds(pl.multiple_of(low * block, block), block), :] = own[...]
            out[pl.ds(pl.multiple_of((1 - low) * block, block), block), :] = other[...]

        (pair_f,) = small_call(pair_rows, [zl], [keep_f, recv_f], [array_of(2 * block, 3 * n_ff)])

        seg_row = segments[0]
        cosine, sine = rope_tables(doc_positions(seg_row))
        x_own = permute_cols(tokens, rel, block)
        x_both = ordered(core, x_own, swap_core(x_own))
        normed_all, inverse_all = norm_parts(x_both.astype(f32))
        h_one = (normed_all * gain_a).astype(bf16)
        pair_f = after(pair_f, weight_qkv, weight_o, h_one, cosine, sine)
        weight_f = lax.all_gather(pair_f, "shard", axis=0, tiled=True, axis_index_groups=groups)
        weight_g, weight_u, weight_d = [weight_f[:, i * n_ff : (i + 1) * n_ff] for i in range(3)]
        qkv = matmul(h_one, weight_qkv)
        mixed, kept = attend_forward(qkv, seg_row, cosine, sine)

        def to_slice(operand, project):
            away = project(rows_of(operand, (1 - core) * rows, rows)).astype(bf16)
            here = rows_of(operand, core * rows, rows)
            away = swap_core(away)
            other = project(rows_of(here, (1 - half) * part, part)) + rows_of(
                away, (1 - half) * part, part
            ).astype(f32)
            other = swap_tp(other.astype(bf16))
            own = project(rows_of(here, half * part, part)) + rows_of(
                away, half * part, part
            ).astype(f32)
            return own + other.astype(f32)

        x_part = rows_of(x_own, half * part, part).astype(f32)
        after_attn = x_part + to_slice(mixed, lambda v: contract_cols(v, weight_o))
        normed_two, inverse_two = norm_parts(after_attn)
        h_part = (normed_two * gain_m).astype(bf16)

        by_tp, by_zl = swap_tp(h_part), across(h_part, 2)
        mid = part // 2
        near = cat([h_part, by_tp, by_zl])
        far_near = swap_core(near)
        both = cat([across(by_tp[:mid], 2), swap_tp(by_zl[mid:])])
        h_two = cat([near, both, far_near, swap_core(both)])

        dy_rel = permute_cols(cotangent, rel, block)
        dy_ff = cat([rows_of(dy_rel, half * part, part), rows_of(dy_rel, (1 - half) * part, part)])
        dy_zl = across(after(dy_ff[:part], both), 2)
        near = cat([dy_ff, dy_zl, swap_tp(dy_zl)])
        grad_out = cat([near, swap_core(near)])

        gate_pre = matmul(h_two, weight_g)
        up_pre = matmul(h_two, weight_u)
        gate_sig = jax.nn.sigmoid(gate_pre)
        gate_act = gate_pre * gate_sig
        hidden = (gate_act * up_pre).astype(bf16)

        def from_tokens(project):
            count = 4 * part
            away = swap_core(project(slice(count, 2 * count)).astype(bf16))
            total = project(slice(0, count)) + away.astype(f32)
            mid = width // 2
            low, high = total[:, :mid], total[:, mid:]

            def pick(values, i):
                return values[i * part : (i + 1) * part]

            low_tp = swap_tp(cat([pick(low, 1), pick(low, 3)]).astype(bf16)).astype(f32)
            high_zl = across(cat([pick(high, 2), pick(high, 3)]).astype(bf16), 2).astype(f32)
            low_zl = across((pick(low, 2) + pick(low_tp, 1)).astype(bf16), 2).astype(f32)
            high_tp = swap_tp((pick(high, 1) + pick(high_zl, 1)).astype(bf16)).astype(f32)
            low_sum = pick(low, 0) + pick(low_tp, 0) + low_zl
            high_sum = pick(high, 0) + pick(high_zl, 0) + high_tp
            return away, cat([low_sum, high_sum], 1)

        grad_hidden = matmul(grad_out, weight_d)
        grad_gate = (grad_hidden * up_pre * gate_sig * (1.0 + gate_pre * (1.0 - gate_sig))).astype(bf16)
        grad_up = (grad_hidden * gate_act).astype(bf16)
        prod_d = contract_rows(grad_out, hidden).astype(bf16)
        prod_gu = cat(
            [contract_rows(h_two, grad_gate).astype(bf16), contract_rows(h_two, grad_up).astype(bf16)], 1
        )
        grad_gate, grad_up = after((grad_gate, grad_up), prod_d, prod_gu)
        event_h, grad_h_two = from_tokens(
            lambda where: contract_cols(grad_gate[where], weight_g)
            + contract_cols(grad_up[where], weight_u)
        )
        late_hidden = after(hidden, grad_h_two)
        event_m, mlp = from_tokens(lambda where: contract_cols(late_hidden[where], weight_d))
        out_part = (after_attn + mlp).astype(bf16)
        output = join_tokens(out_part, swap_tp(out_part), half, nat, block)

        grad_gain_m = jnp.sum(grad_h_two * normed_two, axis=0, keepdims=True)
        dy_part = rows_of(dy_rel, half * part, part).astype(f32)
        grad_after = dy_part + norm_back(grad_h_two * gain_m, normed_two, inverse_two)

        grad_part = grad_after.astype(bf16)
        grad_half = ordered(half, grad_part, swap_tp(grad_part))
        grad_attn = ordered(core, grad_half, swap_core(grad_half))
        grad_mixed = matmul(grad_attn, weight_o).astype(bf16)

        def scatter(values, members):
            return lax.psum_scatter(
                values.astype(bf16), "shard", scatter_dimension=0, tiled=True, axis_index_groups=members
            )

        def rows_pair(own, count):
            other = across(rows_of(own, (1 - zl) * block, block), 2)

            def send_rows(s_ref, mine, theirs, out):
                low, away_rows = s_ref[1], pl.multiple_of((1 - s_ref[0]) * unit, unit)
                rows_m = pl.ds(pl.multiple_of(low * block, block) + away_rows, unit)
                for i in range(count):
                    cols = slice(i * n_ff, (i + 1) * n_ff)
                    out[:, pl.ds(i * 2 * n_ff + pl.multiple_of(low * n_ff, n_ff), n_ff)] = mine[rows_m, cols]
                    out[:, pl.ds(i * 2 * n_ff + pl.multiple_of((1 - low) * n_ff, n_ff), n_ff)] = theirs[
                        pl.ds(away_rows, unit), cols
                    ]

            (sent,) = small_call(send_rows, [core, zl], [own, other], [array_of(unit, 2 * count * n_ff)])
            third = swap_core(sent)

            def join_rows(s_ref, mine, theirs, third_ref, *outs):
                me, low = s_ref[0], s_ref[1]
                start = pl.multiple_of(me * 2 * n_ff, n_ff)
                away = pl.multiple_of((1 - me) * 2 * n_ff, n_ff)
                here = pl.multiple_of(me * unit, unit)
                for i, out in enumerate(outs):
                    cols = slice(i * n_ff, (i + 1) * n_ff)
                    out[:, pl.ds(start + pl.multiple_of(low * n_ff, n_ff), n_ff)] = mine[
                        pl.ds(pl.multiple_of(low * block, block) + here, unit), cols
                    ].astype(f32)
                    out[:, pl.ds(start + pl.multiple_of((1 - low) * n_ff, n_ff), n_ff)] = theirs[
                        pl.ds(here, unit), cols
                    ].astype(f32)
                    out[:, pl.ds(away, 2 * n_ff)] = third_ref[:, i * 2 * n_ff : (i + 1) * 2 * n_ff].astype(f32)

            return small_call(join_rows, [core, zl], [own, other, third], [array_of(unit, 4 * n_ff, f32)] * count)

        def send_unit(s_ref, own, out):
            out[...] = own[pl.ds((1 - s_ref[0]) * unit, unit), :].astype(bf16)

        own_d = scatter(prod_d, groups)
        own_gu = scatter(prod_gu, groups)
        late_o = contract_rows(grad_attn, mixed).astype(bf16)
        own_o = scatter(after(late_o, own_d, own_gu), every)
        grad_mixed = after(grad_mixed, late_o)
        grad_qkv = attend_backward(kept, grad_mixed, seg_row, cosine, sine, 0, heads)
        own_qkv = scatter(after(contract_rows(h_one, grad_qkv).astype(bf16), own_o), every)

        (grad_w_down,) = rows_pair(own_d, 1)
        grad_w_gate, grad_w_up = rows_pair(own_gu, 2)

        grad_h_one = to_slice(grad_qkv, lambda v: contract_cols(v, weight_qkv))

        own_a = cat([own_qkv, own_o], 1)
        (sent_g,) = small_call(send_unit, [core], [own_a], [array_of(unit, 4 * n_attn)])
        other_a = swap_core(sent_g)

        def join_attn(s_ref, own, other, q, k, v, o):
            me = s_ref[0]
            mine = pl.ds(pl.multiple_of(me * unit, unit), unit)
            here, there = me * n_attn, (1 - me) * n_attn
            for start, load in (
                (here, lambda c: own[mine, c].astype(f32)),
                (there, lambda c: other[:, c].astype(f32)),
            ):
                start = pl.multiple_of(start, n_attn)
                for h in range(heads):
                    for i, ref in enumerate((q, k, v)):
                        ref[:, pl.ds(start + h * HD, HD)] = load(slice((3 * h + i) * HD, (3 * h + i + 1) * HD))
                o[:, pl.ds(start, n_attn)] = load(slice(3 * n_attn, 4 * n_attn))

        grad_w_query, grad_w_key, grad_w_value, grad_w_out = small_call(
            join_attn, [core], [own_a, other_a], [array_of(unit, 2 * n_attn, f32)] * 4
        )

        normed_part = rows_of(normed_all, core * rows + half * part, part)
        inverse_part = rows_of(inverse_all, core * rows + half * part, part)
        grad_gain_a = jnp.sum(grad_h_one * normed_part, axis=0, keepdims=True)
        grad_x = (grad_after + norm_back(grad_h_one * gain_a, normed_part, inverse_part)).astype(bf16)
        grad_tokens = join_tokens(grad_x, swap_tp(grad_x), half, nat, block)

        grad_gains = cat([grad_gain_a, grad_gain_m])
        grad_gains = grad_gains + swap_tp(grad_gains)
        for mask in [1 << bit for bit in range(shards.bit_length() - 2, 1, -1)] + [1, 2]:
            mid = grad_gains.shape[1] // 2
            first, second = grad_gains[:, :mid], grad_gains[:, mid:]
            low = (shard & mask) == 0
            grad_gains = jnp.where(low, first, second) + across(jnp.where(low, second, first), mask)
        first, second = grad_gains[:, :unit], grad_gains[:, unit:]
        grad_gains = jnp.where(core == 0, first, second) + swap_core(jnp.where(core == 0, second, first))

        return (
            output,
            grad_tokens,
            grad_gains[0],
            grad_w_query,
            grad_w_key,
            grad_w_value,
            grad_w_out,
            grad_gains[1],
            grad_w_gate,
            grad_w_up,
            grad_w_down,
        )

    return per_device


def solution(mesh):
    wide = P(("shard", "ctx"), None)
    flat = P(("shard", "ctx"))
    both = P(("shard", "ctx"), "tp")
    placed = (wide, P("shard", None), flat, both, both, both, both, flat, both, both, both, wide)
    return jax.shard_map(
        build(mesh.shape["shard"]),
        mesh=mesh,
        in_specs=placed,
        out_specs=(wide, wide, flat, both, both, both, both, flat, both, both, both),
        check_vma=False,
    )
```

```python
import math

import jax
import jax.numpy as jnp
from jax import lax
from jax.experimental import pallas as pl
from jax.experimental.pallas import tpu as pltpu
from jax.sharding import PartitionSpec as P

HD = 128
LENGTH = 1024


norm_eps = 1e-05
rope_base = 10000.0

bf16 = jnp.bfloat16
f32 = jnp.float32


def matmul(left, right):
    return jnp.dot(left, right, preferred_element_type=jnp.float32)


def contract_rows(left, right):
    return lax.dot_general(
        left, right, (((0,), (0,)), ((), ())), preferred_element_type=jnp.float32
    )


def contract_cols(left, right):
    return lax.dot_general(
        left, right, (((1,), (1,)), ((), ())), preferred_element_type=jnp.float32
    )


def norm_parts(values):
    inverse = lax.rsqrt(jnp.mean(values * values, axis=-1, keepdims=True) + norm_eps)
    return (values * inverse, inverse)


def norm_back(grad_scaled, normed, inverse):
    return inverse * (grad_scaled - normed * jnp.mean(grad_scaled * normed, axis=-1, keepdims=True))


def doc_positions(seg_row):
    places = jnp.arange(seg_row.shape[0], dtype=jnp.int32)
    starts_here = jnp.concatenate([jnp.ones((1,), dtype=jnp.bool_), seg_row[1:] != seg_row[:-1]])
    starts = lax.cummax(jnp.where(starts_here, places, jnp.zeros_like(places)), axis=0)
    return places - starts


def rope_tables(positions):
    half_dim = HD // 2
    freqs = rope_base ** (-(jnp.arange(half_dim, dtype=jnp.float32) * (2.0 / HD)))
    angles = positions.astype(jnp.float32)[:, None] * freqs[None, :]
    cosine, sine = jnp.cos(angles), jnp.sin(angles)
    return cat([cosine, cosine], 1), cat([-sine, sine], 1)


def cat(parts, axis=0):
    return jnp.concatenate(parts, axis=axis)


def rows_of(values, start, size):
    return lax.dynamic_slice_in_dim(values, start, size, 0)


def ordered(index, own, other, axis=0):
    return jnp.where(index == 0, cat([own, other], axis), cat([other, own], axis))


def after(values, *events):
    return lax.optimization_barrier((values, events))[0]


def small_call(body, scalars, arrays, outs):
    scalars = jnp.stack([jnp.asarray(v, jnp.int32) for v in scalars])
    return pl.pallas_call(
        body,
        grid_spec=pltpu.PrefetchScalarGridSpec(
            num_scalar_prefetch=1,
            grid=(1,),
            in_specs=[pl.BlockSpec(a.shape, lambda i, s: (0, 0)) for a in arrays],
            out_specs=[pl.BlockSpec(o.shape, lambda i, s: (0, 0)) for o in outs],
        ),
        out_shape=outs,
    )(scalars, *arrays)


def array_of(rows, cols, dtype=bf16):
    return jax.ShapeDtypeStruct((rows, cols), dtype)


def permute_cols(values, index, block):
    rows, width = values.shape
    step = min(rows, 128)
    count = width // block
    if block % 128:
        return cat([lax.dynamic_slice_in_dim(values, index[j] * block, block, 1) for j in range(count)], 1)

    def body(index_ref, in_ref, out_ref):
        for j in range(count):
            start = pl.multiple_of(index_ref[j] * block, block)
            out_ref[:, j * block : (j + 1) * block] = in_ref[:, pl.ds(start, block)]

    spec = pl.BlockSpec((step, width), lambda i, s: (i, 0))
    return pl.pallas_call(
        body,
        grid_spec=pltpu.PrefetchScalarGridSpec(
            num_scalar_prefetch=1, grid=(rows // step,), in_specs=[spec], out_specs=spec
        ),
        out_shape=jax.ShapeDtypeStruct(values.shape, values.dtype),
    )(index, values)


def join_tokens(own, other, half, index, block):
    rows, width = own.shape
    count = width // block
    if block % 128:
        return permute_cols(ordered(half, own, other), index, block)

    def body(index_ref, own_ref, other_ref, out_ref):
        here = pl.program_id(0) == index_ref[count]

        def move(ref):
            for j in range(count):
                start = pl.multiple_of(index_ref[j] * block, block)
                out_ref[:, j * block : (j + 1) * block] = ref[:, pl.ds(start, block)]

        pl.when(here)(lambda: move(own_ref))
        pl.when(jnp.logical_not(here))(lambda: move(other_ref))

    whole = pl.BlockSpec((rows, width), lambda i, s: (0, 0))
    return pl.pallas_call(
        body,
        grid_spec=pltpu.PrefetchScalarGridSpec(
            num_scalar_prefetch=1,
            grid=(2,),
            in_specs=[whole, whole],
            out_specs=pl.BlockSpec((rows, width), lambda i, s: (i, 0)),
        ),
        out_shape=jax.ShapeDtypeStruct((2 * rows, width), own.dtype),
    )(cat([index, half[None]]), own, other)


def score_parts(query, keys, rows_seg, cols_seg, diagonal):
    scores = contract_cols(query, keys) * (1.0 / math.sqrt(HD)) - math.log(LENGTH)
    allowed = rows_seg == cols_seg
    if diagonal:
        size = query.shape[0]
        places = lax.broadcasted_iota(jnp.int32, (size, size), 0)
        allowed = allowed & (places >= lax.broadcasted_iota(jnp.int32, (size, size), 1))
    return jax.nn.sigmoid(scores), allowed


def swap_halves(values):
    return pltpu.roll(values, HD // 2, 1)


def attend_forward(qkv, seg_row, cosine, sine, tile=256):
    length = seg_row.shape[0]
    heads = qkv.shape[1] // (3 * HD)
    tiles = length // tile

    def body(seg_ref, qkv_ref, cos_ref, sin_ref, seg_col, seg_line, out_ref, kept_ref, acc):
        cos_t, sin_t = cos_ref[...], sin_ref[...]
        for part in (0, 1):
            where = slice(part * HD, (part + 1) * HD)
            value = qkv_ref[:, where]
            kept_ref[:, where] = (value * cos_t + swap_halves(value) * sin_t).astype(bf16)
        kept_ref[:, 2 * HD :] = qkv_ref[:, 2 * HD :].astype(bf16)
        for i in range(tiles):
            rows = slice(i * tile, (i + 1) * tile)

            def step(j, diagonal, rows=rows):
                cols = slice(j * tile, (j + 1) * tile)
                sig, allowed = score_parts(
                    kept_ref[rows, :HD], kept_ref[cols, HD : 2 * HD],
                    seg_col[rows, :], seg_line[:, cols], diagonal,
                )
                weights = jnp.where(allowed, sig, 0.0).astype(bf16)
                return matmul(weights, kept_ref[cols, 2 * HD :])

            acc[...] = step(i, True)
            for j in range(i):

                @pl.when(seg_ref[(j + 1) * tile - 1] == seg_ref[i * tile])
                def _(j=j):
                    acc[...] += step(j, False)

            out_ref[rows, :] = acc[...].astype(bf16)

    full = pl.BlockSpec((length, HD), lambda h, s: (0, 0))
    return pl.pallas_call(
        body,
        grid_spec=pltpu.PrefetchScalarGridSpec(
            num_scalar_prefetch=1,
            grid=(heads,),
            in_specs=[
                pl.BlockSpec((length, 3 * HD), lambda h, s: (0, h)),
                full,
                full,
                pl.BlockSpec((length, 1), lambda h, s: (0, 0)),
                pl.BlockSpec((1, length), lambda h, s: (0, 0)),
            ],
            out_specs=[
                pl.BlockSpec((length, HD), lambda h, s: (0, h)),
                pl.BlockSpec((length, 3 * HD), lambda h, s: (0, h)),
            ],
            scratch_shapes=[pltpu.VMEM((tile, HD), f32)],
        ),
        out_shape=[array_of(length, heads * HD), array_of(length, 3 * heads * HD)],
    )(seg_row, qkv, cosine, sine, seg_row[:, None], seg_row[None, :])


def attend_backward(kept, grad_heads, seg_row, cosine, sine, first, heads, tile=256):
    length = seg_row.shape[0]
    tiles = length // tile
    scale = 1.0 / math.sqrt(HD)

    def body(seg_ref, kept_ref, do_ref, cos_ref, sin_ref, seg_col, seg_line, out_ref, dq, dk, dv):
        dk[...] = jnp.zeros_like(dk)
        dv[...] = jnp.zeros_like(dv)
        for i in range(tiles):
            rows = slice(i * tile, (i + 1) * tile)

            def step(j, diagonal, rows=rows):
                cols = slice(j * tile, (j + 1) * tile)
                query, grad = kept_ref[rows, :HD], do_ref[rows, :]
                keys = kept_ref[cols, HD : 2 * HD]
                sig, allowed = score_parts(query, keys, seg_col[rows, :], seg_line[:, cols], diagonal)
                weights = jnp.where(allowed, sig, 0.0).astype(bf16)
                dv[cols, :] += contract_rows(weights, grad)
                grad_probs = contract_cols(grad, kept_ref[cols, 2 * HD :])
                grad_scores = jnp.where(allowed, grad_probs * sig * (1.0 - sig), 0.0).astype(bf16)
                dk[cols, :] += contract_rows(grad_scores, query)
                return matmul(grad_scores, keys)

            dq[rows, :] = step(i, True)
            for j in range(i):

                @pl.when(seg_ref[(j + 1) * tile - 1] == seg_ref[i * tile])
                def _(j=j, rows=rows):
                    dq[rows, :] += step(j, False)

        cos_t, sin_t = cos_ref[...], sin_ref[...]
        for part, ref in ((0, dq), (1, dk)):
            grad = ref[...] * scale
            out_ref[:, part * HD : (part + 1) * HD] = (grad * cos_t - swap_halves(grad) * sin_t).astype(bf16)
        out_ref[:, 2 * HD :] = dv[...].astype(bf16)

    full = pl.BlockSpec((length, HD), lambda h, s: (0, 0))
    return pl.pallas_call(
        body,
        grid_spec=pltpu.PrefetchScalarGridSpec(
            num_scalar_prefetch=1,
            grid=(heads,),
            in_specs=[
                pl.BlockSpec((length, 3 * HD), lambda h, s: (0, first + h)),
                pl.BlockSpec((length, HD), lambda h, s: (0, first + h)),
                full,
                full,
                pl.BlockSpec((length, 1), lambda h, s: (0, 0)),
                pl.BlockSpec((1, length), lambda h, s: (0, 0)),
            ],
            out_specs=pl.BlockSpec((length, 3 * HD), lambda h, s: (0, h)),
            scratch_shapes=[pltpu.VMEM((length, HD), f32)] * 3,
        ),
        out_shape=array_of(length, 3 * heads * HD),
    )(seg_row, kept, grad_heads, cosine, sine, seg_row[:, None], seg_row[None, :])


def build(shards):
    line = [k << 1 for k in range(1, shards // 2)]

    groups = [[i for i in range(shards) if (i >> 1) & 1 == bit] for bit in (0, 1)]
    every = [[(i & ~3) | ((i & 1) << 1) | ((i >> 1) & 1) for i in range(shards)]]

    def across(values, mask):
        return lax.ppermute(values, "shard", [(i, i ^ mask) for i in range(shards)])

    def swap_core(values):
        return lax.ppermute(values, "ctx", [(0, 1), (1, 0)])

    def swap_tp(values):
        return lax.ppermute(values, "tp", [(0, 1), (1, 0)])

    def per_device(
        tokens,
        segments,
        gain_attn,
        w_query,
        w_key,
        w_value,
        w_out,
        gain_mlp,
        w_gate,
        w_up,
        w_down,
        cotangent,
    ):
        shard = lax.axis_index("shard").astype(jnp.int32)
        core = lax.axis_index("ctx").astype(jnp.int32)
        half = lax.axis_index("tp").astype(jnp.int32)
        y, zl = shard & 1, (shard >> 1) & 1
        rows, width = tokens.shape
        part = rows // 2
        block = width // shards
        unit = block // 2
        n_attn = w_query.shape[1] // 2
        n_ff = w_gate.shape[1] // 4
        heads = n_attn // HD
        half_s = shards // 2

        def place_of(number):
            return (number & ~3) | ((number & 1) << 1) | ((number >> 1) & 1)

        rel = place_of(jnp.arange(shards, dtype=jnp.int32))
        nat = rel

        attn_w = [w_query, w_key, w_value, w_out]
        ff_w = [w_gate, w_up, w_down]

        def send_attn(s_ref, q, k, v, o, out):
            start = pl.multiple_of((1 - s_ref[0]) * n_attn, n_attn)
            for h in range(heads):
                for i, ref in enumerate((q, k, v)):
                    out[:, (3 * h + i) * HD : (3 * h + i + 1) * HD] = ref[:, pl.ds(start + h * HD, HD)]
            out[:, 3 * n_attn :] = o[:, pl.ds(start, n_attn)]

        (sent_a,) = small_call(send_attn, [core], attn_w, [array_of(unit, 4 * n_attn)])
        other_a = swap_core(sent_a)
        gains = jnp.stack([gain_attn, gain_mlp])
        other_gains = swap_core(gains)

        def keep_attn(s_ref, q, k, v, o, other, out):
            me = s_ref[0]
            start = pl.multiple_of(me * n_attn, n_attn)
            mine = pl.ds(pl.multiple_of(me * unit, unit), unit)
            theirs = pl.ds(pl.multiple_of((1 - me) * unit, unit), unit)
            for h in range(heads):
                for i, ref in enumerate((q, k, v)):
                    where = slice((3 * h + i) * HD, (3 * h + i + 1) * HD)
                    out[mine, where] = ref[:, pl.ds(start + h * HD, HD)]
            out[mine, 3 * n_attn :] = o[:, pl.ds(start, n_attn)]
            out[theirs, :] = other[...]

        (block_a,) = small_call(keep_attn, [core], attn_w + [other_a], [array_of(block, 4 * n_attn)])
        weight_a = lax.all_gather(block_a, "shard", axis=0, tiled=True, axis_index_groups=every)
        weight_qkv, weight_o = weight_a[:, : 3 * n_attn], weight_a[:, 3 * n_attn :]

        own_g = ordered(core, gains, other_gains, 1)
        near_g = cat([own_g] + [across(own_g, mask) for mask in line])
        parts_g = cat([near_g, across(near_g, 1)]).reshape(shards, 2, block)
        away_bits = place_of(jnp.arange(shards, dtype=jnp.int32)) ^ shard
        parts_g = parts_g[(away_bits >> 1) + half_s * (away_bits & 1)]
        gains_rel = jnp.transpose(parts_g, (1, 0, 2)).reshape(2, width).astype(f32)
        gain_a, gain_m = gains_rel[0:1], gains_rel[1:2]

        def send_ff(s_ref, g, u, d, out):
            start = pl.multiple_of((1 - s_ref[0]) * 2 * n_ff, n_ff)
            for i, ref in enumerate((g, u, d)):
                out[:, i * 2 * n_ff : (i + 1) * 2 * n_ff] = ref[:, pl.ds(start, 2 * n_ff)]

        (sent_f,) = small_call(send_ff, [core], ff_w, [array_of(unit, 6 * n_ff)])
        other_f = swap_core(sent_f)

        def keep_ff(s_ref, g, u, d, other, keep, send):
            me, low = s_ref[0], s_ref[1]
            mine, theirs = pl.ds(pl.multiple_of(me * unit, unit), unit), pl.ds(pl.multiple_of((1 - me) * unit, unit), unit)
            for out, which in ((keep, low), (send, 1 - low)):
                start = pl.multiple_of(which * n_ff, n_ff)
                for i, ref in enumerate((g, u, d)):
                    cols = slice(i * n_ff, (i + 1) * n_ff)
                    out[mine, cols] = ref[:, pl.ds(pl.multiple_of(me * 2 * n_ff, n_ff) + start, n_ff)]
                    out[theirs, cols] = other[:, pl.ds(i * 2 * n_ff + start, n_ff)]

        keep_f, send_f = small_call(keep_ff, [core, zl], ff_w + [other_f], [array_of(block, 3 * n_ff)] * 2)
        recv_f = across(send_f, 2)

        def pair_rows(s_ref, own, other, out):
            low = s_ref[0]
            out[pl.ds(pl.multiple_of(low * block, block), block), :] = own[...]
            out[pl.ds(pl.multiple_of((1 - low) * block, block), block), :] = other[...]

        (pair_f,) = small_call(pair_rows, [zl], [keep_f, recv_f], [array_of(2 * block, 3 * n_ff)])

        seg_row = segments[0]
        cosine, sine = rope_tables(doc_positions(seg_row))
        x_own = permute_cols(tokens, rel, block)
        x_both = ordered(core, x_own, swap_core(x_own))
        normed_all, inverse_all = norm_parts(x_both.astype(f32))
        h_one = (normed_all * gain_a).astype(bf16)
        pair_f = after(pair_f, weight_a, h_one, cosine, sine)
        weight_f = lax.all_gather(pair_f, "shard", axis=0, tiled=True, axis_index_groups=groups)
        weight_g, weight_u, weight_d = [weight_f[:, i * n_ff : (i + 1) * n_ff] for i in range(3)]
        qkv = matmul(h_one, weight_qkv)
        mixed, kept = attend_forward(qkv, seg_row, cosine, sine)

        def to_slice(operand, project):
            away = project(rows_of(operand, (1 - core) * rows, rows)).astype(bf16)
            here = rows_of(operand, core * rows, rows)
            away = swap_core(away)
            other = project(rows_of(here, (1 - half) * part, part)) + rows_of(
                away, (1 - half) * part, part
            ).astype(f32)
            other = swap_tp(other.astype(bf16))
            own = project(rows_of(here, half * part, part)) + rows_of(
                away, half * part, part
            ).astype(f32)
            return own + other.astype(f32)

        x_part = rows_of(x_own, half * part, part).astype(f32)
        after_attn = x_part + to_slice(mixed, lambda v: contract_cols(v, weight_o))
        normed_two, inverse_two = norm_parts(after_attn)
        h_part = (normed_two * gain_m).astype(bf16)

        by_tp, by_zl = swap_tp(h_part), across(h_part, 2)
        mid = part // 2
        near = cat([h_part, by_tp, by_zl])
        far_near = swap_core(near)
        both = cat([across(by_tp[:mid], 2), swap_tp(by_zl[mid:])])
        h_two = cat([near, both, far_near, swap_core(both)])

        dy_rel = permute_cols(cotangent, rel, block)
        dy_ff = cat([rows_of(dy_rel, half * part, part), rows_of(dy_rel, (1 - half) * part, part)])
        dy_zl = across(after(dy_ff[:part], both), 2)
        near = cat([dy_ff, dy_zl, swap_tp(dy_zl)])
        grad_out = cat([near, swap_core(near)])

        gate_pre = matmul(h_two, weight_g)
        up_pre = matmul(h_two, weight_u)
        gate_sig = jax.nn.sigmoid(gate_pre)
        gate_act = gate_pre * gate_sig
        hidden = (gate_act * up_pre).astype(bf16)

        def from_tokens(project):
            count = 4 * part
            away = swap_core(project(slice(count, 2 * count)).astype(bf16))
            total = project(slice(0, count)) + away.astype(f32)
            mid = width // 2
            low, high = total[:, :mid], total[:, mid:]

            def pick(values, i):
                return values[i * part : (i + 1) * part]

            low_tp = swap_tp(cat([pick(low, 1), pick(low, 3)]).astype(bf16)).astype(f32)
            high_zl = across(cat([pick(high, 2), pick(high, 3)]).astype(bf16), 2).astype(f32)
            low_sent = (pick(low, 2) + pick(low_tp, 1)).astype(bf16)
            high_sent = (pick(high, 1) + pick(high_zl, 1)).astype(bf16)
            low_zl = across(low_sent, 2).astype(f32)
            high_tp = swap_tp(high_sent).astype(f32)
            low_sum = pick(low, 0) + pick(low_tp, 0) + low_zl
            high_sum = pick(high, 0) + pick(high_zl, 0) + high_tp
            return cat([low_sum, high_sum], 1)

        grad_hidden = matmul(grad_out, weight_d)
        grad_gate = (grad_hidden * up_pre * gate_sig * (1.0 + gate_pre * (1.0 - gate_sig))).astype(bf16)
        grad_up = (grad_hidden * gate_act).astype(bf16)
        prod_d = contract_rows(grad_out, hidden).astype(bf16)
        prod_gu = cat(
            [contract_rows(h_two, grad_gate).astype(bf16), contract_rows(h_two, grad_up).astype(bf16)], 1
        )
        grad_gate, grad_up = after((grad_gate, grad_up), prod_d, prod_gu)
        grad_h_two = from_tokens(
            lambda where: contract_cols(grad_gate[where], weight_g)
            + contract_cols(grad_up[where], weight_u)
        )
        grad_gain_m = jnp.sum(grad_h_two * normed_two, axis=0, keepdims=True)
        dy_part = rows_of(dy_rel, half * part, part).astype(f32)
        grad_after = dy_part + norm_back(grad_h_two * gain_m, normed_two, inverse_two)

        grad_part = grad_after.astype(bf16)
        grad_half = ordered(half, grad_part, swap_tp(grad_part))
        grad_attn = ordered(core, grad_half, swap_core(grad_half))
        grad_mixed = matmul(grad_attn, weight_o).astype(bf16)

        def scatter(values, members):
            return lax.psum_scatter(
                values.astype(bf16), "shard", scatter_dimension=0, tiled=True, axis_index_groups=members
            )

        def rows_pair(own, count):
            other = across(rows_of(own, (1 - zl) * block, block), 2)

            def send_rows(s_ref, mine, theirs, out):
                low, away_rows = s_ref[1], pl.multiple_of((1 - s_ref[0]) * unit, unit)
                rows_m = pl.ds(pl.multiple_of(low * block, block) + away_rows, unit)
                for i in range(count):
                    cols = slice(i * n_ff, (i + 1) * n_ff)
                    out[:, pl.ds(i * 2 * n_ff + pl.multiple_of(low * n_ff, n_ff), n_ff)] = mine[rows_m, cols]
                    out[:, pl.ds(i * 2 * n_ff + pl.multiple_of((1 - low) * n_ff, n_ff), n_ff)] = theirs[
                        pl.ds(away_rows, unit), cols
                    ]

            (sent,) = small_call(send_rows, [core, zl], [own, other], [array_of(unit, 2 * count * n_ff)])
            third = swap_core(sent)

            def join_rows(s_ref, mine, theirs, third_ref, *outs):
                me, low = s_ref[0], s_ref[1]
                start = pl.multiple_of(me * 2 * n_ff, n_ff)
                away = pl.multiple_of((1 - me) * 2 * n_ff, n_ff)
                here = pl.multiple_of(me * unit, unit)
                for i, out in enumerate(outs):
                    cols = slice(i * n_ff, (i + 1) * n_ff)
                    out[:, pl.ds(start + pl.multiple_of(low * n_ff, n_ff), n_ff)] = mine[
                        pl.ds(pl.multiple_of(low * block, block) + here, unit), cols
                    ].astype(f32)
                    out[:, pl.ds(start + pl.multiple_of((1 - low) * n_ff, n_ff), n_ff)] = theirs[
                        pl.ds(here, unit), cols
                    ].astype(f32)
                    out[:, pl.ds(away, 2 * n_ff)] = third_ref[:, i * 2 * n_ff : (i + 1) * 2 * n_ff].astype(f32)

            return small_call(join_rows, [core, zl], [own, other, third], [array_of(unit, 4 * n_ff, f32)] * count)

        def send_unit(s_ref, own, out):
            out[...] = own[pl.ds((1 - s_ref[0]) * unit, unit), :].astype(bf16)

        own_d = scatter(prod_d, groups)
        own_gu = scatter(prod_gu, groups)
        late_o = contract_rows(grad_attn, mixed).astype(bf16)
        own_o = scatter(after(late_o, own_d, own_gu), every)
        grad_mixed = after(grad_mixed, late_o)
        grad_qkv = attend_backward(kept, grad_mixed, seg_row, cosine, sine, 0, heads)
        hidden, grad_qkv = lax.optimization_barrier((hidden, grad_qkv))
        mlp = from_tokens(lambda where: contract_cols(hidden[where], weight_d))
        out_part = (after_attn + mlp).astype(bf16)
        output = join_tokens(out_part, swap_tp(out_part), half, nat, block)
        own_qkv = scatter(after(contract_rows(h_one, grad_qkv).astype(bf16), own_o), every)

        (grad_w_down,) = rows_pair(own_d, 1)
        grad_w_gate, grad_w_up = rows_pair(own_gu, 2)

        grad_h_one = to_slice(grad_qkv, lambda v: contract_cols(v, weight_qkv))

        normed_part = rows_of(normed_all, core * rows + half * part, part)
        inverse_part = rows_of(inverse_all, core * rows + half * part, part)
        grad_gain_a = jnp.sum(grad_h_one * normed_part, axis=0, keepdims=True)
        grad_x = (grad_after + norm_back(grad_h_one * gain_a, normed_part, inverse_part)).astype(bf16)
        grad_tokens = join_tokens(grad_x, swap_tp(grad_x), half, nat, block)

        own_qkv = after(own_qkv, output, grad_tokens, grad_w_gate, grad_w_up, grad_w_down)
        own_a = cat([own_qkv, own_o], 1)
        (sent_g,) = small_call(send_unit, [core], [own_a], [array_of(unit, 4 * n_attn)])
        other_a = swap_core(sent_g)

        def join_attn(s_ref, own, other, q, k, v, o):
            me = s_ref[0]
            mine = pl.ds(pl.multiple_of(me * unit, unit), unit)
            here, there = me * n_attn, (1 - me) * n_attn
            for start, load in (
                (here, lambda c: own[mine, c].astype(f32)),
                (there, lambda c: other[:, c].astype(f32)),
            ):
                start = pl.multiple_of(start, n_attn)
                for h in range(heads):
                    for i, ref in enumerate((q, k, v)):
                        ref[:, pl.ds(start + h * HD, HD)] = load(slice((3 * h + i) * HD, (3 * h + i + 1) * HD))
                o[:, pl.ds(start, n_attn)] = load(slice(3 * n_attn, 4 * n_attn))

        grad_w_query, grad_w_key, grad_w_value, grad_w_out = small_call(
            join_attn, [core], [own_a, other_a], [array_of(unit, 2 * n_attn, f32)] * 4
        )

        grad_gains = cat([grad_gain_a, grad_gain_m])
        grad_gains = grad_gains + swap_tp(grad_gains)
        for mask in [1 << bit for bit in range(shards.bit_length() - 2, 1, -1)] + [1, 2]:
            mid = grad_gains.shape[1] // 2
            first, second = grad_gains[:, :mid], grad_gains[:, mid:]
            low = (shard & mask) == 0
            grad_gains = jnp.where(low, first, second) + across(jnp.where(low, second, first), mask)
        first, second = grad_gains[:, :unit], grad_gains[:, unit:]
        grad_gains = jnp.where(core == 0, first, second) + swap_core(jnp.where(core == 0, second, first))

        return (
            output,
            grad_tokens,
            grad_gains[0],
            grad_w_query,
            grad_w_key,
            grad_w_value,
            grad_w_out,
            grad_gains[1],
            grad_w_gate,
            grad_w_up,
            grad_w_down,
        )

    return per_device


def solution(mesh):
    wide = P(("shard", "ctx"), None)
    flat = P(("shard", "ctx"))
    both = P(("shard", "ctx"), "tp")
    placed = (wide, P("shard", None), flat, both, both, both, both, flat, both, both, both, wide)
    return jax.shard_map(
        build(mesh.shape["shard"]),
        mesh=mesh,
        in_specs=placed,
        out_specs=(wide, wide, flat, both, both, both, both, flat, both, both, both),
        check_vma=False,
    )
```

```python
import math

import jax
import jax.numpy as jnp
from jax import lax
from jax.experimental import pallas as pl
from jax.experimental.pallas import tpu as pltpu
from jax.sharding import PartitionSpec as P

HD = 128
LENGTH = 1024


norm_eps = 1e-05
rope_base = 10000.0

bf16 = jnp.bfloat16
f32 = jnp.float32


def matmul(left, right):
    return jnp.dot(left, right, preferred_element_type=jnp.float32)


def contract_rows(left, right):
    return lax.dot_general(
        left, right, (((0,), (0,)), ((), ())), preferred_element_type=jnp.float32
    )


def contract_cols(left, right):
    return lax.dot_general(
        left, right, (((1,), (1,)), ((), ())), preferred_element_type=jnp.float32
    )


def norm_parts(values):
    inverse = lax.rsqrt(jnp.mean(values * values, axis=-1, keepdims=True) + norm_eps)
    return (values * inverse, inverse)


def norm_back(grad_scaled, normed, inverse):
    return inverse * (grad_scaled - normed * jnp.mean(grad_scaled * normed, axis=-1, keepdims=True))


def doc_positions(seg_row):
    places = jnp.arange(seg_row.shape[0], dtype=jnp.int32)
    starts_here = jnp.concatenate([jnp.ones((1,), dtype=jnp.bool_), seg_row[1:] != seg_row[:-1]])
    starts = lax.cummax(jnp.where(starts_here, places, jnp.zeros_like(places)), axis=0)
    return places - starts


def rope_tables(positions):
    half_dim = HD // 2
    freqs = rope_base ** (-(jnp.arange(half_dim, dtype=jnp.float32) * (2.0 / HD)))
    angles = positions.astype(jnp.float32)[:, None] * freqs[None, :]
    cosine, sine = jnp.cos(angles), jnp.sin(angles)
    return cat([cosine, cosine], 1), cat([-sine, sine], 1)


def cat(parts, axis=0):
    return jnp.concatenate(parts, axis=axis)


def rows_of(values, start, size):
    return lax.dynamic_slice_in_dim(values, start, size, 0)


def ordered(index, own, other, axis=0):
    return jnp.where(index == 0, cat([own, other], axis), cat([other, own], axis))


def after(values, *events):
    return lax.optimization_barrier((values, events))[0]


def small_call(body, scalars, arrays, outs):
    scalars = jnp.stack([jnp.asarray(v, jnp.int32) for v in scalars])
    return pl.pallas_call(
        body,
        grid_spec=pltpu.PrefetchScalarGridSpec(
            num_scalar_prefetch=1,
            grid=(1,),
            in_specs=[pl.BlockSpec(a.shape, lambda i, s: (0, 0)) for a in arrays],
            out_specs=[pl.BlockSpec(o.shape, lambda i, s: (0, 0)) for o in outs],
        ),
        out_shape=outs,
    )(scalars, *arrays)


def array_of(rows, cols, dtype=bf16):
    return jax.ShapeDtypeStruct((rows, cols), dtype)


def permute_cols(values, index, block):
    rows, width = values.shape
    step = min(rows, 128)
    count = width // block
    if block % 128:
        return cat([lax.dynamic_slice_in_dim(values, index[j] * block, block, 1) for j in range(count)], 1)

    def body(index_ref, in_ref, out_ref):
        for j in range(count):
            start = pl.multiple_of(index_ref[j] * block, block)
            out_ref[:, j * block : (j + 1) * block] = in_ref[:, pl.ds(start, block)]

    spec = pl.BlockSpec((step, width), lambda i, s: (i, 0))
    return pl.pallas_call(
        body,
        grid_spec=pltpu.PrefetchScalarGridSpec(
            num_scalar_prefetch=1, grid=(rows // step,), in_specs=[spec], out_specs=spec
        ),
        out_shape=jax.ShapeDtypeStruct(values.shape, values.dtype),
    )(index, values)


def join_tokens(own, other, half, index, block):
    rows, width = own.shape
    count = width // block
    if block % 128:
        return permute_cols(ordered(half, own, other), index, block)

    def body(index_ref, own_ref, other_ref, out_ref):
        here = pl.program_id(0) == index_ref[count]

        def move(ref):
            for j in range(count):
                start = pl.multiple_of(index_ref[j] * block, block)
                out_ref[:, j * block : (j + 1) * block] = ref[:, pl.ds(start, block)]

        pl.when(here)(lambda: move(own_ref))
        pl.when(jnp.logical_not(here))(lambda: move(other_ref))

    whole = pl.BlockSpec((rows, width), lambda i, s: (0, 0))
    return pl.pallas_call(
        body,
        grid_spec=pltpu.PrefetchScalarGridSpec(
            num_scalar_prefetch=1,
            grid=(2,),
            in_specs=[whole, whole],
            out_specs=pl.BlockSpec((rows, width), lambda i, s: (i, 0)),
        ),
        out_shape=jax.ShapeDtypeStruct((2 * rows, width), own.dtype),
    )(cat([index, half[None]]), own, other)


def score_parts(query, keys, rows_seg, cols_seg, diagonal):
    scores = contract_cols(query, keys) * (1.0 / math.sqrt(HD)) - math.log(LENGTH)
    allowed = rows_seg == cols_seg
    if diagonal:
        size = query.shape[0]
        places = lax.broadcasted_iota(jnp.int32, (size, size), 0)
        allowed = allowed & (places >= lax.broadcasted_iota(jnp.int32, (size, size), 1))
    return jax.nn.sigmoid(scores), allowed


def swap_halves(values):
    return pltpu.roll(values, HD // 2, 1)


def attend_forward(qkv, seg_row, cosine, sine, tile=256):
    length = seg_row.shape[0]
    heads = qkv.shape[1] // (3 * HD)
    tiles = length // tile

    def body(seg_ref, qkv_ref, cos_ref, sin_ref, seg_col, seg_line, out_ref, kept_ref, acc):
        cos_t, sin_t = cos_ref[...], sin_ref[...]
        for part in (0, 1):
            where = slice(part * HD, (part + 1) * HD)
            value = qkv_ref[:, where]
            kept_ref[:, where] = (value * cos_t + swap_halves(value) * sin_t).astype(bf16)
        kept_ref[:, 2 * HD :] = qkv_ref[:, 2 * HD :].astype(bf16)
        for i in range(tiles):
            rows = slice(i * tile, (i + 1) * tile)

            def step(j, diagonal, rows=rows):
                cols = slice(j * tile, (j + 1) * tile)
                sig, allowed = score_parts(
                    kept_ref[rows, :HD], kept_ref[cols, HD : 2 * HD],
                    seg_col[rows, :], seg_line[:, cols], diagonal,
                )
                weights = jnp.where(allowed, sig, 0.0).astype(bf16)
                return matmul(weights, kept_ref[cols, 2 * HD :])

            acc[...] = step(i, True)
            for j in range(i):

                @pl.when(seg_ref[(j + 1) * tile - 1] == seg_ref[i * tile])
                def _(j=j):
                    acc[...] += step(j, False)

            out_ref[rows, :] = acc[...].astype(bf16)

    full = pl.BlockSpec((length, HD), lambda h, s: (0, 0))
    return pl.pallas_call(
        body,
        grid_spec=pltpu.PrefetchScalarGridSpec(
            num_scalar_prefetch=1,
            grid=(heads,),
            in_specs=[
                pl.BlockSpec((length, 3 * HD), lambda h, s: (0, h)),
                full,
                full,
                pl.BlockSpec((length, 1), lambda h, s: (0, 0)),
                pl.BlockSpec((1, length), lambda h, s: (0, 0)),
            ],
            out_specs=[
                pl.BlockSpec((length, HD), lambda h, s: (0, h)),
                pl.BlockSpec((length, 3 * HD), lambda h, s: (0, h)),
            ],
            scratch_shapes=[pltpu.VMEM((tile, HD), f32)],
        ),
        out_shape=[array_of(length, heads * HD), array_of(length, 3 * heads * HD)],
    )(seg_row, qkv, cosine, sine, seg_row[:, None], seg_row[None, :])


def attend_backward(kept, grad_heads, seg_row, cosine, sine, first, heads, tile=256):
    length = seg_row.shape[0]
    tiles = length // tile
    scale = 1.0 / math.sqrt(HD)

    def body(seg_ref, kept_ref, do_ref, cos_ref, sin_ref, seg_col, seg_line, out_ref, dq, dk, dv):
        dk[...] = jnp.zeros_like(dk)
        dv[...] = jnp.zeros_like(dv)
        for i in range(tiles):
            rows = slice(i * tile, (i + 1) * tile)

            def step(j, diagonal, rows=rows):
                cols = slice(j * tile, (j + 1) * tile)
                query, grad = kept_ref[rows, :HD], do_ref[rows, :]
                keys = kept_ref[cols, HD : 2 * HD]
                sig, allowed = score_parts(query, keys, seg_col[rows, :], seg_line[:, cols], diagonal)
                weights = jnp.where(allowed, sig, 0.0).astype(bf16)
                dv[cols, :] += contract_rows(weights, grad)
                grad_probs = contract_cols(grad, kept_ref[cols, 2 * HD :])
                grad_scores = jnp.where(allowed, grad_probs * sig * (1.0 - sig), 0.0).astype(bf16)
                dk[cols, :] += contract_rows(grad_scores, query)
                return matmul(grad_scores, keys)

            dq[rows, :] = step(i, True)
            for j in range(i):

                @pl.when(seg_ref[(j + 1) * tile - 1] == seg_ref[i * tile])
                def _(j=j, rows=rows):
                    dq[rows, :] += step(j, False)

        cos_t, sin_t = cos_ref[...], sin_ref[...]
        for part, ref in ((0, dq), (1, dk)):
            grad = ref[...] * scale
            out_ref[:, part * HD : (part + 1) * HD] = (grad * cos_t - swap_halves(grad) * sin_t).astype(bf16)
        out_ref[:, 2 * HD :] = dv[...].astype(bf16)

    full = pl.BlockSpec((length, HD), lambda h, s: (0, 0))
    return pl.pallas_call(
        body,
        grid_spec=pltpu.PrefetchScalarGridSpec(
            num_scalar_prefetch=1,
            grid=(heads,),
            in_specs=[
                pl.BlockSpec((length, 3 * HD), lambda h, s: (0, first + h)),
                pl.BlockSpec((length, HD), lambda h, s: (0, first + h)),
                full,
                full,
                pl.BlockSpec((length, 1), lambda h, s: (0, 0)),
                pl.BlockSpec((1, length), lambda h, s: (0, 0)),
            ],
            out_specs=pl.BlockSpec((length, 3 * HD), lambda h, s: (0, h)),
            scratch_shapes=[pltpu.VMEM((length, HD), f32)] * 3,
        ),
        out_shape=array_of(length, 3 * heads * HD),
    )(seg_row, kept, grad_heads, cosine, sine, seg_row[:, None], seg_row[None, :])


def build(shards):
    line = [k << 1 for k in range(1, shards // 2)]

    groups = [[i for i in range(shards) if (i >> 1) & 1 == bit] for bit in (0, 1)]
    every = [[(i & ~3) | ((i & 1) << 1) | ((i >> 1) & 1) for i in range(shards)]]

    def across(values, mask):
        return lax.ppermute(values, "shard", [(i, i ^ mask) for i in range(shards)])

    def swap_core(values):
        return lax.ppermute(values, "ctx", [(0, 1), (1, 0)])

    def swap_tp(values):
        return lax.ppermute(values, "tp", [(0, 1), (1, 0)])

    def per_device(
        tokens,
        segments,
        gain_attn,
        w_query,
        w_key,
        w_value,
        w_out,
        gain_mlp,
        w_gate,
        w_up,
        w_down,
        cotangent,
    ):
        shard = lax.axis_index("shard").astype(jnp.int32)
        core = lax.axis_index("ctx").astype(jnp.int32)
        half = lax.axis_index("tp").astype(jnp.int32)
        y, zl = shard & 1, (shard >> 1) & 1
        rows, width = tokens.shape
        part = rows // 2
        block = width // shards
        unit = block // 2
        n_attn = w_query.shape[1] // 2
        n_ff = w_gate.shape[1] // 4
        heads = n_attn // HD
        half_s = shards // 2
        pad = 16

        def place_of(number):
            return (number & ~3) | ((number & 1) << 1) | ((number >> 1) & 1)

        rel = place_of(jnp.arange(shards, dtype=jnp.int32))
        nat = rel

        attn_w = [w_query, w_key, w_value, w_out]
        ff_w = [w_gate, w_up, w_down]

        def send_attn(s_ref, q, k, v, o, out):
            start = pl.multiple_of((1 - s_ref[0]) * n_attn, n_attn)
            for h in range(heads):
                for i, ref in enumerate((q, k, v)):
                    out[:, (3 * h + i) * HD : (3 * h + i + 1) * HD] = ref[:, pl.ds(start + h * HD, HD)]
            out[:, 3 * n_attn :] = o[:, pl.ds(start, n_attn)]

        (sent_a,) = small_call(send_attn, [core], attn_w, [array_of(unit, 4 * n_attn)])
        other_a = swap_core(sent_a)
        gains = jnp.stack([gain_attn, gain_mlp])
        other_gains = swap_core(gains)

        def keep_attn(s_ref, q, k, v, o, other, own_g, other_g, out_qkv, out_o):
            me = s_ref[0]
            start = pl.multiple_of(me * n_attn, n_attn)
            mine, theirs = pl.ds(me * unit, unit), pl.ds((1 - me) * unit, unit)
            for h in range(heads):
                for i, ref in enumerate((q, k, v)):
                    where = slice((3 * h + i) * HD, (3 * h + i + 1) * HD)
                    out_qkv[mine, where] = ref[:, pl.ds(start + h * HD, HD)]
            out_o[mine, :] = o[:, pl.ds(start, n_attn)]
            out_qkv[theirs, :] = other[:, : 3 * n_attn]
            out_o[theirs, :] = other[:, 3 * n_attn :]
            first, second = own_g[...], other_g[...]
            low = jnp.where(me == 0, first, second)
            high = jnp.where(me == 0, second, first)
            line_g = cat([low, high, jnp.zeros((2, n_attn - block), bf16)], 1)
            out_o[block:, :] = cat([line_g, jnp.zeros((pad - 2, n_attn), bf16)])

        block_qkv, block_o = small_call(
            keep_attn, [core], attn_w + [other_a, gains, other_gains],
            [array_of(block, 3 * n_attn), array_of(block + pad, n_attn)],
        )

        def shard_at(i):
            return shard ^ (((i % half_s) << 1) | (i // half_s))

        weight_qkv = lax.all_gather(block_qkv, "shard", axis=0, tiled=True, axis_index_groups=every)
        near_o = cat([block_o] + [across(block_o, mask) for mask in line])
        parts_o = cat([near_o, across(near_o, 1)]).reshape(shards, block + pad, n_attn)
        weight_o = jnp.zeros((width, n_attn), bf16)
        for i in range(shards):
            weight_o = lax.dynamic_update_slice_in_dim(
                weight_o, parts_o[i, :block], place_of(shard_at(i)) * block, 0
            )
        gain_rows = parts_o[:, block : block + 2, :block]
        away_bits = place_of(jnp.arange(shards, dtype=jnp.int32)) ^ shard
        gain_rows = gain_rows[(away_bits >> 1) + half_s * (away_bits & 1)]
        gains_rel = jnp.transpose(gain_rows, (1, 0, 2)).reshape(2, width).astype(f32)
        gain_a, gain_m = gains_rel[0:1], gains_rel[1:2]

        def send_ff(s_ref, g, u, d, out):
            start = pl.multiple_of((1 - s_ref[0]) * 2 * n_ff, n_ff)
            for i, ref in enumerate((g, u, d)):
                out[:, i * 2 * n_ff : (i + 1) * 2 * n_ff] = ref[:, pl.ds(start, 2 * n_ff)]

        (sent_f,) = small_call(send_ff, [core], ff_w, [array_of(unit, 6 * n_ff)])
        other_f = swap_core(sent_f)

        def keep_ff(s_ref, g, u, d, other, keep, send):
            me, low = s_ref[0], s_ref[1]
            mine, theirs = pl.ds(pl.multiple_of(me * unit, unit), unit), pl.ds(pl.multiple_of((1 - me) * unit, unit), unit)
            for out, which in ((keep, low), (send, 1 - low)):
                start = pl.multiple_of(which * n_ff, n_ff)
                for i, ref in enumerate((g, u, d)):
                    cols = slice(i * n_ff, (i + 1) * n_ff)
                    out[mine, cols] = ref[:, pl.ds(pl.multiple_of(me * 2 * n_ff, n_ff) + start, n_ff)]
                    out[theirs, cols] = other[:, pl.ds(i * 2 * n_ff + start, n_ff)]

        keep_f, send_f = small_call(keep_ff, [core, zl], ff_w + [other_f], [array_of(block, 3 * n_ff)] * 2)
        recv_f = across(send_f, 2)

        def pair_rows(s_ref, own, other, out):
            low = s_ref[0]
            out[pl.ds(pl.multiple_of(low * block, block), block), :] = own[...]
            out[pl.ds(pl.multiple_of((1 - low) * block, block), block), :] = other[...]

        (pair_f,) = small_call(pair_rows, [zl], [keep_f, recv_f], [array_of(2 * block, 3 * n_ff)])

        seg_row = segments[0]
        cosine, sine = rope_tables(doc_positions(seg_row))
        x_own = permute_cols(tokens, rel, block)
        x_both = ordered(core, x_own, swap_core(x_own))
        normed_all, inverse_all = norm_parts(x_both.astype(f32))
        h_one = (normed_all * gain_a).astype(bf16)
        pair_f = after(pair_f, weight_qkv, weight_o, h_one, cosine, sine)
        weight_f = lax.all_gather(pair_f, "shard", axis=0, tiled=True, axis_index_groups=groups)
        weight_g, weight_u, weight_d = [weight_f[:, i * n_ff : (i + 1) * n_ff] for i in range(3)]
        qkv = matmul(h_one, weight_qkv)
        mixed, kept = attend_forward(qkv, seg_row, cosine, sine)

        def to_slice(operand, project):
            away = project(rows_of(operand, (1 - core) * rows, rows)).astype(bf16)
            here = rows_of(operand, core * rows, rows)
            away = swap_core(away)
            other = project(rows_of(here, (1 - half) * part, part)) + rows_of(
                away, (1 - half) * part, part
            ).astype(f32)
            other = swap_tp(other.astype(bf16))
            own = project(rows_of(here, half * part, part)) + rows_of(
                away, half * part, part
            ).astype(f32)
            return own + other.astype(f32)

        x_part = rows_of(x_own, half * part, part).astype(f32)
        after_attn = x_part + to_slice(mixed, lambda v: contract_cols(v, weight_o))
        normed_two, inverse_two = norm_parts(after_attn)
        h_part = (normed_two * gain_m).astype(bf16)

        by_tp, by_zl = swap_tp(h_part), across(h_part, 2)
        mid = part // 2
        near = cat([h_part, by_tp, by_zl])
        far_near = swap_core(near)
        both = cat([across(by_tp[:mid], 2), swap_tp(by_zl[mid:])])
        h_two = cat([near, both, far_near, swap_core(both)])

        dy_rel = permute_cols(cotangent, rel, block)
        dy_ff = cat([rows_of(dy_rel, half * part, part), rows_of(dy_rel, (1 - half) * part, part)])
        dy_zl = across(after(dy_ff[:part], both), 2)
        near = cat([dy_ff, dy_zl, swap_tp(dy_zl)])
        grad_out = cat([near, swap_core(near)])

        gate_pre = matmul(h_two, weight_g)
        up_pre = matmul(h_two, weight_u)
        gate_sig = jax.nn.sigmoid(gate_pre)
        gate_act = gate_pre * gate_sig
        hidden = (gate_act * up_pre).astype(bf16)

        def from_tokens(project, gate=None):
            count = 4 * part
            away = swap_core(project(slice(count, 2 * count)).astype(bf16))
            total = project(slice(0, count)) + away.astype(f32)
            mid = width // 2
            low, high = total[:, :mid], total[:, mid:]

            def pick(values, i):
                return values[i * part : (i + 1) * part]

            low_sent = cat([pick(low, 1), pick(low, 3)]).astype(bf16)
            high_sent = cat([pick(high, 2), pick(high, 3)]).astype(bf16)
            if gate is not None:
                low_sent, high_sent = after((low_sent, high_sent), gate)
            low_tp, high_zl = swap_tp(low_sent), across(high_sent, 2)
            first = (low_tp, high_zl)
            low_tp, high_zl = low_tp.astype(f32), high_zl.astype(f32)
            low_zl = across((pick(low, 2) + pick(low_tp, 1)).astype(bf16), 2)
            high_tp = swap_tp((pick(high, 1) + pick(high_zl, 1)).astype(bf16))
            second = (low_zl, high_tp)
            low_sum = pick(low, 0) + pick(low_tp, 0) + low_zl.astype(f32)
            high_sum = pick(high, 0) + pick(high_zl, 0) + high_tp.astype(f32)
            return (low_sent, first, second), cat([low_sum, high_sum], 1)

        grad_hidden = matmul(grad_out, weight_d)
        grad_gate = (grad_hidden * up_pre * gate_sig * (1.0 + gate_pre * (1.0 - gate_sig))).astype(bf16)
        grad_up = (grad_hidden * gate_act).astype(bf16)
        prod_d = contract_rows(grad_out, hidden).astype(bf16)
        late_hidden = after(hidden, prod_d)
        (sent_m, first_m, second_m), mlp = from_tokens(lambda where: contract_cols(late_hidden[where], weight_d))
        grad_gate, grad_up = after((grad_gate, grad_up), sent_m)
        prod_gu = cat(
            [contract_rows(h_two, grad_gate).astype(bf16), contract_rows(h_two, grad_up).astype(bf16)], 1
        )
        late_gate, late_up = after((grad_gate, grad_up), prod_gu, first_m)
        _, grad_h_two = from_tokens(
            lambda where: contract_cols(late_gate[where], weight_g)
            + contract_cols(late_up[where], weight_u),
            second_m,
        )
        out_part = (after_attn + mlp).astype(bf16)
        output = join_tokens(out_part, swap_tp(out_part), half, nat, block)

        grad_gain_m = jnp.sum(grad_h_two * normed_two, axis=0, keepdims=True)
        dy_part = rows_of(dy_rel, half * part, part).astype(f32)
        grad_after = dy_part + norm_back(grad_h_two * gain_m, normed_two, inverse_two)

        grad_part = grad_after.astype(bf16)
        grad_half = ordered(half, grad_part, swap_tp(grad_part))
        grad_attn = ordered(core, grad_half, swap_core(grad_half))
        grad_mixed = matmul(grad_attn, weight_o).astype(bf16)

        def scatter(values, members):
            return lax.psum_scatter(
                values.astype(bf16), "shard", scatter_dimension=0, tiled=True, axis_index_groups=members
            )

        def rows_pair(own, count):
            other = across(rows_of(own, (1 - zl) * block, block), 2)

            def send_rows(s_ref, mine, theirs, out):
                low, away_rows = s_ref[1], pl.multiple_of((1 - s_ref[0]) * unit, unit)
                rows_m = pl.ds(pl.multiple_of(low * block, block) + away_rows, unit)
                for i in range(count):
                    cols = slice(i * n_ff, (i + 1) * n_ff)
                    out[:, pl.ds(i * 2 * n_ff + pl.multiple_of(low * n_ff, n_ff), n_ff)] = mine[rows_m, cols]
                    out[:, pl.ds(i * 2 * n_ff + pl.multiple_of((1 - low) * n_ff, n_ff), n_ff)] = theirs[
                        pl.ds(away_rows, unit), cols
                    ]

            (sent,) = small_call(send_rows, [core, zl], [own, other], [array_of(unit, 2 * count * n_ff)])
            third = swap_core(sent)

            def join_rows(s_ref, mine, theirs, third_ref, *outs):
                me, low = s_ref[0], s_ref[1]
                start = pl.multiple_of(me * 2 * n_ff, n_ff)
                away = pl.multiple_of((1 - me) * 2 * n_ff, n_ff)
                here = pl.multiple_of(me * unit, unit)
                for i, out in enumerate(outs):
                    cols = slice(i * n_ff, (i + 1) * n_ff)
                    out[:, pl.ds(start + pl.multiple_of(low * n_ff, n_ff), n_ff)] = mine[
                        pl.ds(pl.multiple_of(low * block, block) + here, unit), cols
                    ].astype(f32)
                    out[:, pl.ds(start + pl.multiple_of((1 - low) * n_ff, n_ff), n_ff)] = theirs[
                        pl.ds(here, unit), cols
                    ].astype(f32)
                    out[:, pl.ds(away, 2 * n_ff)] = third_ref[:, i * 2 * n_ff : (i + 1) * 2 * n_ff].astype(f32)

            return small_call(join_rows, [core, zl], [own, other, third], [array_of(unit, 4 * n_ff, f32)] * count)

        def send_unit(s_ref, own, out):
            out[...] = own[pl.ds((1 - s_ref[0]) * unit, unit), :].astype(bf16)

        own_d = scatter(prod_d, groups)
        own_gu = scatter(prod_gu, groups)
        grad_qkv = attend_backward(kept, grad_mixed, seg_row, cosine, sine, 0, heads)
        own_a = scatter(
            cat([contract_rows(h_one, grad_qkv).astype(bf16), contract_rows(grad_attn, mixed).astype(bf16)], 1), every
        )

        (grad_w_down,) = rows_pair(own_d, 1)
        grad_w_gate, grad_w_up = rows_pair(own_gu, 2)

        grad_h_one = to_slice(grad_qkv, lambda v: contract_cols(v, weight_qkv))

        normed_part = rows_of(normed_all, core * rows + half * part, part)
        inverse_part = rows_of(inverse_all, core * rows + half * part, part)
        grad_gain_a = jnp.sum(grad_h_one * normed_part, axis=0, keepdims=True)
        grad_x = (grad_after + norm_back(grad_h_one * gain_a, normed_part, inverse_part)).astype(bf16)
        grad_tokens = join_tokens(grad_x, swap_tp(grad_x), half, nat, block)

        own_a = after(own_a, output, grad_tokens, grad_w_gate, grad_w_up, grad_w_down)
        (sent_g,) = small_call(send_unit, [core], [own_a], [array_of(unit, 4 * n_attn)])
        other_a = swap_core(sent_g)

        def join_attn(s_ref, own, other, q, k, v, o):
            me = s_ref[0]
            mine = pl.ds(pl.multiple_of(me * unit, unit), unit)
            here, there = me * n_attn, (1 - me) * n_attn
            for start, load in (
                (here, lambda c: own[mine, c].astype(f32)),
                (there, lambda c: other[:, c].astype(f32)),
            ):
                start = pl.multiple_of(start, n_attn)
                for h in range(heads):
                    for i, ref in enumerate((q, k, v)):
                        ref[:, pl.ds(start + h * HD, HD)] = load(slice((3 * h + i) * HD, (3 * h + i + 1) * HD))
                o[:, pl.ds(start, n_attn)] = load(slice(3 * n_attn, 4 * n_attn))

        grad_w_query, grad_w_key, grad_w_value, grad_w_out = small_call(
            join_attn, [core], [own_a, other_a], [array_of(unit, 2 * n_attn, f32)] * 4
        )

        grad_gains = cat([grad_gain_a, grad_gain_m])
        grad_gains = grad_gains + swap_tp(grad_gains)
        for mask in [1 << bit for bit in range(shards.bit_length() - 2, 1, -1)] + [1, 2]:
            mid = grad_gains.shape[1] // 2
            first, second = grad_gains[:, :mid], grad_gains[:, mid:]
            low = (shard & mask) == 0
            grad_gains = jnp.where(low, first, second) + across(jnp.where(low, second, first), mask)
        first, second = grad_gains[:, :unit], grad_gains[:, unit:]
        grad_gains = jnp.where(core == 0, first, second) + swap_core(jnp.where(core == 0, second, first))

        return (
            output,
            grad_tokens,
            grad_gains[0],
            grad_w_query,
            grad_w_key,
            grad_w_value,
            grad_w_out,
            grad_gains[1],
            grad_w_gate,
            grad_w_up,
            grad_w_down,
        )

    return per_device


def solution(mesh):
    wide = P(("shard", "ctx"), None)
    flat = P(("shard", "ctx"))
    both = P(("shard", "ctx"), "tp")
    placed = (wide, P("shard", None), flat, both, both, both, both, flat, both, both, both, wide)
    return jax.shard_map(
        build(mesh.shape["shard"]),
        mesh=mesh,
        in_specs=placed,
        out_specs=(wide, wide, flat, both, both, both, both, flat, both, both, both),
        check_vma=False,
    )
```

```python
import math

import jax
import jax.numpy as jnp
from jax import lax
from jax.experimental import pallas as pl
from jax.experimental.pallas import tpu as pltpu
from jax.sharding import PartitionSpec as P

HD = 128
LENGTH = 1024


norm_eps = 1e-05
rope_base = 10000.0

bf16 = jnp.bfloat16
f32 = jnp.float32


def matmul(left, right):
    return jnp.dot(left, right, preferred_element_type=jnp.float32)


def contract_rows(left, right):
    return lax.dot_general(
        left, right, (((0,), (0,)), ((), ())), preferred_element_type=jnp.float32
    )


def contract_cols(left, right):
    return lax.dot_general(
        left, right, (((1,), (1,)), ((), ())), preferred_element_type=jnp.float32
    )


def norm_parts(values):
    inverse = lax.rsqrt(jnp.mean(values * values, axis=-1, keepdims=True) + norm_eps)
    return (values * inverse, inverse)


def norm_back(grad_scaled, normed, inverse):
    return inverse * (grad_scaled - normed * jnp.mean(grad_scaled * normed, axis=-1, keepdims=True))


def doc_positions(seg_row):
    places = jnp.arange(seg_row.shape[0], dtype=jnp.int32)
    starts_here = jnp.concatenate([jnp.ones((1,), dtype=jnp.bool_), seg_row[1:] != seg_row[:-1]])
    starts = lax.cummax(jnp.where(starts_here, places, jnp.zeros_like(places)), axis=0)
    return places - starts


def rope_tables(positions):
    half_dim = HD // 2
    freqs = rope_base ** (-(jnp.arange(half_dim, dtype=jnp.float32) * (2.0 / HD)))
    angles = positions.astype(jnp.float32)[:, None] * freqs[None, :]
    cosine, sine = jnp.cos(angles), jnp.sin(angles)
    return cat([cosine, cosine], 1), cat([-sine, sine], 1)


def cat(parts, axis=0):
    return jnp.concatenate(parts, axis=axis)


def rows_of(values, start, size):
    return lax.dynamic_slice_in_dim(values, start, size, 0)


def ordered(index, own, other, axis=0):
    return jnp.where(index == 0, cat([own, other], axis), cat([other, own], axis))


def after(values, *events):
    return lax.optimization_barrier((values, events))[0]


def small_call(body, scalars, arrays, outs):
    scalars = jnp.stack([jnp.asarray(v, jnp.int32) for v in scalars])
    return pl.pallas_call(
        body,
        grid_spec=pltpu.PrefetchScalarGridSpec(
            num_scalar_prefetch=1,
            grid=(1,),
            in_specs=[pl.BlockSpec(a.shape, lambda i, s: (0, 0)) for a in arrays],
            out_specs=[pl.BlockSpec(o.shape, lambda i, s: (0, 0)) for o in outs],
        ),
        out_shape=outs,
    )(scalars, *arrays)


def array_of(rows, cols, dtype=bf16):
    return jax.ShapeDtypeStruct((rows, cols), dtype)


def permute_cols(values, index, block):
    rows, width = values.shape
    step = min(rows, 128)
    count = width // block
    if block % 128:
        return cat([lax.dynamic_slice_in_dim(values, index[j] * block, block, 1) for j in range(count)], 1)

    def body(index_ref, in_ref, out_ref):
        for j in range(count):
            start = pl.multiple_of(index_ref[j] * block, block)
            out_ref[:, j * block : (j + 1) * block] = in_ref[:, pl.ds(start, block)]

    spec = pl.BlockSpec((step, width), lambda i, s: (i, 0))
    return pl.pallas_call(
        body,
        grid_spec=pltpu.PrefetchScalarGridSpec(
            num_scalar_prefetch=1, grid=(rows // step,), in_specs=[spec], out_specs=spec
        ),
        out_shape=jax.ShapeDtypeStruct(values.shape, values.dtype),
    )(index, values)


def join_tokens(own, other, half, index, block):
    rows, width = own.shape
    count = width // block
    if block % 128:
        return permute_cols(ordered(half, own, other), index, block)

    def body(index_ref, own_ref, other_ref, out_ref):
        here = pl.program_id(0) == index_ref[count]

        def move(ref):
            for j in range(count):
                start = pl.multiple_of(index_ref[j] * block, block)
                out_ref[:, j * block : (j + 1) * block] = ref[:, pl.ds(start, block)]

        pl.when(here)(lambda: move(own_ref))
        pl.when(jnp.logical_not(here))(lambda: move(other_ref))

    whole = pl.BlockSpec((rows, width), lambda i, s: (0, 0))
    return pl.pallas_call(
        body,
        grid_spec=pltpu.PrefetchScalarGridSpec(
            num_scalar_prefetch=1,
            grid=(2,),
            in_specs=[whole, whole],
            out_specs=pl.BlockSpec((rows, width), lambda i, s: (i, 0)),
        ),
        out_shape=jax.ShapeDtypeStruct((2 * rows, width), own.dtype),
    )(cat([index, half[None]]), own, other)


def score_parts(query, keys, rows_seg, cols_seg, diagonal):
    scores = contract_cols(query, keys) * (1.0 / math.sqrt(HD)) - math.log(LENGTH)
    allowed = rows_seg == cols_seg
    if diagonal:
        size = query.shape[0]
        places = lax.broadcasted_iota(jnp.int32, (size, size), 0)
        allowed = allowed & (places >= lax.broadcasted_iota(jnp.int32, (size, size), 1))
    return jax.nn.sigmoid(scores), allowed


def swap_halves(values):
    return pltpu.roll(values, HD // 2, 1)


def attend_forward(qkv, seg_row, cosine, sine, tile=256):
    length = seg_row.shape[0]
    heads = qkv.shape[1] // (3 * HD)
    tiles = length // tile

    def body(seg_ref, qkv_ref, cos_ref, sin_ref, seg_col, seg_line, out_ref, kept_ref, acc):
        cos_t, sin_t = cos_ref[...], sin_ref[...]
        for part in (0, 1):
            where = slice(part * HD, (part + 1) * HD)
            value = qkv_ref[:, where]
            kept_ref[:, where] = (value * cos_t + swap_halves(value) * sin_t).astype(bf16)
        kept_ref[:, 2 * HD :] = qkv_ref[:, 2 * HD :].astype(bf16)
        for i in range(tiles):
            rows = slice(i * tile, (i + 1) * tile)

            def step(j, diagonal, rows=rows):
                cols = slice(j * tile, (j + 1) * tile)
                sig, allowed = score_parts(
                    kept_ref[rows, :HD], kept_ref[cols, HD : 2 * HD],
                    seg_col[rows, :], seg_line[:, cols], diagonal,
                )
                weights = jnp.where(allowed, sig, 0.0).astype(bf16)
                return matmul(weights, kept_ref[cols, 2 * HD :])

            acc[...] = step(i, True)
            for j in range(i):

                @pl.when(seg_ref[(j + 1) * tile - 1] == seg_ref[i * tile])
                def _(j=j):
                    acc[...] += step(j, False)

            out_ref[rows, :] = acc[...].astype(bf16)

    full = pl.BlockSpec((length, HD), lambda h, s: (0, 0))
    return pl.pallas_call(
        body,
        grid_spec=pltpu.PrefetchScalarGridSpec(
            num_scalar_prefetch=1,
            grid=(heads,),
            in_specs=[
                pl.BlockSpec((length, 3 * HD), lambda h, s: (0, h)),
                full,
                full,
                pl.BlockSpec((length, 1), lambda h, s: (0, 0)),
                pl.BlockSpec((1, length), lambda h, s: (0, 0)),
            ],
            out_specs=[
                pl.BlockSpec((length, HD), lambda h, s: (0, h)),
                pl.BlockSpec((length, 3 * HD), lambda h, s: (0, h)),
            ],
            scratch_shapes=[pltpu.VMEM((tile, HD), f32)],
        ),
        out_shape=[array_of(length, heads * HD), array_of(length, 3 * heads * HD)],
    )(seg_row, qkv, cosine, sine, seg_row[:, None], seg_row[None, :])


def attend_backward(kept, grad_heads, seg_row, cosine, sine, first, heads, tile=256):
    length = seg_row.shape[0]
    tiles = length // tile
    scale = 1.0 / math.sqrt(HD)

    def body(seg_ref, kept_ref, do_ref, cos_ref, sin_ref, seg_col, seg_line, out_ref, dq, dk, dv):
        dk[...] = jnp.zeros_like(dk)
        dv[...] = jnp.zeros_like(dv)
        for i in range(tiles):
            rows = slice(i * tile, (i + 1) * tile)

            def step(j, diagonal, rows=rows):
                cols = slice(j * tile, (j + 1) * tile)
                query, grad = kept_ref[rows, :HD], do_ref[rows, :]
                keys = kept_ref[cols, HD : 2 * HD]
                sig, allowed = score_parts(query, keys, seg_col[rows, :], seg_line[:, cols], diagonal)
                weights = jnp.where(allowed, sig, 0.0).astype(bf16)
                dv[cols, :] += contract_rows(weights, grad)
                grad_probs = contract_cols(grad, kept_ref[cols, 2 * HD :])
                grad_scores = jnp.where(allowed, grad_probs * sig * (1.0 - sig), 0.0).astype(bf16)
                dk[cols, :] += contract_rows(grad_scores, query)
                return matmul(grad_scores, keys)

            dq[rows, :] = step(i, True)
            for j in range(i):

                @pl.when(seg_ref[(j + 1) * tile - 1] == seg_ref[i * tile])
                def _(j=j, rows=rows):
                    dq[rows, :] += step(j, False)

        cos_t, sin_t = cos_ref[...], sin_ref[...]
        for part, ref in ((0, dq), (1, dk)):
            grad = ref[...] * scale
            out_ref[:, part * HD : (part + 1) * HD] = (grad * cos_t - swap_halves(grad) * sin_t).astype(bf16)
        out_ref[:, 2 * HD :] = dv[...].astype(bf16)

    full = pl.BlockSpec((length, HD), lambda h, s: (0, 0))
    return pl.pallas_call(
        body,
        grid_spec=pltpu.PrefetchScalarGridSpec(
            num_scalar_prefetch=1,
            grid=(heads,),
            in_specs=[
                pl.BlockSpec((length, 3 * HD), lambda h, s: (0, first + h)),
                pl.BlockSpec((length, HD), lambda h, s: (0, first + h)),
                full,
                full,
                pl.BlockSpec((length, 1), lambda h, s: (0, 0)),
                pl.BlockSpec((1, length), lambda h, s: (0, 0)),
            ],
            out_specs=pl.BlockSpec((length, 3 * HD), lambda h, s: (0, h)),
            scratch_shapes=[pltpu.VMEM((length, HD), f32)] * 3,
        ),
        out_shape=array_of(length, 3 * heads * HD),
    )(seg_row, kept, grad_heads, cosine, sine, seg_row[:, None], seg_row[None, :])


def build(shards):
    line = [k << 1 for k in range(1, shards // 2)]

    groups = [[i for i in range(shards) if (i >> 1) & 1 == bit] for bit in (0, 1)]
    every = [[(i & ~3) | ((i & 1) << 1) | ((i >> 1) & 1) for i in range(shards)]]

    def across(values, mask):
        return lax.ppermute(values, "shard", [(i, i ^ mask) for i in range(shards)])

    def swap_core(values):
        return lax.ppermute(values, "ctx", [(0, 1), (1, 0)])

    def swap_tp(values):
        return lax.ppermute(values, "tp", [(0, 1), (1, 0)])

    def per_device(
        tokens,
        segments,
        gain_attn,
        w_query,
        w_key,
        w_value,
        w_out,
        gain_mlp,
        w_gate,
        w_up,
        w_down,
        cotangent,
    ):
        shard = lax.axis_index("shard").astype(jnp.int32)
        core = lax.axis_index("ctx").astype(jnp.int32)
        half = lax.axis_index("tp").astype(jnp.int32)
        y, zl = shard & 1, (shard >> 1) & 1
        rows, width = tokens.shape
        part = rows // 2
        block = width // shards
        unit = block // 2
        n_attn = w_query.shape[1] // 2
        n_ff = w_gate.shape[1] // 4
        heads = n_attn // HD
        half_s = shards // 2
        pad = 16

        def place_of(number):
            return (number & ~3) | ((number & 1) << 1) | ((number >> 1) & 1)

        rel = place_of(jnp.arange(shards, dtype=jnp.int32))
        nat = rel

        attn_w = [w_query, w_key, w_value, w_out]
        ff_w = [w_gate, w_up, w_down]

        def send_attn(s_ref, q, k, v, o, out):
            start = pl.multiple_of((1 - s_ref[0]) * n_attn, n_attn)
            for h in range(heads):
                for i, ref in enumerate((q, k, v)):
                    out[:, (3 * h + i) * HD : (3 * h + i + 1) * HD] = ref[:, pl.ds(start + h * HD, HD)]
            out[:, 3 * n_attn :] = o[:, pl.ds(start, n_attn)]

        (sent_a,) = small_call(send_attn, [core], attn_w, [array_of(unit, 4 * n_attn)])
        other_a = swap_core(sent_a)
        gains = jnp.stack([gain_attn, gain_mlp])
        other_gains = swap_core(gains)

        def keep_attn(s_ref, q, k, v, o, other, own_g, other_g, out_qkv, out_o):
            me = s_ref[0]
            start = pl.multiple_of(me * n_attn, n_attn)
            mine, theirs = pl.ds(me * unit, unit), pl.ds((1 - me) * unit, unit)
            for h in range(heads):
                for i, ref in enumerate((q, k, v)):
                    where = slice((3 * h + i) * HD, (3 * h + i + 1) * HD)
                    out_qkv[mine, where] = ref[:, pl.ds(start + h * HD, HD)]
            out_o[mine, :] = o[:, pl.ds(start, n_attn)]
            out_qkv[theirs, :] = other[:, : 3 * n_attn]
            out_o[theirs, :] = other[:, 3 * n_attn :]
            first, second = own_g[...], other_g[...]
            low = jnp.where(me == 0, first, second)
            high = jnp.where(me == 0, second, first)
            line_g = cat([low, high, jnp.zeros((2, n_attn - block), bf16)], 1)
            out_o[block:, :] = cat([line_g, jnp.zeros((pad - 2, n_attn), bf16)])

        block_qkv, block_o = small_call(
            keep_attn, [core], attn_w + [other_a, gains, other_gains],
            [array_of(block, 3 * n_attn), array_of(block + pad, n_attn)],
        )

        def shard_at(i):
            return shard ^ (((i % half_s) << 1) | (i // half_s))

        weight_qkv = lax.all_gather(block_qkv, "shard", axis=0, tiled=True, axis_index_groups=every)
        near_o = cat([block_o] + [across(block_o, mask) for mask in line])
        parts_o = cat([near_o, across(near_o, 1)]).reshape(shards, block + pad, n_attn)
        weight_o = jnp.zeros((width, n_attn), bf16)
        for i in range(shards):
            weight_o = lax.dynamic_update_slice_in_dim(
                weight_o, parts_o[i, :block], place_of(shard_at(i)) * block, 0
            )
        gain_rows = parts_o[:, block : block + 2, :block]
        away_bits = place_of(jnp.arange(shards, dtype=jnp.int32)) ^ shard
        gain_rows = gain_rows[(away_bits >> 1) + half_s * (away_bits & 1)]
        gains_rel = jnp.transpose(gain_rows, (1, 0, 2)).reshape(2, width).astype(f32)
        gain_a, gain_m = gains_rel[0:1], gains_rel[1:2]

        def send_ff(s_ref, g, u, d, out):
            start = pl.multiple_of((1 - s_ref[0]) * 2 * n_ff, n_ff)
            for i, ref in enumerate((g, u, d)):
                out[:, i * 2 * n_ff : (i + 1) * 2 * n_ff] = ref[:, pl.ds(start, 2 * n_ff)]

        (sent_f,) = small_call(send_ff, [core], ff_w, [array_of(unit, 6 * n_ff)])
        other_f = swap_core(sent_f)

        def keep_ff(s_ref, g, u, d, other, keep, send):
            me, low = s_ref[0], s_ref[1]
            mine, theirs = pl.ds(pl.multiple_of(me * unit, unit), unit), pl.ds(pl.multiple_of((1 - me) * unit, unit), unit)
            for out, which in ((keep, low), (send, 1 - low)):
                start = pl.multiple_of(which * n_ff, n_ff)
                for i, ref in enumerate((g, u, d)):
                    cols = slice(i * n_ff, (i + 1) * n_ff)
                    out[mine, cols] = ref[:, pl.ds(pl.multiple_of(me * 2 * n_ff, n_ff) + start, n_ff)]
                    out[theirs, cols] = other[:, pl.ds(i * 2 * n_ff + start, n_ff)]

        keep_f, send_f = small_call(keep_ff, [core, zl], ff_w + [other_f], [array_of(block, 3 * n_ff)] * 2)
        recv_f = across(send_f, 2)

        def pair_rows(s_ref, own, other, out):
            low = s_ref[0]
            out[pl.ds(pl.multiple_of(low * block, block), block), :] = own[...]
            out[pl.ds(pl.multiple_of((1 - low) * block, block), block), :] = other[...]

        (pair_f,) = small_call(pair_rows, [zl], [keep_f, recv_f], [array_of(2 * block, 3 * n_ff)])

        seg_row = segments[0]
        cosine, sine = rope_tables(doc_positions(seg_row))
        x_own = permute_cols(tokens, rel, block)
        x_both = ordered(core, x_own, swap_core(x_own))
        normed_all, inverse_all = norm_parts(x_both.astype(f32))
        h_one = (normed_all * gain_a).astype(bf16)
        pair_f = after(pair_f, weight_qkv, weight_o, h_one, cosine, sine)
        weight_f = lax.all_gather(pair_f, "shard", axis=0, tiled=True, axis_index_groups=groups)
        weight_g, weight_u, weight_d = [weight_f[:, i * n_ff : (i + 1) * n_ff] for i in range(3)]
        qkv = matmul(h_one, weight_qkv)
        mixed, kept = attend_forward(qkv, seg_row, cosine, sine)

        def to_slice(operand, project):
            away = project(rows_of(operand, (1 - core) * rows, rows)).astype(bf16)
            here = rows_of(operand, core * rows, rows)
            away = swap_core(away)
            other = project(rows_of(here, (1 - half) * part, part)) + rows_of(
                away, (1 - half) * part, part
            ).astype(f32)
            other = swap_tp(other.astype(bf16))
            own = project(rows_of(here, half * part, part)) + rows_of(
                away, half * part, part
            ).astype(f32)
            return own + other.astype(f32)

        x_part = rows_of(x_own, half * part, part).astype(f32)
        after_attn = x_part + to_slice(mixed, lambda v: contract_cols(v, weight_o))
        normed_two, inverse_two = norm_parts(after_attn)
        h_part = (normed_two * gain_m).astype(bf16)

        by_tp, by_zl = swap_tp(h_part), across(h_part, 2)
        mid = part // 2
        near = cat([h_part, by_tp, by_zl])
        far_near = swap_core(near)
        both = cat([across(by_tp[:mid], 2), swap_tp(by_zl[mid:])])
        h_two = cat([near, both, far_near, swap_core(both)])

        dy_rel = permute_cols(cotangent, rel, block)
        dy_ff = cat([rows_of(dy_rel, half * part, part), rows_of(dy_rel, (1 - half) * part, part)])
        dy_zl = across(after(dy_ff[:part], both), 2)
        near = cat([dy_ff, dy_zl, swap_tp(dy_zl)])
        grad_out = cat([near, swap_core(near)])

        gate_pre = matmul(h_two, weight_g)
        up_pre = matmul(h_two, weight_u)
        gate_sig = jax.nn.sigmoid(gate_pre)
        gate_act = gate_pre * gate_sig
        hidden = (gate_act * up_pre).astype(bf16)

        def from_tokens(project, gate=None):
            count = 4 * part
            away = swap_core(project(slice(count, 2 * count)).astype(bf16))
            total = project(slice(0, count)) + away.astype(f32)
            mid = width // 2
            low, high = total[:, :mid], total[:, mid:]

            def pick(values, i):
                return values[i * part : (i + 1) * part]

            low_sent = cat([pick(low, 1), pick(low, 3)]).astype(bf16)
            high_sent = cat([pick(high, 2), pick(high, 3)]).astype(bf16)
            if gate is not None:
                low_sent, high_sent = after((low_sent, high_sent), gate)
            low_tp, high_zl = swap_tp(low_sent), across(high_sent, 2)
            first = (low_tp, high_zl)
            low_tp, high_zl = low_tp.astype(f32), high_zl.astype(f32)
            low_zl = across((pick(low, 2) + pick(low_tp, 1)).astype(bf16), 2)
            high_tp = swap_tp((pick(high, 1) + pick(high_zl, 1)).astype(bf16))
            second = (low_zl, high_tp)
            low_sum = pick(low, 0) + pick(low_tp, 0) + low_zl.astype(f32)
            high_sum = pick(high, 0) + pick(high_zl, 0) + high_tp.astype(f32)
            return (low_sent, first, second), cat([low_sum, high_sum], 1)

        grad_hidden = matmul(grad_out, weight_d)
        grad_gate = (grad_hidden * up_pre * gate_sig * (1.0 + gate_pre * (1.0 - gate_sig))).astype(bf16)
        grad_up = (grad_hidden * gate_act).astype(bf16)
        prod_d = contract_rows(grad_out, hidden).astype(bf16)
        late_hidden = after(hidden, prod_d)
        (sent_m, first_m, second_m), mlp = from_tokens(lambda where: contract_cols(late_hidden[where], weight_d))
        grad_gate, grad_up = after((grad_gate, grad_up), sent_m)
        prod_gu = cat(
            [contract_rows(h_two, grad_gate).astype(bf16), contract_rows(h_two, grad_up).astype(bf16)], 1
        )
        late_gate, late_up = after((grad_gate, grad_up), prod_gu, first_m)
        _, grad_h_two = from_tokens(
            lambda where: contract_cols(late_gate[where], weight_g)
            + contract_cols(late_up[where], weight_u),
            second_m,
        )
        out_part = (after_attn + mlp).astype(bf16)
        output = join_tokens(out_part, swap_tp(out_part), half, nat, block)

        grad_gain_m = jnp.sum(grad_h_two * normed_two, axis=0, keepdims=True)
        dy_part = rows_of(dy_rel, half * part, part).astype(f32)
        grad_after = dy_part + norm_back(grad_h_two * gain_m, normed_two, inverse_two)

        grad_part = grad_after.astype(bf16)
        grad_half = ordered(half, grad_part, swap_tp(grad_part))
        grad_attn = ordered(core, grad_half, swap_core(grad_half))
        grad_mixed = matmul(grad_attn, weight_o).astype(bf16)

        def scatter(values, members):
            return lax.psum_scatter(
                values.astype(bf16), "shard", scatter_dimension=0, tiled=True, axis_index_groups=members
            )

        def away_rows(own):
            return across(rows_of(own, (1 - zl) * block, block), 2)

        def rows_pair(own, other, count):
            def send_rows(s_ref, mine, theirs, out):
                low, away_rows = s_ref[1], pl.multiple_of((1 - s_ref[0]) * unit, unit)
                rows_m = pl.ds(pl.multiple_of(low * block, block) + away_rows, unit)
                for i in range(count):
                    cols = slice(i * n_ff, (i + 1) * n_ff)
                    out[:, pl.ds(i * 2 * n_ff + pl.multiple_of(low * n_ff, n_ff), n_ff)] = mine[rows_m, cols]
                    out[:, pl.ds(i * 2 * n_ff + pl.multiple_of((1 - low) * n_ff, n_ff), n_ff)] = theirs[
                        pl.ds(away_rows, unit), cols
                    ]

            (sent,) = small_call(send_rows, [core, zl], [own, other], [array_of(unit, 2 * count * n_ff)])
            third = swap_core(sent)

            def join_rows(s_ref, mine, theirs, third_ref, *outs):
                me, low = s_ref[0], s_ref[1]
                start = pl.multiple_of(me * 2 * n_ff, n_ff)
                away = pl.multiple_of((1 - me) * 2 * n_ff, n_ff)
                here = pl.multiple_of(me * unit, unit)
                for i, out in enumerate(outs):
                    cols = slice(i * n_ff, (i + 1) * n_ff)
                    out[:, pl.ds(start + pl.multiple_of(low * n_ff, n_ff), n_ff)] = mine[
                        pl.ds(pl.multiple_of(low * block, block) + here, unit), cols
                    ].astype(f32)
                    out[:, pl.ds(start + pl.multiple_of((1 - low) * n_ff, n_ff), n_ff)] = theirs[
                        pl.ds(here, unit), cols
                    ].astype(f32)
                    out[:, pl.ds(away, 2 * n_ff)] = third_ref[:, i * 2 * n_ff : (i + 1) * 2 * n_ff].astype(f32)

            return small_call(join_rows, [core, zl], [own, other, third], [array_of(unit, 4 * n_ff, f32)] * count)

        def send_unit(s_ref, own, out):
            out[...] = own[pl.ds((1 - s_ref[0]) * unit, unit), :].astype(bf16)

        own_d = scatter(prod_d, groups)
        own_gu = scatter(prod_gu, groups)
        late_o = contract_rows(grad_attn, mixed).astype(bf16)
        own_o = scatter(after(late_o, own_d, own_gu), every)
        grad_mixed = after(grad_mixed, late_o)
        grad_qkv = attend_backward(kept, grad_mixed, seg_row, cosine, sine, 0, heads)
        other_d, other_gu = away_rows(own_d), away_rows(own_gu)
        grad_qkv = after(grad_qkv, other_gu)
        own_qkv = scatter(after(contract_rows(h_one, grad_qkv).astype(bf16), own_o), every)

        (grad_w_down,) = rows_pair(own_d, other_d, 1)
        grad_w_gate, grad_w_up = rows_pair(own_gu, other_gu, 2)

        grad_h_one = to_slice(grad_qkv, lambda v: contract_cols(v, weight_qkv))

        normed_part = rows_of(normed_all, core * rows + half * part, part)
        inverse_part = rows_of(inverse_all, core * rows + half * part, part)
        grad_gain_a = jnp.sum(grad_h_one * normed_part, axis=0, keepdims=True)
        grad_x = (grad_after + norm_back(grad_h_one * gain_a, normed_part, inverse_part)).astype(bf16)
        grad_tokens = join_tokens(grad_x, swap_tp(grad_x), half, nat, block)

        own_qkv = after(own_qkv, output, grad_tokens, grad_w_gate, grad_w_up, grad_w_down)
        own_a = cat([own_qkv, own_o], 1)
        (sent_g,) = small_call(send_unit, [core], [own_a], [array_of(unit, 4 * n_attn)])
        other_a = swap_core(sent_g)

        def join_attn(s_ref, own, other, q, k, v, o):
            me = s_ref[0]
            mine = pl.ds(pl.multiple_of(me * unit, unit), unit)
            here, there = me * n_attn, (1 - me) * n_attn
            for start, load in (
                (here, lambda c: own[mine, c].astype(f32)),
                (there, lambda c: other[:, c].astype(f32)),
            ):
                start = pl.multiple_of(start, n_attn)
                for h in range(heads):
                    for i, ref in enumerate((q, k, v)):
                        ref[:, pl.ds(start + h * HD, HD)] = load(slice((3 * h + i) * HD, (3 * h + i + 1) * HD))
                o[:, pl.ds(start, n_attn)] = load(slice(3 * n_attn, 4 * n_attn))

        grad_w_query, grad_w_key, grad_w_value, grad_w_out = small_call(
            join_attn, [core], [own_a, other_a], [array_of(unit, 2 * n_attn, f32)] * 4
        )

        grad_gains = cat([grad_gain_a, grad_gain_m])
        grad_gains = grad_gains + swap_tp(grad_gains)
        for mask in [1 << bit for bit in range(shards.bit_length() - 2, 1, -1)] + [1, 2]:
            mid = grad_gains.shape[1] // 2
            first, second = grad_gains[:, :mid], grad_gains[:, mid:]
            low = (shard & mask) == 0
            grad_gains = jnp.where(low, first, second) + across(jnp.where(low, second, first), mask)
        first, second = grad_gains[:, :unit], grad_gains[:, unit:]
        grad_gains = jnp.where(core == 0, first, second) + swap_core(jnp.where(core == 0, second, first))

        return (
            output,
            grad_tokens,
            grad_gains[0],
            grad_w_query,
            grad_w_key,
            grad_w_value,
            grad_w_out,
            grad_gains[1],
            grad_w_gate,
            grad_w_up,
            grad_w_down,
        )

    return per_device


def solution(mesh):
    wide = P(("shard", "ctx"), None)
    flat = P(("shard", "ctx"))
    both = P(("shard", "ctx"), "tp")
    placed = (wide, P("shard", None), flat, both, both, both, both, flat, both, both, both, wide)
    return jax.shard_map(
        build(mesh.shape["shard"]),
        mesh=mesh,
        in_specs=placed,
        out_specs=(wide, wide, flat, both, both, both, both, flat, both, both, both),
        check_vma=False,
    )
```

```python
import math

import jax
import jax.numpy as jnp
from jax import lax
from jax.experimental import pallas as pl
from jax.experimental.pallas import tpu as pltpu
from jax.sharding import PartitionSpec as P

HD = 128
LENGTH = 1024


norm_eps = 1e-05
rope_base = 10000.0

bf16 = jnp.bfloat16
f32 = jnp.float32


def matmul(left, right):
    return jnp.dot(left, right, preferred_element_type=jnp.float32)


def contract_rows(left, right):
    return lax.dot_general(
        left, right, (((0,), (0,)), ((), ())), preferred_element_type=jnp.float32
    )


def contract_cols(left, right):
    return lax.dot_general(
        left, right, (((1,), (1,)), ((), ())), preferred_element_type=jnp.float32
    )


def norm_parts(values):
    inverse = lax.rsqrt(jnp.mean(values * values, axis=-1, keepdims=True) + norm_eps)
    return (values * inverse, inverse)


def norm_back(grad_scaled, normed, inverse):
    return inverse * (grad_scaled - normed * jnp.mean(grad_scaled * normed, axis=-1, keepdims=True))


def doc_positions(seg_row):
    places = jnp.arange(seg_row.shape[0], dtype=jnp.int32)
    starts_here = jnp.concatenate([jnp.ones((1,), dtype=jnp.bool_), seg_row[1:] != seg_row[:-1]])
    starts = lax.cummax(jnp.where(starts_here, places, jnp.zeros_like(places)), axis=0)
    return places - starts


def rope_tables(positions):
    half_dim = HD // 2
    freqs = rope_base ** (-(jnp.arange(half_dim, dtype=jnp.float32) * (2.0 / HD)))
    angles = positions.astype(jnp.float32)[:, None] * freqs[None, :]
    cosine, sine = jnp.cos(angles), jnp.sin(angles)
    return cat([cosine, cosine], 1), cat([-sine, sine], 1)


def cat(parts, axis=0):
    return jnp.concatenate(parts, axis=axis)


def rows_of(values, start, size):
    return lax.dynamic_slice_in_dim(values, start, size, 0)


def ordered(index, own, other, axis=0):
    return jnp.where(index == 0, cat([own, other], axis), cat([other, own], axis))


def after(values, *events):
    return lax.optimization_barrier((values, events))[0]


def small_call(body, scalars, arrays, outs):
    scalars = jnp.stack([jnp.asarray(v, jnp.int32) for v in scalars])
    return pl.pallas_call(
        body,
        grid_spec=pltpu.PrefetchScalarGridSpec(
            num_scalar_prefetch=1,
            grid=(1,),
            in_specs=[pl.BlockSpec(a.shape, lambda i, s: (0, 0)) for a in arrays],
            out_specs=[pl.BlockSpec(o.shape, lambda i, s: (0, 0)) for o in outs],
        ),
        out_shape=outs,
    )(scalars, *arrays)


def array_of(rows, cols, dtype=bf16):
    return jax.ShapeDtypeStruct((rows, cols), dtype)


def permute_cols(values, index, block):
    rows, width = values.shape
    step = min(rows, 128)
    count = width // block
    if block % 128:
        return cat([lax.dynamic_slice_in_dim(values, index[j] * block, block, 1) for j in range(count)], 1)

    def body(index_ref, in_ref, out_ref):
        for j in range(count):
            start = pl.multiple_of(index_ref[j] * block, block)
            out_ref[:, j * block : (j + 1) * block] = in_ref[:, pl.ds(start, block)]

    spec = pl.BlockSpec((step, width), lambda i, s: (i, 0))
    return pl.pallas_call(
        body,
        grid_spec=pltpu.PrefetchScalarGridSpec(
            num_scalar_prefetch=1, grid=(rows // step,), in_specs=[spec], out_specs=spec
        ),
        out_shape=jax.ShapeDtypeStruct(values.shape, values.dtype),
    )(index, values)


def join_tokens(own, other, half, index, block):
    rows, width = own.shape
    count = width // block
    if block % 128:
        return permute_cols(ordered(half, own, other), index, block)

    def body(index_ref, own_ref, other_ref, out_ref):
        here = pl.program_id(0) == index_ref[count]

        def move(ref):
            for j in range(count):
                start = pl.multiple_of(index_ref[j] * block, block)
                out_ref[:, j * block : (j + 1) * block] = ref[:, pl.ds(start, block)]

        pl.when(here)(lambda: move(own_ref))
        pl.when(jnp.logical_not(here))(lambda: move(other_ref))

    whole = pl.BlockSpec((rows, width), lambda i, s: (0, 0))
    return pl.pallas_call(
        body,
        grid_spec=pltpu.PrefetchScalarGridSpec(
            num_scalar_prefetch=1,
            grid=(2,),
            in_specs=[whole, whole],
            out_specs=pl.BlockSpec((rows, width), lambda i, s: (i, 0)),
        ),
        out_shape=jax.ShapeDtypeStruct((2 * rows, width), own.dtype),
    )(cat([index, half[None]]), own, other)


def score_parts(query, keys, rows_seg, cols_seg, diagonal):
    scores = contract_cols(query, keys) * (1.0 / math.sqrt(HD)) - math.log(LENGTH)
    allowed = rows_seg == cols_seg
    if diagonal:
        size = query.shape[0]
        places = lax.broadcasted_iota(jnp.int32, (size, size), 0)
        allowed = allowed & (places >= lax.broadcasted_iota(jnp.int32, (size, size), 1))
    return jax.nn.sigmoid(scores), allowed


def swap_halves(values):
    return pltpu.roll(values, HD // 2, 1)


def attend_forward(qkv, seg_row, cosine, sine, tile=256):
    length = seg_row.shape[0]
    heads = qkv.shape[1] // (3 * HD)
    tiles = length // tile

    def body(seg_ref, qkv_ref, cos_ref, sin_ref, seg_col, seg_line, out_ref, kept_ref, acc):
        cos_t, sin_t = cos_ref[...], sin_ref[...]
        for part in (0, 1):
            where = slice(part * HD, (part + 1) * HD)
            value = qkv_ref[:, where]
            kept_ref[:, where] = (value * cos_t + swap_halves(value) * sin_t).astype(bf16)
        kept_ref[:, 2 * HD :] = qkv_ref[:, 2 * HD :].astype(bf16)
        for i in range(tiles):
            rows = slice(i * tile, (i + 1) * tile)

            def step(j, diagonal, rows=rows):
                cols = slice(j * tile, (j + 1) * tile)
                sig, allowed = score_parts(
                    kept_ref[rows, :HD], kept_ref[cols, HD : 2 * HD],
                    seg_col[rows, :], seg_line[:, cols], diagonal,
                )
                weights = jnp.where(allowed, sig, 0.0).astype(bf16)
                return matmul(weights, kept_ref[cols, 2 * HD :])

            acc[...] = step(i, True)
            for j in range(i):

                @pl.when(seg_ref[(j + 1) * tile - 1] == seg_ref[i * tile])
                def _(j=j):
                    acc[...] += step(j, False)

            out_ref[rows, :] = acc[...].astype(bf16)

    full = pl.BlockSpec((length, HD), lambda h, s: (0, 0))
    return pl.pallas_call(
        body,
        grid_spec=pltpu.PrefetchScalarGridSpec(
            num_scalar_prefetch=1,
            grid=(heads,),
            in_specs=[
                pl.BlockSpec((length, 3 * HD), lambda h, s: (0, h)),
                full,
                full,
                pl.BlockSpec((length, 1), lambda h, s: (0, 0)),
                pl.BlockSpec((1, length), lambda h, s: (0, 0)),
            ],
            out_specs=[
                pl.BlockSpec((length, HD), lambda h, s: (0, h)),
                pl.BlockSpec((length, 3 * HD), lambda h, s: (0, h)),
            ],
            scratch_shapes=[pltpu.VMEM((tile, HD), f32)],
        ),
        out_shape=[array_of(length, heads * HD), array_of(length, 3 * heads * HD)],
    )(seg_row, qkv, cosine, sine, seg_row[:, None], seg_row[None, :])


def attend_backward(kept, grad_heads, seg_row, cosine, sine, first, heads, tile=256):
    length = seg_row.shape[0]
    tiles = length // tile
    scale = 1.0 / math.sqrt(HD)

    def body(seg_ref, kept_ref, do_ref, cos_ref, sin_ref, seg_col, seg_line, out_ref, dq, dk, dv):
        dk[...] = jnp.zeros_like(dk)
        dv[...] = jnp.zeros_like(dv)
        for i in range(tiles):
            rows = slice(i * tile, (i + 1) * tile)

            def step(j, diagonal, rows=rows):
                cols = slice(j * tile, (j + 1) * tile)
                query, grad = kept_ref[rows, :HD], do_ref[rows, :]
                keys = kept_ref[cols, HD : 2 * HD]
                sig, allowed = score_parts(query, keys, seg_col[rows, :], seg_line[:, cols], diagonal)
                weights = jnp.where(allowed, sig, 0.0).astype(bf16)
                dv[cols, :] += contract_rows(weights, grad)
                grad_probs = contract_cols(grad, kept_ref[cols, 2 * HD :])
                grad_scores = jnp.where(allowed, grad_probs * sig * (1.0 - sig), 0.0).astype(bf16)
                dk[cols, :] += contract_rows(grad_scores, query)
                return matmul(grad_scores, keys)

            dq[rows, :] = step(i, True)
            for j in range(i):

                @pl.when(seg_ref[(j + 1) * tile - 1] == seg_ref[i * tile])
                def _(j=j, rows=rows):
                    dq[rows, :] += step(j, False)

        cos_t, sin_t = cos_ref[...], sin_ref[...]
        for part, ref in ((0, dq), (1, dk)):
            grad = ref[...] * scale
            out_ref[:, part * HD : (part + 1) * HD] = (grad * cos_t - swap_halves(grad) * sin_t).astype(bf16)
        out_ref[:, 2 * HD :] = dv[...].astype(bf16)

    full = pl.BlockSpec((length, HD), lambda h, s: (0, 0))
    return pl.pallas_call(
        body,
        grid_spec=pltpu.PrefetchScalarGridSpec(
            num_scalar_prefetch=1,
            grid=(heads,),
            in_specs=[
                pl.BlockSpec((length, 3 * HD), lambda h, s: (0, first + h)),
                pl.BlockSpec((length, HD), lambda h, s: (0, first + h)),
                full,
                full,
                pl.BlockSpec((length, 1), lambda h, s: (0, 0)),
                pl.BlockSpec((1, length), lambda h, s: (0, 0)),
            ],
            out_specs=pl.BlockSpec((length, 3 * HD), lambda h, s: (0, h)),
            scratch_shapes=[pltpu.VMEM((length, HD), f32)] * 3,
        ),
        out_shape=array_of(length, 3 * heads * HD),
    )(seg_row, kept, grad_heads, cosine, sine, seg_row[:, None], seg_row[None, :])


def build(shards):
    line = [k << 1 for k in range(1, shards // 2)]

    groups = [[i for i in range(shards) if (i >> 1) & 1 == bit] for bit in (0, 1)]
    every = [[(i & ~3) | ((i & 1) << 1) | ((i >> 1) & 1) for i in range(shards)]]

    def across(values, mask):
        return lax.ppermute(values, "shard", [(i, i ^ mask) for i in range(shards)])

    def swap_core(values):
        return lax.ppermute(values, "ctx", [(0, 1), (1, 0)])

    def swap_tp(values):
        return lax.ppermute(values, "tp", [(0, 1), (1, 0)])

    def per_device(
        tokens,
        segments,
        gain_attn,
        w_query,
        w_key,
        w_value,
        w_out,
        gain_mlp,
        w_gate,
        w_up,
        w_down,
        cotangent,
    ):
        shard = lax.axis_index("shard").astype(jnp.int32)
        core = lax.axis_index("ctx").astype(jnp.int32)
        half = lax.axis_index("tp").astype(jnp.int32)
        y, zl = shard & 1, (shard >> 1) & 1
        rows, width = tokens.shape
        part = rows // 2
        block = width // shards
        unit = block // 2
        n_attn = w_query.shape[1] // 2
        n_ff = w_gate.shape[1] // 4
        heads = n_attn // HD
        half_s = shards // 2
        pad = 16

        def place_of(number):
            return (number & ~3) | ((number & 1) << 1) | ((number >> 1) & 1)

        rel = place_of(jnp.arange(shards, dtype=jnp.int32))
        nat = rel

        attn_w = [w_query, w_key, w_value, w_out]
        ff_w = [w_gate, w_up, w_down]

        def send_attn(s_ref, q, k, v, o, out):
            start = pl.multiple_of((1 - s_ref[0]) * n_attn, n_attn)
            for h in range(heads):
                for i, ref in enumerate((q, k, v)):
                    out[:, (3 * h + i) * HD : (3 * h + i + 1) * HD] = ref[:, pl.ds(start + h * HD, HD)]
            out[:, 3 * n_attn :] = o[:, pl.ds(start, n_attn)]

        (sent_a,) = small_call(send_attn, [core], attn_w, [array_of(unit, 4 * n_attn)])
        other_a = swap_core(sent_a)
        gains = jnp.stack([gain_attn, gain_mlp])
        other_gains = swap_core(gains)

        def keep_attn(s_ref, q, k, v, o, other, own_g, other_g, out_qkv, out_o):
            me = s_ref[0]
            start = pl.multiple_of(me * n_attn, n_attn)
            mine, theirs = pl.ds(me * unit, unit), pl.ds((1 - me) * unit, unit)
            for h in range(heads):
                for i, ref in enumerate((q, k, v)):
                    where = slice((3 * h + i) * HD, (3 * h + i + 1) * HD)
                    out_qkv[mine, where] = ref[:, pl.ds(start + h * HD, HD)]
            out_o[mine, :] = o[:, pl.ds(start, n_attn)]
            out_qkv[theirs, :] = other[:, : 3 * n_attn]
            out_o[theirs, :] = other[:, 3 * n_attn :]
            first, second = own_g[...], other_g[...]
            low = jnp.where(me == 0, first, second)
            high = jnp.where(me == 0, second, first)
            line_g = cat([low, high, jnp.zeros((2, n_attn - block), bf16)], 1)
            out_o[block:, :] = cat([line_g, jnp.zeros((pad - 2, n_attn), bf16)])

        block_qkv, block_o = small_call(
            keep_attn, [core], attn_w + [other_a, gains, other_gains],
            [array_of(block, 3 * n_attn), array_of(block + pad, n_attn)],
        )

        def shard_at(i):
            return shard ^ (((i % half_s) << 1) | (i // half_s))

        weight_qkv = lax.all_gather(block_qkv, "shard", axis=0, tiled=True, axis_index_groups=every)
        near_o = cat([block_o] + [across(block_o, mask) for mask in line])
        parts_o = cat([near_o, across(near_o, 1)]).reshape(shards, block + pad, n_attn)
        weight_o = jnp.zeros((width, n_attn), bf16)
        for i in range(shards):
            weight_o = lax.dynamic_update_slice_in_dim(
                weight_o, parts_o[i, :block], place_of(shard_at(i)) * block, 0
            )
        gain_rows = parts_o[:, block : block + 2, :block]
        away_bits = place_of(jnp.arange(shards, dtype=jnp.int32)) ^ shard
        gain_rows = gain_rows[(away_bits >> 1) + half_s * (away_bits & 1)]
        gains_rel = jnp.transpose(gain_rows, (1, 0, 2)).reshape(2, width).astype(f32)
        gain_a, gain_m = gains_rel[0:1], gains_rel[1:2]

        def send_ff(s_ref, g, u, d, out):
            start = pl.multiple_of((1 - s_ref[0]) * 2 * n_ff, n_ff)
            for i, ref in enumerate((g, u, d)):
                out[:, i * 2 * n_ff : (i + 1) * 2 * n_ff] = ref[:, pl.ds(start, 2 * n_ff)]

        (sent_f,) = small_call(send_ff, [core], ff_w, [array_of(unit, 6 * n_ff)])
        other_f = swap_core(sent_f)

        def keep_ff(s_ref, g, u, d, other, keep, send):
            me, low = s_ref[0], s_ref[1]
            mine, theirs = pl.ds(pl.multiple_of(me * unit, unit), unit), pl.ds(pl.multiple_of((1 - me) * unit, unit), unit)
            for out, which in ((keep, low), (send, 1 - low)):
                start = pl.multiple_of(which * n_ff, n_ff)
                for i, ref in enumerate((g, u, d)):
                    cols = slice(i * n_ff, (i + 1) * n_ff)
                    out[mine, cols] = ref[:, pl.ds(pl.multiple_of(me * 2 * n_ff, n_ff) + start, n_ff)]
                    out[theirs, cols] = other[:, pl.ds(i * 2 * n_ff + start, n_ff)]

        keep_f, send_f = small_call(keep_ff, [core, zl], ff_w + [other_f], [array_of(block, 3 * n_ff)] * 2)
        recv_f = across(send_f, 2)

        def pair_rows(s_ref, own, other, out):
            low = s_ref[0]
            out[pl.ds(pl.multiple_of(low * block, block), block), :] = own[...]
            out[pl.ds(pl.multiple_of((1 - low) * block, block), block), :] = other[...]

        (pair_f,) = small_call(pair_rows, [zl], [keep_f, recv_f], [array_of(2 * block, 3 * n_ff)])

        seg_row = segments[0]
        cosine, sine = rope_tables(doc_positions(seg_row))
        x_own = permute_cols(tokens, rel, block)
        x_both = ordered(core, x_own, swap_core(x_own))
        normed_all, inverse_all = norm_parts(x_both.astype(f32))
        h_one = (normed_all * gain_a).astype(bf16)
        pair_f = after(pair_f, weight_qkv, weight_o, h_one, cosine, sine)
        weight_f = lax.all_gather(pair_f, "shard", axis=0, tiled=True, axis_index_groups=groups)
        weight_g, weight_u, weight_d = [weight_f[:, i * n_ff : (i + 1) * n_ff] for i in range(3)]
        qkv = matmul(h_one, weight_qkv)
        mixed, kept = attend_forward(qkv, seg_row, cosine, sine)

        def to_slice(operand, project):
            away = project(rows_of(operand, (1 - core) * rows, rows)).astype(bf16)
            here = rows_of(operand, core * rows, rows)
            away = swap_core(away)
            other = project(rows_of(here, (1 - half) * part, part)) + rows_of(
                away, (1 - half) * part, part
            ).astype(f32)
            other = swap_tp(other.astype(bf16))
            own = project(rows_of(here, half * part, part)) + rows_of(
                away, half * part, part
            ).astype(f32)
            return own + other.astype(f32)

        x_part = rows_of(x_own, half * part, part).astype(f32)
        after_attn = x_part + to_slice(mixed, lambda v: contract_cols(v, weight_o))
        normed_two, inverse_two = norm_parts(after_attn)
        h_part = (normed_two * gain_m).astype(bf16)

        by_tp, by_zl = swap_tp(h_part), across(h_part, 2)
        mid = part // 2
        near = cat([h_part, by_tp, by_zl])
        far_near = swap_core(near)
        both = cat([across(by_tp[:mid], 2), swap_tp(by_zl[mid:])])
        h_two = cat([near, both, far_near, swap_core(both)])

        dy_rel = permute_cols(cotangent, rel, block)
        dy_ff = cat([rows_of(dy_rel, half * part, part), rows_of(dy_rel, (1 - half) * part, part)])
        dy_zl = across(after(dy_ff[:part], both), 2)
        near = cat([dy_ff, dy_zl, swap_tp(dy_zl)])
        grad_out = cat([near, swap_core(near)])

        gate_pre = matmul(h_two, weight_g)
        up_pre = matmul(h_two, weight_u)
        gate_sig = jax.nn.sigmoid(gate_pre)
        gate_act = gate_pre * gate_sig
        hidden = (gate_act * up_pre).astype(bf16)

        def from_tokens(project, gate=None):
            count = 4 * part
            away = swap_core(project(slice(count, 2 * count)).astype(bf16))
            total = project(slice(0, count)) + away.astype(f32)
            mid = width // 2
            low, high = total[:, :mid], total[:, mid:]

            def pick(values, i):
                return values[i * part : (i + 1) * part]

            low_sent = cat([pick(low, 1), pick(low, 3)]).astype(bf16)
            high_sent = cat([pick(high, 2), pick(high, 3)]).astype(bf16)
            if gate is not None:
                low_sent, high_sent = after((low_sent, high_sent), gate)
            low_tp, high_zl = swap_tp(low_sent), across(high_sent, 2)
            first = (low_tp, high_zl)
            low_tp, high_zl = low_tp.astype(f32), high_zl.astype(f32)
            low_zl = across((pick(low, 2) + pick(low_tp, 1)).astype(bf16), 2)
            high_tp = swap_tp((pick(high, 1) + pick(high_zl, 1)).astype(bf16))
            second = (low_zl, high_tp)
            low_sum = pick(low, 0) + pick(low_tp, 0) + low_zl.astype(f32)
            high_sum = pick(high, 0) + pick(high_zl, 0) + high_tp.astype(f32)
            return (low_sent, first, second), cat([low_sum, high_sum], 1)

        grad_hidden = matmul(grad_out, weight_d)
        grad_gate = (grad_hidden * up_pre * gate_sig * (1.0 + gate_pre * (1.0 - gate_sig))).astype(bf16)
        grad_up = (grad_hidden * gate_act).astype(bf16)
        prod_d = contract_rows(grad_out, hidden).astype(bf16)
        late_hidden = after(hidden, prod_d)
        (sent_m, first_m, second_m), mlp = from_tokens(lambda where: contract_cols(late_hidden[where], weight_d))
        grad_gate, grad_up = after((grad_gate, grad_up), sent_m)
        grad_gu = cat([grad_gate, grad_up], 1)
        prod_gu = contract_rows(h_two, grad_gu).astype(bf16)
        late_gu = after(grad_gu, prod_gu, first_m)
        weight_gu = weight_f[:, : 2 * n_ff]
        _, grad_h_two = from_tokens(lambda where: contract_cols(late_gu[where], weight_gu), second_m)
        out_part = (after_attn + mlp).astype(bf16)
        output = join_tokens(out_part, swap_tp(out_part), half, nat, block)

        grad_gain_m = jnp.sum(grad_h_two * normed_two, axis=0, keepdims=True)
        dy_part = rows_of(dy_rel, half * part, part).astype(f32)
        grad_after = dy_part + norm_back(grad_h_two * gain_m, normed_two, inverse_two)

        grad_part = grad_after.astype(bf16)
        grad_half = ordered(half, grad_part, swap_tp(grad_part))
        grad_attn = ordered(core, grad_half, swap_core(grad_half))
        grad_mixed = matmul(grad_attn, weight_o).astype(bf16)

        def scatter(values, members):
            return lax.psum_scatter(
                values.astype(bf16), "shard", scatter_dimension=0, tiled=True, axis_index_groups=members
            )

        def away_rows(own):
            return across(rows_of(own, (1 - zl) * block, block), 2)

        def rows_pair(own, other, count):
            def send_rows(s_ref, mine, theirs, out):
                low, away_rows = s_ref[1], pl.multiple_of((1 - s_ref[0]) * unit, unit)
                rows_m = pl.ds(pl.multiple_of(low * block, block) + away_rows, unit)
                for i in range(count):
                    cols = slice(i * n_ff, (i + 1) * n_ff)
                    out[:, pl.ds(i * 2 * n_ff + pl.multiple_of(low * n_ff, n_ff), n_ff)] = mine[rows_m, cols]
                    out[:, pl.ds(i * 2 * n_ff + pl.multiple_of((1 - low) * n_ff, n_ff), n_ff)] = theirs[
                        pl.ds(away_rows, unit), cols
                    ]

            (sent,) = small_call(send_rows, [core, zl], [own, other], [array_of(unit, 2 * count * n_ff)])
            third = swap_core(sent)

            def join_rows(s_ref, mine, theirs, third_ref, *outs):
                me, low = s_ref[0], s_ref[1]
                start = pl.multiple_of(me * 2 * n_ff, n_ff)
                away = pl.multiple_of((1 - me) * 2 * n_ff, n_ff)
                here = pl.multiple_of(me * unit, unit)
                for i, out in enumerate(outs):
                    cols = slice(i * n_ff, (i + 1) * n_ff)
                    out[:, pl.ds(start + pl.multiple_of(low * n_ff, n_ff), n_ff)] = mine[
                        pl.ds(pl.multiple_of(low * block, block) + here, unit), cols
                    ].astype(f32)
                    out[:, pl.ds(start + pl.multiple_of((1 - low) * n_ff, n_ff), n_ff)] = theirs[
                        pl.ds(here, unit), cols
                    ].astype(f32)
                    out[:, pl.ds(away, 2 * n_ff)] = third_ref[:, i * 2 * n_ff : (i + 1) * 2 * n_ff].astype(f32)

            return small_call(join_rows, [core, zl], [own, other, third], [array_of(unit, 4 * n_ff, f32)] * count)

        def send_unit(s_ref, own, out):
            out[...] = own[pl.ds((1 - s_ref[0]) * unit, unit), :].astype(bf16)

        own_d = scatter(prod_d, groups)
        own_gu = scatter(prod_gu, groups)
        late_o = contract_rows(grad_attn, mixed).astype(bf16)
        own_o = scatter(after(late_o, own_d, own_gu), every)
        grad_mixed = after(grad_mixed, late_o)
        grad_qkv = attend_backward(kept, grad_mixed, seg_row, cosine, sine, 0, heads)
        other_d, other_gu = away_rows(own_d), away_rows(own_gu)
        grad_qkv = after(grad_qkv, other_gu)
        own_qkv = scatter(after(contract_rows(h_one, grad_qkv).astype(bf16), own_o), every)

        (grad_w_down,) = rows_pair(own_d, other_d, 1)
        grad_w_gate, grad_w_up = rows_pair(own_gu, other_gu, 2)

        grad_h_one = to_slice(grad_qkv, lambda v: contract_cols(v, weight_qkv))

        normed_part = rows_of(normed_all, core * rows + half * part, part)
        inverse_part = rows_of(inverse_all, core * rows + half * part, part)
        grad_gain_a = jnp.sum(grad_h_one * normed_part, axis=0, keepdims=True)
        grad_x = (grad_after + norm_back(grad_h_one * gain_a, normed_part, inverse_part)).astype(bf16)
        grad_tokens = join_tokens(grad_x, swap_tp(grad_x), half, nat, block)

        own_qkv = after(own_qkv, output, grad_tokens, grad_w_gate, grad_w_up, grad_w_down)
        own_a = cat([own_qkv, own_o], 1)
        (sent_g,) = small_call(send_unit, [core], [own_a], [array_of(unit, 4 * n_attn)])
        other_a = swap_core(sent_g)

        def join_attn(s_ref, own, other, q, k, v, o):
            me = s_ref[0]
            mine = pl.ds(pl.multiple_of(me * unit, unit), unit)
            here, there = me * n_attn, (1 - me) * n_attn
            for start, load in (
                (here, lambda c: own[mine, c].astype(f32)),
                (there, lambda c: other[:, c].astype(f32)),
            ):
                start = pl.multiple_of(start, n_attn)
                for h in range(heads):
                    for i, ref in enumerate((q, k, v)):
                        ref[:, pl.ds(start + h * HD, HD)] = load(slice((3 * h + i) * HD, (3 * h + i + 1) * HD))
                o[:, pl.ds(start, n_attn)] = load(slice(3 * n_attn, 4 * n_attn))

        grad_w_query, grad_w_key, grad_w_value, grad_w_out = small_call(
            join_attn, [core], [own_a, other_a], [array_of(unit, 2 * n_attn, f32)] * 4
        )

        grad_gains = cat([grad_gain_a, grad_gain_m])
        grad_gains = grad_gains + swap_tp(grad_gains)
        for mask in [1 << bit for bit in range(shards.bit_length() - 2, 1, -1)] + [1, 2]:
            mid = grad_gains.shape[1] // 2
            first, second = grad_gains[:, :mid], grad_gains[:, mid:]
            low = (shard & mask) == 0
            grad_gains = jnp.where(low, first, second) + across(jnp.where(low, second, first), mask)
        first, second = grad_gains[:, :unit], grad_gains[:, unit:]
        grad_gains = jnp.where(core == 0, first, second) + swap_core(jnp.where(core == 0, second, first))

        return (
            output,
            grad_tokens,
            grad_gains[0],
            grad_w_query,
            grad_w_key,
            grad_w_value,
            grad_w_out,
            grad_gains[1],
            grad_w_gate,
            grad_w_up,
            grad_w_down,
        )

    return per_device


def solution(mesh):
    wide = P(("shard", "ctx"), None)
    flat = P(("shard", "ctx"))
    both = P(("shard", "ctx"), "tp")
    placed = (wide, P("shard", None), flat, both, both, both, both, flat, both, both, both, wide)
    return jax.shard_map(
        build(mesh.shape["shard"]),
        mesh=mesh,
        in_specs=placed,
        out_specs=(wide, wide, flat, both, both, both, both, flat, both, both, both),
        check_vma=False,
    )
```

```python
import math

import jax
import jax.numpy as jnp
from jax import lax
from jax.experimental import pallas as pl
from jax.experimental.pallas import tpu as pltpu
from jax.sharding import PartitionSpec as P

HD = 128
LENGTH = 1024


norm_eps = 1e-05
rope_base = 10000.0

bf16 = jnp.bfloat16
f32 = jnp.float32


def matmul(left, right):
    return jnp.dot(left, right, preferred_element_type=jnp.float32)


def contract_rows(left, right):
    return lax.dot_general(
        left, right, (((0,), (0,)), ((), ())), preferred_element_type=jnp.float32
    )


def contract_cols(left, right):
    return lax.dot_general(
        left, right, (((1,), (1,)), ((), ())), preferred_element_type=jnp.float32
    )


def norm_parts(values):
    inverse = lax.rsqrt(jnp.mean(values * values, axis=-1, keepdims=True) + norm_eps)
    return (values * inverse, inverse)


def norm_back(grad_scaled, normed, inverse):
    return inverse * (grad_scaled - normed * jnp.mean(grad_scaled * normed, axis=-1, keepdims=True))


def doc_positions(seg_row):
    places = jnp.arange(seg_row.shape[0], dtype=jnp.int32)
    starts_here = jnp.concatenate([jnp.ones((1,), dtype=jnp.bool_), seg_row[1:] != seg_row[:-1]])
    starts = lax.cummax(jnp.where(starts_here, places, jnp.zeros_like(places)), axis=0)
    return places - starts


def rope_tables(positions):
    half_dim = HD // 2
    freqs = rope_base ** (-(jnp.arange(half_dim, dtype=jnp.float32) * (2.0 / HD)))
    angles = positions.astype(jnp.float32)[:, None] * freqs[None, :]
    cosine, sine = jnp.cos(angles), jnp.sin(angles)
    return cat([cosine, cosine], 1), cat([-sine, sine], 1)


def cat(parts, axis=0):
    return jnp.concatenate(parts, axis=axis)


def rows_of(values, start, size):
    return lax.dynamic_slice_in_dim(values, start, size, 0)


def ordered(index, own, other, axis=0):
    return jnp.where(index == 0, cat([own, other], axis), cat([other, own], axis))


def after(values, *events):
    return lax.optimization_barrier((values, events))[0]


def small_call(body, scalars, arrays, outs):
    scalars = jnp.stack([jnp.asarray(v, jnp.int32) for v in scalars])
    return pl.pallas_call(
        body,
        grid_spec=pltpu.PrefetchScalarGridSpec(
            num_scalar_prefetch=1,
            grid=(1,),
            in_specs=[pl.BlockSpec(a.shape, lambda i, s: (0, 0)) for a in arrays],
            out_specs=[pl.BlockSpec(o.shape, lambda i, s: (0, 0)) for o in outs],
        ),
        out_shape=outs,
    )(scalars, *arrays)


def array_of(rows, cols, dtype=bf16):
    return jax.ShapeDtypeStruct((rows, cols), dtype)


def permute_cols(values, index, block):
    rows, width = values.shape
    step = min(rows, 128)
    count = width // block
    if block % 128:
        return cat([lax.dynamic_slice_in_dim(values, index[j] * block, block, 1) for j in range(count)], 1)

    def body(index_ref, in_ref, out_ref):
        for j in range(count):
            start = pl.multiple_of(index_ref[j] * block, block)
            out_ref[:, j * block : (j + 1) * block] = in_ref[:, pl.ds(start, block)]

    spec = pl.BlockSpec((step, width), lambda i, s: (i, 0))
    return pl.pallas_call(
        body,
        grid_spec=pltpu.PrefetchScalarGridSpec(
            num_scalar_prefetch=1, grid=(rows // step,), in_specs=[spec], out_specs=spec
        ),
        out_shape=jax.ShapeDtypeStruct(values.shape, values.dtype),
    )(index, values)


def join_tokens(own, other, half, index, block):
    rows, width = own.shape
    count = width // block
    if block % 128:
        return permute_cols(ordered(half, own, other), index, block)

    def body(index_ref, own_ref, other_ref, out_ref):
        here = pl.program_id(0) == index_ref[count]

        def move(ref):
            for j in range(count):
                start = pl.multiple_of(index_ref[j] * block, block)
                out_ref[:, j * block : (j + 1) * block] = ref[:, pl.ds(start, block)]

        pl.when(here)(lambda: move(own_ref))
        pl.when(jnp.logical_not(here))(lambda: move(other_ref))

    whole = pl.BlockSpec((rows, width), lambda i, s: (0, 0))
    return pl.pallas_call(
        body,
        grid_spec=pltpu.PrefetchScalarGridSpec(
            num_scalar_prefetch=1,
            grid=(2,),
            in_specs=[whole, whole],
            out_specs=pl.BlockSpec((rows, width), lambda i, s: (i, 0)),
        ),
        out_shape=jax.ShapeDtypeStruct((2 * rows, width), own.dtype),
    )(cat([index, half[None]]), own, other)


def score_parts(query, keys, rows_seg, cols_seg, diagonal):
    scores = contract_cols(query, keys) * (1.0 / math.sqrt(HD)) - math.log(LENGTH)
    allowed = rows_seg == cols_seg
    if diagonal:
        size = query.shape[0]
        places = lax.broadcasted_iota(jnp.int32, (size, size), 0)
        allowed = allowed & (places >= lax.broadcasted_iota(jnp.int32, (size, size), 1))
    return jax.nn.sigmoid(scores), allowed


def swap_halves(values):
    return pltpu.roll(values, HD // 2, 1)


def attend_forward(qkv, seg_row, cosine, sine, tile=256):
    length = seg_row.shape[0]
    heads = qkv.shape[1] // (3 * HD)
    tiles = length // tile

    def body(seg_ref, qkv_ref, cos_ref, sin_ref, seg_col, seg_line, out_ref, kept_ref, acc):
        cos_t, sin_t = cos_ref[...], sin_ref[...]
        for part in (0, 1):
            where = slice(part * HD, (part + 1) * HD)
            value = qkv_ref[:, where]
            kept_ref[:, where] = (value * cos_t + swap_halves(value) * sin_t).astype(bf16)
        kept_ref[:, 2 * HD :] = qkv_ref[:, 2 * HD :].astype(bf16)
        for i in range(tiles):
            rows = slice(i * tile, (i + 1) * tile)

            def step(j, diagonal, rows=rows):
                cols = slice(j * tile, (j + 1) * tile)
                sig, allowed = score_parts(
                    kept_ref[rows, :HD], kept_ref[cols, HD : 2 * HD],
                    seg_col[rows, :], seg_line[:, cols], diagonal,
                )
                weights = jnp.where(allowed, sig, 0.0).astype(bf16)
                return matmul(weights, kept_ref[cols, 2 * HD :])

            acc[...] = step(i, True)
            for j in range(i):

                @pl.when(seg_ref[(j + 1) * tile - 1] == seg_ref[i * tile])
                def _(j=j):
                    acc[...] += step(j, False)

            out_ref[rows, :] = acc[...].astype(bf16)

    full = pl.BlockSpec((length, HD), lambda h, s: (0, 0))
    return pl.pallas_call(
        body,
        grid_spec=pltpu.PrefetchScalarGridSpec(
            num_scalar_prefetch=1,
            grid=(heads,),
            in_specs=[
                pl.BlockSpec((length, 3 * HD), lambda h, s: (0, h)),
                full,
                full,
                pl.BlockSpec((length, 1), lambda h, s: (0, 0)),
                pl.BlockSpec((1, length), lambda h, s: (0, 0)),
            ],
            out_specs=[
                pl.BlockSpec((length, HD), lambda h, s: (0, h)),
                pl.BlockSpec((length, 3 * HD), lambda h, s: (0, h)),
            ],
            scratch_shapes=[pltpu.VMEM((tile, HD), f32)],
        ),
        out_shape=[array_of(length, heads * HD), array_of(length, 3 * heads * HD)],
    )(seg_row, qkv, cosine, sine, seg_row[:, None], seg_row[None, :])


def attend_backward(kept, grad_heads, seg_row, cosine, sine, first, heads, tile=256):
    length = seg_row.shape[0]
    tiles = length // tile
    scale = 1.0 / math.sqrt(HD)

    def body(seg_ref, kept_ref, do_ref, cos_ref, sin_ref, seg_col, seg_line, out_ref, dq, dk, dv):
        dk[...] = jnp.zeros_like(dk)
        dv[...] = jnp.zeros_like(dv)
        for i in range(tiles):
            rows = slice(i * tile, (i + 1) * tile)

            def step(j, diagonal, rows=rows):
                cols = slice(j * tile, (j + 1) * tile)
                query, grad = kept_ref[rows, :HD], do_ref[rows, :]
                keys = kept_ref[cols, HD : 2 * HD]
                sig, allowed = score_parts(query, keys, seg_col[rows, :], seg_line[:, cols], diagonal)
                weights = jnp.where(allowed, sig, 0.0).astype(bf16)
                dv[cols, :] += contract_rows(weights, grad)
                grad_probs = contract_cols(grad, kept_ref[cols, 2 * HD :])
                grad_scores = jnp.where(allowed, grad_probs * sig * (1.0 - sig), 0.0).astype(bf16)
                dk[cols, :] += contract_rows(grad_scores, query)
                return matmul(grad_scores, keys)

            dq[rows, :] = step(i, True)
            for j in range(i):

                @pl.when(seg_ref[(j + 1) * tile - 1] == seg_ref[i * tile])
                def _(j=j, rows=rows):
                    dq[rows, :] += step(j, False)

        cos_t, sin_t = cos_ref[...], sin_ref[...]
        for part, ref in ((0, dq), (1, dk)):
            grad = ref[...] * scale
            out_ref[:, part * HD : (part + 1) * HD] = (grad * cos_t - swap_halves(grad) * sin_t).astype(bf16)
        out_ref[:, 2 * HD :] = dv[...].astype(bf16)

    full = pl.BlockSpec((length, HD), lambda h, s: (0, 0))
    return pl.pallas_call(
        body,
        grid_spec=pltpu.PrefetchScalarGridSpec(
            num_scalar_prefetch=1,
            grid=(heads,),
            in_specs=[
                pl.BlockSpec((length, 3 * HD), lambda h, s: (0, first + h)),
                pl.BlockSpec((length, HD), lambda h, s: (0, first + h)),
                full,
                full,
                pl.BlockSpec((length, 1), lambda h, s: (0, 0)),
                pl.BlockSpec((1, length), lambda h, s: (0, 0)),
            ],
            out_specs=pl.BlockSpec((length, 3 * HD), lambda h, s: (0, h)),
            scratch_shapes=[pltpu.VMEM((length, HD), f32)] * 3,
        ),
        out_shape=array_of(length, 3 * heads * HD),
    )(seg_row, kept, grad_heads, cosine, sine, seg_row[:, None], seg_row[None, :])


def build(shards):
    line = [k << 1 for k in range(1, shards // 2)]

    groups = [[i for i in range(shards) if (i >> 1) & 1 == bit] for bit in (0, 1)]
    every = [[(i & ~3) | ((i & 1) << 1) | ((i >> 1) & 1) for i in range(shards)]]

    def across(values, mask):
        return lax.ppermute(values, "shard", [(i, i ^ mask) for i in range(shards)])

    def swap_core(values):
        return lax.ppermute(values, "ctx", [(0, 1), (1, 0)])

    def swap_tp(values):
        return lax.ppermute(values, "tp", [(0, 1), (1, 0)])

    def per_device(
        tokens,
        segments,
        gain_attn,
        w_query,
        w_key,
        w_value,
        w_out,
        gain_mlp,
        w_gate,
        w_up,
        w_down,
        cotangent,
    ):
        shard = lax.axis_index("shard").astype(jnp.int32)
        core = lax.axis_index("ctx").astype(jnp.int32)
        half = lax.axis_index("tp").astype(jnp.int32)
        y, zl = shard & 1, (shard >> 1) & 1
        rows, width = tokens.shape
        part = rows // 2
        block = width // shards
        unit = block // 2
        n_attn = w_query.shape[1] // 2
        n_ff = w_gate.shape[1] // 4
        heads = n_attn // HD
        half_s = shards // 2
        pad = 16

        def place_of(number):
            return (number & ~3) | ((number & 1) << 1) | ((number >> 1) & 1)

        rel = place_of(jnp.arange(shards, dtype=jnp.int32))
        nat = rel

        attn_w = [w_query, w_key, w_value, w_out]
        ff_w = [w_gate, w_up, w_down]

        def send_attn(s_ref, q, k, v, o, out):
            start = pl.multiple_of((1 - s_ref[0]) * n_attn, n_attn)
            for h in range(heads):
                for i, ref in enumerate((q, k, v)):
                    out[:, (3 * h + i) * HD : (3 * h + i + 1) * HD] = ref[:, pl.ds(start + h * HD, HD)]
            out[:, 3 * n_attn :] = o[:, pl.ds(start, n_attn)]

        (sent_a,) = small_call(send_attn, [core], attn_w, [array_of(unit, 4 * n_attn)])
        other_a = swap_core(sent_a)
        gains = jnp.stack([gain_attn, gain_mlp])
        other_gains = swap_core(gains)

        def keep_attn(s_ref, q, k, v, o, other, own_g, other_g, out_qkv, out_o):
            me = s_ref[0]
            start = pl.multiple_of(me * n_attn, n_attn)
            mine, theirs = pl.ds(me * unit, unit), pl.ds((1 - me) * unit, unit)
            for h in range(heads):
                for i, ref in enumerate((q, k, v)):
                    where = slice((3 * h + i) * HD, (3 * h + i + 1) * HD)
                    out_qkv[mine, where] = ref[:, pl.ds(start + h * HD, HD)]
            out_o[mine, :] = o[:, pl.ds(start, n_attn)]
            out_qkv[theirs, :] = other[:, : 3 * n_attn]
            out_o[theirs, :] = other[:, 3 * n_attn :]
            first, second = own_g[...], other_g[...]
            low = jnp.where(me == 0, first, second)
            high = jnp.where(me == 0, second, first)
            line_g = cat([low, high, jnp.zeros((2, n_attn - block), bf16)], 1)
            out_o[block:, :] = cat([line_g, jnp.zeros((pad - 2, n_attn), bf16)])

        block_qkv, block_o = small_call(
            keep_attn, [core], attn_w + [other_a, gains, other_gains],
            [array_of(block, 3 * n_attn), array_of(block + pad, n_attn)],
        )

        def shard_at(i):
            return shard ^ (((i % half_s) << 1) | (i // half_s))

        weight_qkv = lax.all_gather(block_qkv, "shard", axis=0, tiled=True, axis_index_groups=every)
        near_o = cat([block_o] + [across(block_o, mask) for mask in line])
        parts_o = cat([near_o, across(near_o, 1)]).reshape(shards, block + pad, n_attn)
        weight_o = jnp.zeros((width, n_attn), bf16)
        for i in range(shards):
            weight_o = lax.dynamic_update_slice_in_dim(
                weight_o, parts_o[i, :block], place_of(shard_at(i)) * block, 0
            )
        gain_rows = parts_o[:, block : block + 2, :block]
        away_bits = place_of(jnp.arange(shards, dtype=jnp.int32)) ^ shard
        gain_rows = gain_rows[(away_bits >> 1) + half_s * (away_bits & 1)]
        gains_rel = jnp.transpose(gain_rows, (1, 0, 2)).reshape(2, width).astype(f32)
        gain_a, gain_m = gains_rel[0:1], gains_rel[1:2]

        def send_ff(s_ref, g, u, d, out):
            start = pl.multiple_of((1 - s_ref[0]) * 2 * n_ff, n_ff)
            for i, ref in enumerate((g, u, d)):
                out[:, i * 2 * n_ff : (i + 1) * 2 * n_ff] = ref[:, pl.ds(start, 2 * n_ff)]

        (sent_f,) = small_call(send_ff, [core], ff_w, [array_of(unit, 6 * n_ff)])
        other_f = swap_core(sent_f)

        def keep_ff(s_ref, g, u, d, other, keep, send):
            me, low = s_ref[0], s_ref[1]
            mine, theirs = pl.ds(pl.multiple_of(me * unit, unit), unit), pl.ds(pl.multiple_of((1 - me) * unit, unit), unit)
            for out, which in ((keep, low), (send, 1 - low)):
                start = pl.multiple_of(which * n_ff, n_ff)
                for i, ref in enumerate((g, u, d)):
                    cols = slice(i * n_ff, (i + 1) * n_ff)
                    out[mine, cols] = ref[:, pl.ds(pl.multiple_of(me * 2 * n_ff, n_ff) + start, n_ff)]
                    out[theirs, cols] = other[:, pl.ds(i * 2 * n_ff + start, n_ff)]

        keep_f, send_f = small_call(keep_ff, [core, zl], ff_w + [other_f], [array_of(block, 3 * n_ff)] * 2)
        recv_f = across(send_f, 2)

        def pair_rows(s_ref, own, other, out):
            low = s_ref[0]
            out[pl.ds(pl.multiple_of(low * block, block), block), :] = own[...]
            out[pl.ds(pl.multiple_of((1 - low) * block, block), block), :] = other[...]

        (pair_f,) = small_call(pair_rows, [zl], [keep_f, recv_f], [array_of(2 * block, 3 * n_ff)])

        seg_row = segments[0]
        cosine, sine = rope_tables(doc_positions(seg_row))
        x_own = permute_cols(tokens, rel, block)
        x_both = ordered(core, x_own, swap_core(x_own))
        normed_all, inverse_all = norm_parts(x_both.astype(f32))
        h_one = (normed_all * gain_a).astype(bf16)
        pair_f = after(pair_f, weight_qkv, weight_o, h_one, cosine, sine)
        weight_f = lax.all_gather(pair_f, "shard", axis=0, tiled=True, axis_index_groups=groups)
        weight_g, weight_u, weight_d = [weight_f[:, i * n_ff : (i + 1) * n_ff] for i in range(3)]
        qkv = matmul(h_one, weight_qkv)
        mixed, kept = attend_forward(qkv, seg_row, cosine, sine)

        def to_slice(operand, project):
            away = project(rows_of(operand, (1 - core) * rows, rows)).astype(bf16)
            here = rows_of(operand, core * rows, rows)
            away = swap_core(away)
            other = project(rows_of(here, (1 - half) * part, part)) + rows_of(
                away, (1 - half) * part, part
            ).astype(f32)
            other = swap_tp(other.astype(bf16))
            own = project(rows_of(here, half * part, part)) + rows_of(
                away, half * part, part
            ).astype(f32)
            return own + other.astype(f32)

        x_part = rows_of(x_own, half * part, part).astype(f32)
        after_attn = x_part + to_slice(mixed, lambda v: contract_cols(v, weight_o))
        normed_two, inverse_two = norm_parts(after_attn)
        h_part = (normed_two * gain_m).astype(bf16)

        by_tp, by_zl = swap_tp(h_part), across(h_part, 2)
        mid = part // 2
        near = cat([h_part, by_tp, by_zl])
        far_near = swap_core(near)
        both = cat([across(by_tp[:mid], 2), swap_tp(by_zl[mid:])])
        h_two = cat([near, both, far_near, swap_core(both)])

        dy_rel = permute_cols(cotangent, rel, block)
        dy_ff = cat([rows_of(dy_rel, half * part, part), rows_of(dy_rel, (1 - half) * part, part)])
        dy_zl = across(after(dy_ff[:part], both), 2)
        near = cat([dy_ff, dy_zl, swap_tp(dy_zl)])
        grad_out = cat([near, swap_core(near)])

        gate_pre = matmul(h_two, weight_g)
        up_pre = matmul(h_two, weight_u)
        gate_sig = jax.nn.sigmoid(gate_pre)
        gate_act = gate_pre * gate_sig
        hidden = (gate_act * up_pre).astype(bf16)

        def from_tokens(project, gate=None):
            count = 4 * part
            away = swap_core(project(slice(count, 2 * count)).astype(bf16))
            total = project(slice(0, count)) + away.astype(f32)
            mid = width // 2
            low, high = total[:, :mid], total[:, mid:]

            def pick(values, i):
                return values[i * part : (i + 1) * part]

            low_sent = cat([pick(low, 1), pick(low, 3)]).astype(bf16)
            high_sent = cat([pick(high, 2), pick(high, 3)]).astype(bf16)
            if gate is not None:
                low_sent, high_sent = after((low_sent, high_sent), gate)
            low_tp, high_zl = swap_tp(low_sent), across(high_sent, 2)
            first = (low_tp, high_zl)
            low_tp, high_zl = low_tp.astype(f32), high_zl.astype(f32)
            low_zl = across((pick(low, 2) + pick(low_tp, 1)).astype(bf16), 2)
            high_tp = swap_tp((pick(high, 1) + pick(high_zl, 1)).astype(bf16))
            second = (low_zl, high_tp)
            low_sum = pick(low, 0) + pick(low_tp, 0) + low_zl.astype(f32)
            high_sum = pick(high, 0) + pick(high_zl, 0) + high_tp.astype(f32)
            return (low_sent, first, second), cat([low_sum, high_sum], 1)

        prod_d = contract_rows(grad_out, hidden).astype(bf16)
        grad_hidden = matmul(after(grad_out, prod_d), weight_d)
        grad_gate = (grad_hidden * up_pre * gate_sig * (1.0 + gate_pre * (1.0 - gate_sig))).astype(bf16)
        grad_up = (grad_hidden * gate_act).astype(bf16)
        late_hidden = after(hidden, prod_d)
        (sent_m, first_m, second_m), mlp = from_tokens(lambda where: contract_cols(late_hidden[where], weight_d))
        grad_gate, grad_up = after((grad_gate, grad_up), sent_m)
        grad_gu = cat([grad_gate, grad_up], 1)
        prod_gu = contract_rows(h_two, grad_gu).astype(bf16)
        late_gu = after(grad_gu, prod_gu, first_m)
        weight_gu = weight_f[:, : 2 * n_ff]
        _, grad_h_two = from_tokens(lambda where: contract_cols(late_gu[where], weight_gu), second_m)
        out_part = (after_attn + mlp).astype(bf16)
        output = join_tokens(out_part, swap_tp(out_part), half, nat, block)

        grad_gain_m = jnp.sum(grad_h_two * normed_two, axis=0, keepdims=True)
        dy_part = rows_of(dy_rel, half * part, part).astype(f32)
        grad_after = dy_part + norm_back(grad_h_two * gain_m, normed_two, inverse_two)

        grad_part = grad_after.astype(bf16)
        grad_half = ordered(half, grad_part, swap_tp(grad_part))
        grad_attn = ordered(core, grad_half, swap_core(grad_half))
        grad_mixed = matmul(grad_attn, weight_o).astype(bf16)

        def scatter(values, members):
            return lax.psum_scatter(
                values.astype(bf16), "shard", scatter_dimension=0, tiled=True, axis_index_groups=members
            )

        def away_rows(own):
            return across(rows_of(own, (1 - zl) * block, block), 2)

        def rows_pair(own, other, count):
            def send_rows(s_ref, mine, theirs, out):
                low, away_rows = s_ref[1], pl.multiple_of((1 - s_ref[0]) * unit, unit)
                rows_m = pl.ds(pl.multiple_of(low * block, block) + away_rows, unit)
                for i in range(count):
                    cols = slice(i * n_ff, (i + 1) * n_ff)
                    out[:, pl.ds(i * 2 * n_ff + pl.multiple_of(low * n_ff, n_ff), n_ff)] = mine[rows_m, cols]
                    out[:, pl.ds(i * 2 * n_ff + pl.multiple_of((1 - low) * n_ff, n_ff), n_ff)] = theirs[
                        pl.ds(away_rows, unit), cols
                    ]

            (sent,) = small_call(send_rows, [core, zl], [own, other], [array_of(unit, 2 * count * n_ff)])
            third = swap_core(sent)

            def join_rows(s_ref, mine, theirs, third_ref, *outs):
                me, low = s_ref[0], s_ref[1]
                start = pl.multiple_of(me * 2 * n_ff, n_ff)
                away = pl.multiple_of((1 - me) * 2 * n_ff, n_ff)
                here = pl.multiple_of(me * unit, unit)
                for i, out in enumerate(outs):
                    cols = slice(i * n_ff, (i + 1) * n_ff)
                    out[:, pl.ds(start + pl.multiple_of(low * n_ff, n_ff), n_ff)] = mine[
                        pl.ds(pl.multiple_of(low * block, block) + here, unit), cols
                    ].astype(f32)
                    out[:, pl.ds(start + pl.multiple_of((1 - low) * n_ff, n_ff), n_ff)] = theirs[
                        pl.ds(here, unit), cols
                    ].astype(f32)
                    out[:, pl.ds(away, 2 * n_ff)] = third_ref[:, i * 2 * n_ff : (i + 1) * 2 * n_ff].astype(f32)

            return small_call(join_rows, [core, zl], [own, other, third], [array_of(unit, 4 * n_ff, f32)] * count)

        def send_unit(s_ref, own, out):
            out[...] = own[pl.ds((1 - s_ref[0]) * unit, unit), :].astype(bf16)

        own_d = scatter(prod_d, groups)
        own_gu = scatter(prod_gu, groups)
        late_o = contract_rows(grad_attn, mixed).astype(bf16)
        own_o = scatter(after(late_o, own_d, own_gu), every)
        grad_mixed = after(grad_mixed, late_o)
        grad_qkv = attend_backward(kept, grad_mixed, seg_row, cosine, sine, 0, heads)
        other_d, other_gu = away_rows(own_d), away_rows(own_gu)
        grad_qkv = after(grad_qkv, other_gu)
        own_qkv = scatter(after(contract_rows(h_one, grad_qkv).astype(bf16), own_o), every)

        (grad_w_down,) = rows_pair(own_d, other_d, 1)
        grad_w_gate, grad_w_up = rows_pair(own_gu, other_gu, 2)

        grad_h_one = to_slice(grad_qkv, lambda v: contract_cols(v, weight_qkv))

        normed_part = rows_of(normed_all, core * rows + half * part, part)
        inverse_part = rows_of(inverse_all, core * rows + half * part, part)
        grad_gain_a = jnp.sum(grad_h_one * normed_part, axis=0, keepdims=True)
        grad_x = (grad_after + norm_back(grad_h_one * gain_a, normed_part, inverse_part)).astype(bf16)
        grad_tokens = join_tokens(grad_x, swap_tp(grad_x), half, nat, block)

        own_qkv = after(own_qkv, output, grad_tokens, grad_w_gate, grad_w_up, grad_w_down)
        own_a = cat([own_qkv, own_o], 1)
        (sent_g,) = small_call(send_unit, [core], [own_a], [array_of(unit, 4 * n_attn)])
        other_a = swap_core(sent_g)

        def join_attn(s_ref, own, other, q, k, v, o):
            me = s_ref[0]
            mine = pl.ds(pl.multiple_of(me * unit, unit), unit)
            here, there = me * n_attn, (1 - me) * n_attn
            for start, load in (
                (here, lambda c: own[mine, c].astype(f32)),
                (there, lambda c: other[:, c].astype(f32)),
            ):
                start = pl.multiple_of(start, n_attn)
                for h in range(heads):
                    for i, ref in enumerate((q, k, v)):
                        ref[:, pl.ds(start + h * HD, HD)] = load(slice((3 * h + i) * HD, (3 * h + i + 1) * HD))
                o[:, pl.ds(start, n_attn)] = load(slice(3 * n_attn, 4 * n_attn))

        grad_w_query, grad_w_key, grad_w_value, grad_w_out = small_call(
            join_attn, [core], [own_a, other_a], [array_of(unit, 2 * n_attn, f32)] * 4
        )

        grad_gains = cat([grad_gain_a, grad_gain_m])
        grad_gains = grad_gains + swap_tp(grad_gains)
        for mask in [1 << bit for bit in range(shards.bit_length() - 2, 1, -1)] + [1, 2]:
            mid = grad_gains.shape[1] // 2
            first, second = grad_gains[:, :mid], grad_gains[:, mid:]
            low = (shard & mask) == 0
            grad_gains = jnp.where(low, first, second) + across(jnp.where(low, second, first), mask)
        first, second = grad_gains[:, :unit], grad_gains[:, unit:]
        grad_gains = jnp.where(core == 0, first, second) + swap_core(jnp.where(core == 0, second, first))

        return (
            output,
            grad_tokens,
            grad_gains[0],
            grad_w_query,
            grad_w_key,
            grad_w_value,
            grad_w_out,
            grad_gains[1],
            grad_w_gate,
            grad_w_up,
            grad_w_down,
        )

    return per_device


def solution(mesh):
    wide = P(("shard", "ctx"), None)
    flat = P(("shard", "ctx"))
    both = P(("shard", "ctx"), "tp")
    placed = (wide, P("shard", None), flat, both, both, both, both, flat, both, both, both, wide)
    return jax.shard_map(
        build(mesh.shape["shard"]),
        mesh=mesh,
        in_specs=placed,
        out_specs=(wide, wide, flat, both, both, both, both, flat, both, both, both),
        check_vma=False,
    )
```
